32 devices in a mesh: dp: 8 (over y, x, core), seq: 4 (over z).
Axes of the slice: x: 2, y: 2, z: 4, core: 2. Of those that a mesh axis runs over, the one named last changes fastest.
Arguments:
- queries: bfloat16 [8, 4, 512, 32, 128], P('dp', 'seq'), may hold values from -6 to 6
- key_rows: bfloat16 [8, 4, 512, 32, 128], P('dp', 'seq'), may hold values from -6 to 6
- value_rows: bfloat16 [8, 4, 512, 32, 128], P('dp', 'seq'), may hold values from -6 to 6
- destination: int32 [8, 4, 512], P('dp', 'seq'), may hold values from 0 to 7, as said below
- doc_starts: int32 [8, 4, 512], P('dp', 'seq'), may hold values 0 or 1
- decay_rate: float32 [32], replicated, may hold values from 7.6293945e-06 to 0.04
- norm_gain: float32 [32, 128], replicated, may hold values from 0.1 to 1.9
Outputs:
- attended: bfloat16 [8, 4, 512, 32, 128], P('dp', 'seq')
The draws below stay inside these ranges and needn't reach their ends.
Inputs may be any that keep to these rules, and one draw needn't show every extreme that they name: `destination`: each loader sends at most 96 of its rows to one sequence; at each seq index one sequence, drawn afresh, receives exactly 96 rows from every loader.
All inputs are finite; a program needn't handle non-finite values. No bound on the sum of `doc_starts` on one device may be relied on, other than what follows from the above.
Results may differ from the reference program's by a relative error of at most 0.0055.
Values may be sent and summed in bfloat16 or wider, within the bound.
A program may use at most 192 MiB of HBM per device.

```python
import math
import jax
import jax.numpy as jnp
from jax import lax

H = 32
DH = 128
BLK = 384
TOK_DEV = 512
LOADERS = 8
SHARDS = 4
CAP = 96
CHAIN = 2048


def draw_destination(key, part):
    hot_key, row_key = jax.random.split(jax.random.fold_in(key, 11))
    hot_seq = jax.random.randint(hot_key, (SHARDS,), 0, LOADERS).astype(jnp.int32)
    hot_all = jnp.tile(hot_seq, LOADERS)
    row_keys = jax.random.split(row_key, LOADERS * SHARDS)

    def one_loader(loader_key, hot_target):
        pick_key, order_key = jax.random.split(loader_key)
        picks = jax.random.permutation(pick_key, (LOADERS - 1) * CAP)[:TOK_DEV - CAP].astype(jnp.int32)
        others = picks // CAP
        others = others + (others >= hot_target).astype(jnp.int32)
        targets = jnp.concatenate([jnp.full((CAP,), hot_target, jnp.int32), others.astype(jnp.int32)])
        order = jax.random.permutation(order_key, TOK_DEV).astype(jnp.int32)
        return targets[order]
    rows = jax.vmap(one_loader)(row_keys, hot_all)
    return rows.reshape(LOADERS, SHARDS, TOK_DEV).astype(jnp.int32)


def draw_decay_rate(key, part):
    uniform_part = jax.random.uniform(jax.random.fold_in(key, 23), (H,), jnp.float32)
    low_end = math.log(1.0 / (64.0 * CHAIN))
    high_end = math.log(1.0 / 25.0)
    return jnp.exp(low_end + (high_end - low_end) * uniform_part).astype(jnp.float32)


def touch_ends(result, rng, least, top_value):
    longest = result.shape.index(max(result.shape))
    spots = []
    for shift in (0, 1):
        where = [jax.random.randint(jax.random.fold_in(rng, axis), (), 0, length) for axis, length in enumerate(result.shape)]
        where[longest] = (where[longest] + shift) % result.shape[longest]
        spots.append(tuple(where))
    return result.at[spots[0]].set(least).at[spots[1]].set(top_value)


def level_of(rng, shape, cuts, smallest, high):
    level, own = 1.0, jax.random.fold_in(rng, 6)
    for dim, blocks in cuts:
        heights = jnp.exp(jax.random.uniform(jax.random.fold_in(own, dim), (blocks,), jnp.float32, smallest / len(cuts), high / len(cuts)))
        level = level * jnp.repeat(heights, shape[dim] // blocks).reshape([-1 if axis == dim else 1 for axis in range(len(shape))])
    return level


def gaussian(rng, shape, spread, reach, cuts=(), held_as=jnp.bfloat16):
    factor_of = level_of(rng, shape, cuts, -0.22, 0.18) if cuts else 1.0
    array = jax.random.normal(rng, shape, jnp.float32) * spread * factor_of
    return jnp.minimum(jnp.maximum(array, -reach), reach).astype(held_as)


def setup_inputs(seed: int = 0) -> dict:
    streams_of = jax.random.split(jax.random.key(seed), 8)
    return {
        "queries": gaussian(streams_of[0], (LOADERS, SHARDS, TOK_DEV, H, DH), 1.0, 6.0, ((0, 8), (1, 4))),
        "key_rows": gaussian(streams_of[1], (LOADERS, SHARDS, TOK_DEV, H, DH), 1.0, 6.0, ((0, 8), (1, 4))),
        "value_rows": gaussian(streams_of[2], (LOADERS, SHARDS, TOK_DEV, H, DH), 1.0, 6.0, ((0, 8), (1, 4))),
        "destination": draw_destination(jax.random.fold_in(streams_of[7], 71), 0),
        "doc_starts": touch_ends((jax.random.randint(streams_of[4], (LOADERS, SHARDS, TOK_DEV), 0, 4 * CHAIN) < 1).astype(jnp.int32), jax.random.fold_in(streams_of[4], 1), 0, 1),
        "decay_rate": draw_decay_rate(jax.random.fold_in(streams_of[7], 71), 0),
        "norm_gain": jnp.clip(1.0 + 0.18 * jax.random.normal(streams_of[6], (H, DH), jnp.float32), 0.1, 1.9),
    }


eps_norm = 1e-06

def to_half(values_in):
    return lax.optimization_barrier(values_in.astype(jnp.bfloat16)).astype(jnp.float32)

def attend_block(carry_state, block_inputs, decay_rate, norm_gain):
    block_query, block_key, block_value, block_count, block_doc, block_live, block_start = block_inputs
    before_count = block_count[0] - block_live[0]
    before_doc = block_doc[0] - block_start[0]
    positions = jnp.arange(BLK, dtype=jnp.int32)
    causal = positions[:, None] >= positions[None, :]
    same_doc = block_doc[:, None] == block_doc[None, :]
    keep_mask = causal & same_doc & (block_live[None, :] == 1)
    distance = jnp.maximum(block_count[:, None] - block_count[None, :], 0).astype(jnp.float32)
    weight = jnp.where(keep_mask[None], jnp.exp(-decay_rate[:, None, None] * distance[None]), 0.0)
    query_wide = block_query.astype(jnp.float32)
    key_wide = block_key.astype(jnp.float32)
    value_wide = block_value.astype(jnp.float32)
    scores = jnp.einsum('phd,qhd->hpq', query_wide, key_wide)
    weights_half = to_half(scores * weight)
    intra_term = jnp.einsum('hpq,qhd->phd', weights_half, value_wide)
    since = (block_count - before_count).astype(jnp.float32)
    carry_weight = jnp.where((block_doc == before_doc)[:, None], jnp.exp(-decay_rate[None, :] * since[:, None]), 0.0)
    state_half = to_half(carry_state)
    inter_term = jnp.einsum('phd,hde->phe', query_wide, state_half) * carry_weight[:, :, None]
    mixed_out = intra_term + inter_term
    end_count = block_count[-1]
    end_doc = block_doc[-1]
    until = (end_count - block_count).astype(jnp.float32)
    key_keep = (block_live == 1) & (block_doc == end_doc)
    key_weight = jnp.where(key_keep[:, None], jnp.exp(-decay_rate[None, :] * until[:, None]), 0.0)
    scaled_keys = to_half(key_wide * key_weight[:, :, None])
    update = jnp.einsum('phd,phe->hde', scaled_keys, value_wide)
    block_span = (end_count - before_count).astype(jnp.float32)
    block_decay = jnp.where(end_doc == before_doc, jnp.exp(-decay_rate * block_span), 0.0)
    new_state = block_decay[:, None, None] * carry_state + update
    mean_square = lax.optimization_barrier(jnp.mean(mixed_out * mixed_out, axis=(1, 2)))
    normed = (mixed_out * lax.rsqrt(mean_square + eps_norm)[:, None, None] * norm_gain[None]).astype(jnp.bfloat16)
    return (new_state, normed)

def attend_sequence(table_query, table_key, table_value, table_live, table_start, decay_rate, norm_gain):
    total = SHARDS * LOADERS * CAP
    live_flat = table_live.reshape(total)
    start_flat = table_start.reshape(total)
    live_count = jnp.cumsum(live_flat, dtype=jnp.int32)
    doc_count = jnp.cumsum(start_flat, dtype=jnp.int32)
    block_total = total // BLK

    def shaped(values_in):
        return values_in.reshape((block_total, BLK) + values_in.shape[3:])
    block_inputs = (shaped(table_query), shaped(table_key), shaped(table_value), live_count.reshape(block_total, BLK), doc_count.reshape(block_total, BLK), live_flat.reshape(block_total, BLK), start_flat.reshape(block_total, BLK))

    def advance(carry_state, inputs):
        return attend_block(carry_state, inputs, decay_rate, norm_gain)
    first_state = jnp.zeros((H, DH, DH), jnp.float32)
    final_state, normed = lax.scan(advance, first_state, block_inputs)
    return normed.reshape(SHARDS, LOADERS, CAP, H, DH)

def reference(queries, key_rows, value_rows, destination, doc_starts, decay_rate, norm_gain):
    targets = jnp.arange(LOADERS, dtype=jnp.int32)
    onehot = (destination[..., None] == targets).astype(jnp.int32)
    slot = lax.optimization_barrier(jnp.sum(jnp.cumsum(onehot, axis=2, dtype=jnp.int32) * onehot, axis=-1, dtype=jnp.int32)) - 1
    shard_ids = jnp.broadcast_to(jnp.arange(SHARDS, dtype=jnp.int32)[None, :, None], destination.shape)
    source_ids = jnp.broadcast_to(jnp.arange(LOADERS, dtype=jnp.int32)[:, None, None], destination.shape)
    slot_read = jnp.minimum(slot, CAP - 1).astype(jnp.int32)

    def one_sequence(output_acc, sequence_id):
        chosen = destination == sequence_id
        slot_write = jnp.where(chosen, slot, CAP).astype(jnp.int32)

        def table(values_in, dtype):
            empty = jnp.zeros((SHARDS, LOADERS, CAP) + values_in.shape[3:], dtype)
            return empty.at[shard_ids, source_ids, slot_write].set(values_in, mode='drop')
        table_query = table(queries, jnp.bfloat16)
        table_key = table(key_rows, jnp.bfloat16)
        table_value = table(value_rows, jnp.bfloat16)
        table_live = table(jnp.ones_like(destination), jnp.int32)
        table_start = table(doc_starts, jnp.int32)
        normed = attend_sequence(table_query, table_key, table_value, table_live, table_start, decay_rate, norm_gain)
        rows_back = normed[shard_ids, source_ids, slot_read]
        return (jnp.where(chosen[..., None, None], rows_back, output_acc), None)
    initial = jnp.zeros(queries.shape, jnp.bfloat16)
    attended, unused = lax.scan(one_sequence, initial, jnp.arange(LOADERS, dtype=jnp.int32))
    return attended
```

```python
import functools
import jax
import jax.numpy as jnp
from jax import lax
from jax.experimental import pallas as pl
from jax.experimental.pallas import tpu as pltpu
from jax.sharding import PartitionSpec as P

MESH = pl.DeviceIdType.MESH
F32 = jnp.float32
BF16 = jnp.bfloat16
I32 = jnp.int32
eps_norm = 1e-06
LANES = 128
HG = 8
HI = 16
HC = 2
NEVER = 1e30
UP_LAG = 2
Z_LAG = 2


def prep_kernel(seqs, cap, dest_ref, start_ref, src_ref, flat_ref, fact_ref, until_ref, since_ref, gap_ref):
    rows = dest_ref.shape[-1]
    drow = dest_ref[0, 0].astype(F32)
    srow = start_ref[0, 0].astype(F32)
    drow = drow.reshape(1, rows)
    srow = srow.reshape(1, rows)
    ri = lax.broadcasted_iota(I32, (rows, rows), 0)
    ci = lax.broadcasted_iota(I32, (rows, rows), 1)
    dcol = jnp.sum(jnp.where(ri == ci, drow, 0.0), axis=1, keepdims=True)
    scol = jnp.sum(jnp.where(ri == ci, srow, 0.0), axis=1, keepdims=True)
    same = jnp.where(dcol == drow, 1.0, 0.0)
    slot_col = jnp.sum(jnp.where(ci < ri, same, 0.0), axis=1, keepdims=True)
    slot_row = jnp.sum(jnp.where(ri < ci, same, 0.0), axis=0, keepdims=True)
    flat_ref[...] = (drow * cap + slot_row).astype(I32)
    slot_wide = dcol * LANES + slot_col
    rcol = lax.broadcasted_iota(I32, (rows, 1), 0).astype(F32)
    place = lax.broadcasted_iota(I32, (rows, LANES), 1).astype(F32)
    pi = lax.broadcasted_iota(I32, (cap, LANES), 0)
    pj = lax.broadcasted_iota(I32, (cap, LANES), 1)
    position = pi.astype(F32)
    for g in range(seqs):
        hit = slot_wide == place + float(g * LANES)
        source = jnp.sum(jnp.where(hit, rcol, 0.0), axis=0, keepdims=True)
        src_ref[:, g * LANES : (g + 1) * LANES] = source.astype(I32)
        begin = jnp.sum(jnp.where(hit, scol, 0.0), axis=0, keepdims=True)
        number = jnp.sum(jnp.where(drow == float(g), 1.0, 0.0), axis=1, keepdims=True)
        doc_end = jnp.sum(begin, axis=1, keepdims=True)
        doc_col = jnp.sum(jnp.where(pj <= pi, begin, 0.0), axis=1, keepdims=True)
        begin_col = jnp.sum(jnp.where(pj == pi, begin, 0.0), axis=1, keepdims=True)
        doc_row = jnp.sum(jnp.where(pi <= pj, begin_col, 0.0), axis=0, keepdims=True)
        here = slice(g * cap, (g + 1) * cap)
        fact_ref[0, g : g + 1, :] = jnp.broadcast_to(number, (1, LANES))
        fact_ref[1, g : g + 1, :] = jnp.broadcast_to(doc_end, (1, LANES))
        ends = (position < number) & (doc_col == doc_end)
        until_ref[here, :] = jnp.where(ends, number - 1.0 - position, NEVER)
        since_ref[here, :] = jnp.where(
            jnp.broadcast_to(doc_col, (cap, LANES)) == 0.0, position + 1.0, NEVER
        )
        keep = (pi >= pj) & (doc_col == doc_row)
        gap_ref[here, :] = jnp.where(keep, (pi - pj).astype(F32), NEVER)


def prepare(destination, doc_starts, seqs, cap):
    rows = destination.shape[-1]
    total = seqs * cap
    table = jax.ShapeDtypeStruct((total, LANES), F32)
    return pl.pallas_call(
        functools.partial(prep_kernel, seqs, cap),
        out_shape=[
            jax.ShapeDtypeStruct((1, seqs * LANES), I32),
            jax.ShapeDtypeStruct((1, rows), I32),
            jax.ShapeDtypeStruct((2, seqs, LANES), F32),
            table,
            table,
            table,
        ],
        in_specs=[pl.BlockSpec(memory_space=pltpu.VMEM)] * 2,
        out_specs=[pl.BlockSpec(memory_space=pltpu.VMEM)] * 6,
        compiler_params=pltpu.CompilerParams(vmem_limit_bytes=32 * 1024 * 1024),
    )(destination, doc_starts)


def scan_kernel(levels, shards, seqs, heads, cap, base, *refs):
    fact_ref, rate_ref, src_ref, until_ref, since_ref, gap_ref = refs[:6]
    sources = refs[6:9]
    mixed_hbm, square_ref = refs[9:11]
    u_ref, out_ref, packed, tall = refs[11:15]
    inbuf = refs[15:18]
    in_sem, row_sem, facts, spans_ref, dec, f_s, f_r, total, zin = refs[18:27]
    up_s, up_r, dn_s, dn_r, z_s, z_r = refs[27:33]
    got = refs[33:]
    d = LANES
    rows_total = seqs * cap
    me = lax.axis_index("dp")
    shard = lax.axis_index("seq")
    chunks = heads // HC
    per_group = HG // HC
    per_load = HI // HC
    tables = 2 * levels + 1
    share = [2 ** (levels - k - 1) for k in range(levels)]

    def bit(k):
        return lax.rem(lax.div(me, 2**k), 2)

    def partner(k):
        return me + 2**k - bit(k) * (2 ** (k + 1))

    def low(k):
        return lax.rem(me, 2**k)

    def decay(table, seq, head):
        return dec[head, pl.ds(table * seqs + seq, 1), :]

    def in_copy(n, b):
        return pltpu.make_async_copy(
            sources[n].at[0, 0, :, pl.ds(pl.multiple_of(base + b * HI, HI), HI), :],
            inbuf[n],
            in_sem.at[n],
        )

    for n in range(3):
        in_copy(n, 0).start()
    barrier = pltpu.get_barrier_semaphore()
    for i in range(1, seqs):
        peer = lax.rem(me + i, seqs)
        pl.semaphore_signal(barrier, inc=1, device_id=(peer, shard), device_id_type=MESH)

    @pl.when(shard > 0)
    def _():
        pl.semaphore_signal(barrier, inc=1, device_id=(me, shard - 1), device_id_type=MESH)

    @pl.when(shard < shards - 1)
    def _():
        pl.semaphore_signal(barrier, inc=1, device_id=(me, shard + 1), device_id_type=MESH)

    @pl.when(shard == 0)
    def _():
        def clear(i, _):
            zin[pl.ds(i, 1)] = jnp.zeros((1,) + zin.shape[1:], zin.dtype)
            return 0

        lax.fori_loop(0, heads, clear, 0)

    square_ref[...] = jnp.zeros(square_ref.shape, F32)

    def part(c):
        return pl.ds(c * HC, HC)

    def slot(k, j):
        return share[k] - 1 + j

    def up_copy(k, c, j):
        seq = j * 2 ** (k + 1) + (1 - bit(k)) * 2**k + low(k)
        return pltpu.make_async_remote_copy(
            src_ref=u_ref.at[seq, part(c)],
            dst_ref=got[k].at[j, part(c)],
            send_sem=up_s.at[slot(k, j), c],
            recv_sem=up_r.at[slot(k, j), c],
            device_id=(partner(k), shard),
            device_id_type=MESH,
        )

    def down_copy(k, c, j, receive):
        owner = partner(k) if receive else me
        seq = j * 2 ** (k + 1) + lax.rem(owner, 2 ** (k + 1))
        return pltpu.make_async_remote_copy(
            src_ref=got[k].at[j, part(c)],
            dst_ref=out_ref.at[seq, part(c)],
            send_sem=dn_s.at[slot(k, j), c],
            recv_sem=dn_r.at[slot(k, j), c],
            device_id=(partner(k), shard),
            device_id_type=MESH,
        )

    def z_copy(c, target):
        return pltpu.make_async_remote_copy(
            src_ref=total.at[part(c)],
            dst_ref=zin.at[part(c)],
            send_sem=z_s.at[c],
            recv_sem=z_r.at[c],
            device_id=(me, target),
            device_id_type=MESH,
        )

    def row_copy(i):
        return pltpu.make_async_copy(
            tall.at[lax.rem(i, 2)], mixed_hbm.at[i], row_sem.at[lax.rem(i, 2)]
        )

    def gather_side(n, side, target):
        steps = cap // 16
        part_heads = slice(side * HG, (side + 1) * HG)

        def body(it, _):
            first = lax.div(it, steps) * LANES + lax.rem(it, steps) * 16
            for e in range(16):
                row = src_ref[0, first + e]
                place = pl.multiple_of((it * 16 + e) * HG, HG)
                tall[target, pl.ds(place, HG), :] = inbuf[n][row, part_heads, :].astype(F32)
            return 0

        lax.fori_loop(0, seqs * steps, body, 0)

    def gather(n, i, target):
        for side in range(HI // HG):

            @pl.when(lax.rem(i, HI // HG) == side)
            def _():
                gather_side(n, side, target)

    def update(c):
        def body(g, _):
            here = pl.ds(pl.multiple_of(g * cap, 16), cap)
            until = until_ref[here, :]
            for e in range(HC):
                head = c * HC + e
                j = lax.rem(head, HG)
                cols = pl.ds(pl.multiple_of(head * d, d), d)
                strided = pl.ds(g * cap * HG + j, cap, stride=HG)
                key = tall[0, strided, :]
                value = tall[1, strided, :].astype(BF16)
                weight = jnp.exp(-rate_ref[base + head] * until)
                scaled = (key * weight).astype(BF16)
                packed[0, here, cols] = key.astype(BF16)
                packed[1, here, cols] = value
                change = lax.dot_general(
                    scaled, value, (((0,), (0,)), ((), ())), preferred_element_type=F32
                )
                u_ref[g, head] = change.astype(BF16)
            return 0

        lax.fori_loop(0, seqs, body, 0)
        for j in range(share[0]):
            up_copy(0, c, j).start()

    def gather_query(i):
        gather(2, i, 0)

        def body(g, _):
            here = pl.ds(pl.multiple_of(g * cap, 16), cap)
            for j in range(HG):
                cols = pl.ds(pl.multiple_of((i * HG + j) * d, d), d)
                strided = pl.ds(g * cap * HG + j, cap, stride=HG)
                packed[2, here, cols] = tall[0, strided, :].astype(BF16)
            return 0

        lax.fori_loop(0, seqs, body, 0)

    def up(k, c):
        for j in range(share[k]):
            up_copy(k, c, j).wait_recv()
        first = (bit(k) == 0).astype(F32)

        def body(i, _):
            j, head = lax.div(i, HC), c * HC + lax.rem(i, HC)
            seq = j * 2 ** (k + 1) + low(k + 1)
            own = u_ref[seq, head].astype(F32)
            other = got[k][j, head].astype(F32)
            hi = decay(k, seq, head)
            own_w = first * hi + (1.0 - first)
            other_w = first + (1.0 - first) * hi
            both = own * own_w + other * other_w
            got[k][j, head] = (first * own + (1.0 - first) * other).astype(BF16)
            if k + 1 < levels:
                u_ref[seq, head] = both.astype(BF16)
            else:
                total[head] = both
            return 0

        lax.fori_loop(0, share[k] * HC, body, 0)
        if k + 1 < levels:
            for j in range(share[k + 1]):
                up_copy(k + 1, c, j).start()

    def across(c):
        @pl.when(shard > 0)
        def _():
            z_copy(c, shard).wait_recv()

        def body(i, _):
            head = c * HC + i
            state = zin[head]
            out_ref[me, head] = state.astype(BF16)
            total[head] = state * decay(2 * levels, me, head) + total[head]
            return 0

        lax.fori_loop(0, HC, body, 0)

        @pl.when(shard < shards - 1)
        def _():
            z_copy(c, shard + 1).start()

    def down(k, c):
        if k + 1 < levels:
            for j in range(share[k + 1]):
                down_copy(k + 1, c, j, True).wait_recv()
        first = (bit(k) == 0).astype(F32)

        def body(i, _):
            j, head = lax.div(i, HC), c * HC + lax.rem(i, HC)
            seq = j * 2 ** (k + 1) + low(k + 1)
            start = out_ref[seq, head].astype(F32)
            later = start * decay(levels + k, seq, head) + got[k][j, head].astype(F32)
            out_ref[seq, head] = (first * start + (1.0 - first) * later).astype(BF16)
            got[k][j, head] = (first * later + (1.0 - first) * start).astype(BF16)
            return 0

        lax.fori_loop(0, share[k] * HC, body, 0)
        for j in range(share[k]):
            down_copy(k, c, j, False).start()

    def attend(c):
        i = lax.div(c, per_group)
        side = lax.rem(i, 2)

        @pl.when((lax.rem(c, per_group) == 0) & (i >= 2))
        def _():
            row_copy(i - 2).wait()

        for j in range(share[0]):
            down_copy(0, c, j, True).wait_recv()

        def body(g, _):
            here = pl.ds(pl.multiple_of(g * cap, 16), cap)
            gap = gap_ref[here, :cap]
            since = since_ref[here, :]
            squares = square_ref[here, :]
            for e in range(HC):
                head = c * HC + e
                j = lax.rem(head, HG)
                cols = pl.ds(pl.multiple_of(head * d, d), d)
                rate = rate_ref[base + head]
                query = packed[2, here, cols]
                scores = lax.dot_general(
                    query,
                    packed[0, here, cols],
                    (((1,), (1,)), ((), ())),
                    preferred_element_type=F32,
                )
                half = (scores * jnp.exp(-rate * gap)).astype(BF16)
                intra = jnp.dot(half, packed[1, here, cols], preferred_element_type=F32)
                inter = jnp.dot(query, out_ref[g, head], preferred_element_type=F32)
                mixed = intra + inter * jnp.exp(-rate * since)
                tall[side, pl.ds(g * cap * HG + j, cap, stride=HG), :] = mixed
                squares = squares + mixed * mixed
            square_ref[here, :] = squares
            return 0

        lax.fori_loop(0, seqs, body, 0)

        @pl.when(lax.rem(c, per_group) == per_group - 1)
        def _():
            row_copy(i).start()

    def fact_copy(i, receive):
        owner = lax.rem(me + seqs - i, seqs) if receive else me
        return pltpu.make_async_remote_copy(
            src_ref=fact_ref,
            dst_ref=facts.at[owner],
            send_sem=f_s.at[i - 1],
            recv_sem=f_r.at[i - 1],
            device_id=(lax.rem(me + i, seqs), shard),
            device_id_type=MESH,
        )

    in_copy(0, 0).wait()
    gather_side(0, 0, 0)
    in_copy(1, 0).wait()
    gather_side(1, 0, 1)
    ends = (shard > 0).astype(I32) + (shard < shards - 1).astype(I32)
    pl.semaphore_wait(barrier, seqs - 1 + ends)
    for i in range(1, seqs):
        fact_copy(i, False).start()
    update(0)
    facts[pl.ds(me, 1)] = fact_ref[...][None]
    for i in range(1, seqs):
        fact_copy(i, True).wait_recv()
    spans = [((me // 2 ** (k + 1) * 2 + 1) * 2**k, 2**k) for k in range(levels)]
    spans += [((me // 2 ** (k + 1) * 2) * 2**k, 2**k) for k in range(levels)]
    spans += [(me * 0, seqs)]
    for table, (begin, size) in enumerate(spans):
        count = jnp.zeros(fact_ref.shape[1:], F32)
        docs = jnp.zeros(fact_ref.shape[1:], F32)
        for loader in range(seqs):
            inside = ((loader >= begin) & (loader < begin + size)).astype(F32)
            count = count + facts[loader, 0] * inside
            docs = docs + facts[loader, 1] * inside
        spans_ref[table * seqs : (table + 1) * seqs, :] = jnp.where(docs == 0.0, count, NEVER)

    def fill(head, _):
        dec[head] = jnp.exp(-rate_ref[base + head] * spans_ref[...])
        return 0

    lax.fori_loop(0, heads, fill, 0)

    ups = [1 + UP_LAG * k for k in range(levels)]
    z_first = ups[-1] + 1
    d_first = max(z_first + Z_LAG * (shards - 1) + 1, chunks - levels)
    downs = [d_first + (levels - 1 - k) + (1 if k == 0 else 0) for k in range(levels)]
    a_first = downs[0] + 1

    def during(c):
        return (c >= 0) & (c < chunks)

    def step(t, _):
        fresh = t < chunks

        @pl.when(fresh & (lax.rem(t, per_group) == 0))
        def _():
            i = lax.div(t, per_group)

            @pl.when(lax.rem(t, per_load) == 0)
            def _():
                in_copy(0, lax.div(t, per_load)).wait()
                in_copy(1, lax.div(t, per_load)).wait()

            gather(0, i, 0)
            gather(1, i, 1)

            @pl.when((t < chunks - per_load) & (lax.rem(t, per_load) == per_load - per_group))
            def _():
                in_copy(0, lax.div(t, per_load) + 1).start()
                in_copy(1, lax.div(t, per_load) + 1).start()

        @pl.when(fresh)
        def _():
            update(t)

        for k in range(levels):

            @pl.when(during(t - ups[k]))
            def _():
                up(k, t - ups[k])

        @pl.when(fresh & (lax.rem(t, per_group) == per_group - 1))
        def _():
            @pl.when(lax.rem(t, per_load) == per_group - 1)
            def _():
                in_copy(2, lax.div(t, per_load)).wait()

            gather_query(lax.div(t, per_group))

            @pl.when((t < chunks - per_load) & (lax.rem(t, per_load) == per_load - 1))
            def _():
                in_copy(2, lax.div(t, per_load) + 1).start()

        cz = t - z_first - Z_LAG * shard

        @pl.when(during(cz))
        def _():
            across(cz)

        for k in range(levels - 1, -1, -1):

            @pl.when(during(t - downs[k]))
            def _():
                down(k, t - downs[k])

        @pl.when(during(t - a_first))
        def _():
            attend(t - a_first)

        return 0

    lax.fori_loop(1, chunks + a_first, step, 0)
    for i in range(max(0, heads // HG - 2), heads // HG):
        row_copy(i).wait()

    def settle(c, _):
        for k in range(levels):
            for j in range(share[k]):
                up_copy(k, c, j).wait_send()
                down_copy(k, c, j, False).wait_send()
        return 0

    lax.fori_loop(0, chunks, settle, 0)
    for i in range(1, seqs):
        fact_copy(i, False).wait_send()

    @pl.when(shard < shards - 1)
    def _():
        def settle_z(c, _):
            z_copy(c, shard + 1).wait_send()
            return 0

        lax.fori_loop(0, chunks, settle_z, 0)


def scan_states(prepared, rate, key, value, query, heads, base, levels, shards, cap, call):
    src, facts, until, since, gap = prepared
    d = key.shape[-1]
    rows = key.shape[2]
    seqs = facts.shape[1]
    total = seqs * cap
    chunks = heads // HC
    vm = pltpu.VMEM
    share = [2 ** (levels - k - 1) for k in range(levels)]
    dma = pltpu.SemaphoreType.DMA
    whole = pl.BlockSpec(memory_space=pltpu.VMEM)
    scalar = pl.BlockSpec(memory_space=pltpu.SMEM)
    away = pl.BlockSpec(memory_space=pl.ANY)
    return pl.pallas_call(
        functools.partial(scan_kernel, levels, shards, seqs, heads, cap, base),
        out_shape=[
            jax.ShapeDtypeStruct((heads // HG, total * HG, d), F32),
            jax.ShapeDtypeStruct((total, d), F32),
        ],
        in_specs=[whole, scalar, scalar, whole, whole, whole, away, away, away],
        out_specs=[away, whole],
        scratch_shapes=[
            vm((seqs, heads, d, d), BF16),
            vm((seqs, heads, d, d), BF16),
            vm((3, total, heads * d), BF16),
            vm((2, total * HG, d), F32),
            vm((rows, HI, d), BF16),
            vm((rows, HI, d), BF16),
            vm((rows, HI, d), BF16),
            dma((3,)),
            dma((2,)),
            vm((seqs,) + facts.shape, F32),
            vm(((2 * levels + 1) * seqs, d), F32),
            vm((heads, (2 * levels + 1) * seqs, d), F32),
            dma((seqs - 1,)),
            dma((seqs - 1,)),
            vm((heads, d, d), F32),
            vm((heads, d, d), F32),
            dma((seqs - 1, chunks)),
            dma((seqs - 1, chunks)),
            dma((seqs - 1, chunks)),
            dma((seqs - 1, chunks)),
            dma((chunks,)),
            dma((chunks,)),
        ]
        + [vm((share[k], heads, d, d), BF16) for k in range(levels)],
        compiler_params=pltpu.CompilerParams(
            collective_id=call, has_side_effects=True, vmem_limit_bytes=67043328
        ),
    )(facts, rate, src, until, since, gap, key, value, query)


def finish_kernel(width, flat_ref, square_ref, gain_ref, mixed_ref, o_ref, scale):
    rows = o_ref.shape[0]

    @pl.when(pl.program_id(0) == 0)
    def _():
        mean = jnp.sum(square_ref[...], axis=1, keepdims=True) * (1.0 / width)
        scale[...] = jnp.broadcast_to(lax.rsqrt(mean + eps_norm), scale.shape)

    gains = [gain_ref[b * HG : (b + 1) * HG, :] for b in range(HI // HG)]

    def body(it, _):
        for e in range(8):
            r = it * 8 + e
            place = flat_ref[0, r]
            factor = scale[pl.ds(place, 1), :]
            here = pl.ds(pl.multiple_of(place * HG, HG), HG)
            parts = [mixed_ref[b, here, :] * factor * gains[b] for b in range(HI // HG)]
            o_ref[r] = jnp.concatenate(parts, axis=0).astype(BF16)
        return 0

    lax.fori_loop(0, rows // 8, body, 0)


def finish(flat, squares, gain, mixed):
    rows = flat.shape[1]
    heads, d = gain.shape
    total = squares.shape[0]
    return pl.pallas_call(
        functools.partial(finish_kernel, heads * d),
        grid=(heads // HI,),
        out_shape=jax.ShapeDtypeStruct((rows, heads, d), BF16),
        in_specs=[
            pl.BlockSpec(memory_space=pltpu.SMEM),
            pl.BlockSpec((total, d), lambda i: (0, 0)),
            pl.BlockSpec((HI, d), lambda i: (i, 0)),
            pl.BlockSpec((HI // HG, total * HG, d), lambda i: (i, 0, 0)),
        ],
        out_specs=pl.BlockSpec((rows, HI, d), lambda i: (0, i, 0)),
        scratch_shapes=[pltpu.VMEM((total, d), F32)],
        compiler_params=pltpu.CompilerParams(vmem_limit_bytes=48 * 1024 * 1024),
    )(flat, squares, gain, mixed)


def per_device(queries, key_rows, value_rows, destination, doc_starts, decay_rate, norm_gain):
    loaders = lax.axis_size("dp")
    shards = lax.axis_size("seq")
    rows, heads, d = queries.shape[2:]
    cap = 3 * rows // (2 * loaders)
    levels = loaders.bit_length() - 1
    src, flat, facts, until, since, gap = prepare(destination, doc_starts, loaders, cap)
    passes = max(1, loaders // 8)
    width = heads // passes
    results = []
    for i in range(passes):
        results.append(
            scan_states(
                (src, facts, until, since, gap),
                decay_rate,
                key_rows,
                value_rows,
                queries,
                width,
                i * width,
                levels,
                shards,
                cap,
                i,
            )
        )
    mixed = results[0][0] if passes == 1 else jnp.concatenate([x[0] for x in results], axis=0)
    squares = sum(x[1] for x in results)
    return finish(flat, squares, norm_gain, mixed)[None, None]


def solution(mesh):
    placed = (
        P("dp", "seq", None, None, None),
        P("dp", "seq", None, None, None),
        P("dp", "seq", None, None, None),
        P("dp", "seq", None),
        P("dp", "seq", None),
        P(),
        P(),
    )
    return jax.shard_map(
        per_device,
        mesh=mesh,
        in_specs=placed,
        out_specs=P("dp", "seq", None, None, None),
        check_vma=False,
    )
```

```python
import functools
import jax
import jax.numpy as jnp
from jax import lax
from jax.experimental import pallas as pl
from jax.experimental.pallas import tpu as pltpu
from jax.sharding import PartitionSpec as P

MESH = pl.DeviceIdType.MESH
F32 = jnp.float32
BF16 = jnp.bfloat16
I32 = jnp.int32
eps_norm = 1e-06
LANES = 128
HG = 8
HI = 16
HC = 2
NEVER = 1e30
UP_LAG = 2
Z_LAG = 2


def prep_kernel(seqs, cap, dest_ref, start_ref, src_ref, flat_ref, fact_ref, until_ref, since_ref, gap_ref):
    rows = dest_ref.shape[-1]
    drow = dest_ref[0, 0].astype(F32)
    srow = start_ref[0, 0].astype(F32)
    drow = drow.reshape(1, rows)
    srow = srow.reshape(1, rows)
    ri = lax.broadcasted_iota(I32, (rows, rows), 0)
    ci = lax.broadcasted_iota(I32, (rows, rows), 1)
    dcol = jnp.sum(jnp.where(ri == ci, drow, 0.0), axis=1, keepdims=True)
    scol = jnp.sum(jnp.where(ri == ci, srow, 0.0), axis=1, keepdims=True)
    same = jnp.where(dcol == drow, 1.0, 0.0)
    slot_col = jnp.sum(jnp.where(ci < ri, same, 0.0), axis=1, keepdims=True)
    slot_row = jnp.sum(jnp.where(ri < ci, same, 0.0), axis=0, keepdims=True)
    flat_ref[...] = (drow * cap + slot_row).astype(I32)
    slot_wide = dcol * LANES + slot_col
    rcol = lax.broadcasted_iota(I32, (rows, 1), 0).astype(F32)
    place = lax.broadcasted_iota(I32, (rows, LANES), 1).astype(F32)
    pi = lax.broadcasted_iota(I32, (cap, LANES), 0)
    pj = lax.broadcasted_iota(I32, (cap, LANES), 1)
    position = pi.astype(F32)
    for g in range(seqs):
        hit = slot_wide == place + float(g * LANES)
        source = jnp.sum(jnp.where(hit, rcol, 0.0), axis=0, keepdims=True)
        src_ref[:, g * LANES : (g + 1) * LANES] = source.astype(I32)
        begin = jnp.sum(jnp.where(hit, scol, 0.0), axis=0, keepdims=True)
        number = jnp.sum(jnp.where(drow == float(g), 1.0, 0.0), axis=1, keepdims=True)
        doc_end = jnp.sum(begin, axis=1, keepdims=True)
        doc_col = jnp.sum(jnp.where(pj <= pi, begin, 0.0), axis=1, keepdims=True)
        begin_col = jnp.sum(jnp.where(pj == pi, begin, 0.0), axis=1, keepdims=True)
        doc_row = jnp.sum(jnp.where(pi <= pj, begin_col, 0.0), axis=0, keepdims=True)
        here = slice(g * cap, (g + 1) * cap)
        fact_ref[0, g : g + 1, :] = jnp.broadcast_to(number, (1, LANES))
        fact_ref[1, g : g + 1, :] = jnp.broadcast_to(doc_end, (1, LANES))
        ends = (position < number) & (doc_col == doc_end)
        until_ref[here, :] = jnp.where(ends, number - 1.0 - position, NEVER)
        since_ref[here, :] = jnp.where(
            jnp.broadcast_to(doc_col, (cap, LANES)) == 0.0, position + 1.0, NEVER
        )
        keep = (pi >= pj) & (doc_col == doc_row)
        gap_ref[here, :] = jnp.where(keep, (pi - pj).astype(F32), NEVER)


def prepare(destination, doc_starts, seqs, cap):
    rows = destination.shape[-1]
    total = seqs * cap
    table = jax.ShapeDtypeStruct((total, LANES), F32)
    return pl.pallas_call(
        functools.partial(prep_kernel, seqs, cap),
        out_shape=[
            jax.ShapeDtypeStruct((1, seqs * LANES), I32),
            jax.ShapeDtypeStruct((1, rows), I32),
            jax.ShapeDtypeStruct((2, seqs, LANES), F32),
            table,
            table,
            table,
        ],
        in_specs=[pl.BlockSpec(memory_space=pltpu.VMEM)] * 2,
        out_specs=[pl.BlockSpec(memory_space=pltpu.VMEM)] * 6,
        compiler_params=pltpu.CompilerParams(vmem_limit_bytes=32 * 1024 * 1024),
    )(destination, doc_starts)


def scan_kernel(levels, shards, seqs, heads, cap, base, *refs):
    fact_ref, rate_ref, src_ref, until_ref, since_ref, gap_ref = refs[:6]
    sources = refs[6:9]
    mixed_hbm, square_ref = refs[9:11]
    u_ref, out_ref, packed, tall = refs[11:15]
    inbuf = refs[15:18]
    in_sem, row_sem, facts, spans_ref, dec, f_s, f_r, total, zin = refs[18:27]
    up_s, up_r, dn_s, dn_r, z_s, z_r = refs[27:33]
    got = refs[33:]
    d = LANES
    rows_total = seqs * cap
    me = lax.axis_index("dp")
    shard = lax.axis_index("seq")
    chunks = heads // HC
    per_group = HG // HC
    per_load = HI // HC
    tables = 2 * levels + 1
    share = [2 ** (levels - k - 1) for k in range(levels)]

    def bit(k):
        return lax.rem(lax.div(me, 2**k), 2)

    def partner(k):
        return me + 2**k - bit(k) * (2 ** (k + 1))

    def low(k):
        return lax.rem(me, 2**k)

    def decay(table, seq, head):
        return dec[head, pl.ds(table * seqs + seq, 1), :]

    def in_copy(n, b):
        return pltpu.make_async_copy(
            sources[n].at[0, 0, :, pl.ds(pl.multiple_of(base + b * HI, HI), HI), :],
            inbuf[n],
            in_sem.at[n],
        )

    for n in range(3):
        in_copy(n, 0).start()
    barrier = pltpu.get_barrier_semaphore()
    for i in range(1, seqs):
        peer = lax.rem(me + i, seqs)
        pl.semaphore_signal(barrier, inc=1, device_id=(peer, shard), device_id_type=MESH)

    @pl.when(shard > 0)
    def _():
        pl.semaphore_signal(barrier, inc=1, device_id=(me, shard - 1), device_id_type=MESH)

    @pl.when(shard < shards - 1)
    def _():
        pl.semaphore_signal(barrier, inc=1, device_id=(me, shard + 1), device_id_type=MESH)

    @pl.when(shard == 0)
    def _():
        def clear(i, _):
            zin[pl.ds(i, 1)] = jnp.zeros((1,) + zin.shape[1:], zin.dtype)
            return 0

        lax.fori_loop(0, heads, clear, 0)

    square_ref[...] = jnp.zeros(square_ref.shape, F32)

    def part(c):
        return pl.ds(c * HC, HC)

    def slot(k, j):
        return share[k] - 1 + j

    def up_copy(k, c, j):
        seq = j * 2 ** (k + 1) + (1 - bit(k)) * 2**k + low(k)
        return pltpu.make_async_remote_copy(
            src_ref=u_ref.at[seq, part(c)],
            dst_ref=got[k].at[j, part(c)],
            send_sem=up_s.at[slot(k, j), c],
            recv_sem=up_r.at[slot(k, j), c],
            device_id=(partner(k), shard),
            device_id_type=MESH,
        )

    def down_copy(k, c, j, receive):
        owner = partner(k) if receive else me
        seq = j * 2 ** (k + 1) + lax.rem(owner, 2 ** (k + 1))
        return pltpu.make_async_remote_copy(
            src_ref=got[k].at[j, part(c)],
            dst_ref=out_ref.at[seq, part(c)],
            send_sem=dn_s.at[slot(k, j), c],
            recv_sem=dn_r.at[slot(k, j), c],
            device_id=(partner(k), shard),
            device_id_type=MESH,
        )

    def z_copy(c, target):
        return pltpu.make_async_remote_copy(
            src_ref=total.at[part(c)],
            dst_ref=zin.at[part(c)],
            send_sem=z_s.at[c],
            recv_sem=z_r.at[c],
            device_id=(me, target),
            device_id_type=MESH,
        )

    def row_copy(i):
        return pltpu.make_async_copy(
            tall.at[lax.rem(i, 2)], mixed_hbm.at[i], row_sem.at[lax.rem(i, 2)]
        )

    def gather_side(side):
        steps = cap // 16
        part_heads = slice(side * HG, (side + 1) * HG)

        def body(it, _):
            first = lax.div(it, steps) * LANES + lax.rem(it, steps) * 16
            for e in range(16):
                row = src_ref[0, first + e]
                place = pl.multiple_of((it * 16 + e) * HG, HG)
                for n in range(3):
                    tall[n, pl.ds(place, HG), :] = inbuf[n][row, part_heads, :].astype(F32)
            return 0

        lax.fori_loop(0, seqs * steps, body, 0)

    def gather(i):
        for side in range(HI // HG):

            @pl.when(lax.rem(i, HI // HG) == side)
            def _():
                gather_side(side)

    def update(c):
        def body(g, _):
            here = pl.ds(pl.multiple_of(g * cap, 16), cap)
            until = until_ref[here, :]
            for e in range(HC):
                head = c * HC + e
                j = lax.rem(head, HG)
                cols = pl.ds(pl.multiple_of(head * d, d), d)
                strided = pl.ds(g * cap * HG + j, cap, stride=HG)
                key = tall[0, strided, :]
                value = tall[1, strided, :].astype(BF16)
                weight = jnp.exp(-rate_ref[base + head] * until)
                scaled = (key * weight).astype(BF16)
                packed[0, here, cols] = key.astype(BF16)
                packed[1, here, cols] = value
                packed[2, here, cols] = tall[2, strided, :].astype(BF16)
                change = lax.dot_general(
                    scaled, value, (((0,), (0,)), ((), ())), preferred_element_type=F32
                )
                u_ref[g, head] = change.astype(BF16)
            return 0

        lax.fori_loop(0, seqs, body, 0, unroll=4)
        for j in range(share[0]):
            up_copy(0, c, j).start()

    def up(k, c):
        for j in range(share[k]):
            up_copy(k, c, j).wait_recv()
        first = (bit(k) == 0).astype(F32)

        def body(i, _):
            j, head = lax.div(i, HC), c * HC + lax.rem(i, HC)
            seq = j * 2 ** (k + 1) + low(k + 1)
            own = u_ref[seq, head].astype(F32)
            other = got[k][j, head].astype(F32)
            hi = decay(k, seq, head)
            own_w = first * hi + (1.0 - first)
            other_w = first + (1.0 - first) * hi
            both = own * own_w + other * other_w
            got[k][j, head] = (first * own + (1.0 - first) * other).astype(BF16)
            if k + 1 < levels:
                u_ref[seq, head] = both.astype(BF16)
            else:
                total[head] = both
            return 0

        lax.fori_loop(0, share[k] * HC, body, 0, unroll=2)
        if k + 1 < levels:
            for j in range(share[k + 1]):
                up_copy(k + 1, c, j).start()

    def across(c):
        @pl.when(shard > 0)
        def _():
            z_copy(c, shard).wait_recv()

        def body(i, _):
            head = c * HC + i
            state = zin[head]
            out_ref[me, head] = state.astype(BF16)
            total[head] = state * decay(2 * levels, me, head) + total[head]
            return 0

        lax.fori_loop(0, HC, body, 0)

        @pl.when(shard < shards - 1)
        def _():
            z_copy(c, shard + 1).start()

    def down(k, c):
        if k + 1 < levels:
            for j in range(share[k + 1]):
                down_copy(k + 1, c, j, True).wait_recv()
        first = (bit(k) == 0).astype(F32)

        def body(i, _):
            j, head = lax.div(i, HC), c * HC + lax.rem(i, HC)
            seq = j * 2 ** (k + 1) + low(k + 1)
            start = out_ref[seq, head].astype(F32)
            later = start * decay(levels + k, seq, head) + got[k][j, head].astype(F32)
            out_ref[seq, head] = (first * start + (1.0 - first) * later).astype(BF16)
            got[k][j, head] = (first * later + (1.0 - first) * start).astype(BF16)
            return 0

        lax.fori_loop(0, share[k] * HC, body, 0, unroll=2)
        for j in range(share[k]):
            down_copy(k, c, j, False).start()

    def attend(c):
        i = lax.div(c, per_group)
        side = lax.rem(i, 2)

        @pl.when((lax.rem(c, per_group) == 0) & (i >= 2))
        def _():
            row_copy(i - 2).wait()

        for j in range(share[0]):
            down_copy(0, c, j, True).wait_recv()

        def body(g, _):
            here = pl.ds(pl.multiple_of(g * cap, 16), cap)
            gap = gap_ref[here, :cap]
            since = since_ref[here, :]
            squares = square_ref[here, :]
            for e in range(HC):
                head = c * HC + e
                j = lax.rem(head, HG)
                cols = pl.ds(pl.multiple_of(head * d, d), d)
                rate = rate_ref[base + head]
                query = packed[2, here, cols]
                scores = lax.dot_general(
                    query,
                    packed[0, here, cols],
                    (((1,), (1,)), ((), ())),
                    preferred_element_type=F32,
                )
                half = (scores * jnp.exp(-rate * gap)).astype(BF16)
                intra = jnp.dot(half, packed[1, here, cols], preferred_element_type=F32)
                inter = jnp.dot(query, out_ref[g, head], preferred_element_type=F32)
                mixed = intra + inter * jnp.exp(-rate * since)
                tall[side, pl.ds(g * cap * HG + j, cap, stride=HG), :] = mixed
                squares = squares + mixed * mixed
            square_ref[here, :] = squares
            return 0

        lax.fori_loop(0, seqs, body, 0, unroll=4)

        @pl.when(lax.rem(c, per_group) == per_group - 1)
        def _():
            row_copy(i).start()

    def fact_copy(i, receive):
        owner = lax.rem(me + seqs - i, seqs) if receive else me
        return pltpu.make_async_remote_copy(
            src_ref=fact_ref,
            dst_ref=facts.at[owner],
            send_sem=f_s.at[i - 1],
            recv_sem=f_r.at[i - 1],
            device_id=(lax.rem(me + i, seqs), shard),
            device_id_type=MESH,
        )

    for n in range(3):
        in_copy(n, 0).wait()
    gather_side(0)
    ends = (shard > 0).astype(I32) + (shard < shards - 1).astype(I32)
    pl.semaphore_wait(barrier, seqs - 1 + ends)
    for i in range(1, seqs):
        fact_copy(i, False).start()
    update(0)
    facts[pl.ds(me, 1)] = fact_ref[...][None]
    for i in range(1, seqs):
        fact_copy(i, True).wait_recv()
    spans = [((me // 2 ** (k + 1) * 2 + 1) * 2**k, 2**k) for k in range(levels)]
    spans += [((me // 2 ** (k + 1) * 2) * 2**k, 2**k) for k in range(levels)]
    spans += [(me * 0, seqs)]
    for table, (begin, size) in enumerate(spans):
        count = jnp.zeros(fact_ref.shape[1:], F32)
        docs = jnp.zeros(fact_ref.shape[1:], F32)
        for loader in range(seqs):
            inside = ((loader >= begin) & (loader < begin + size)).astype(F32)
            count = count + facts[loader, 0] * inside
            docs = docs + facts[loader, 1] * inside
        spans_ref[table * seqs : (table + 1) * seqs, :] = jnp.where(docs == 0.0, count, NEVER)

    def fill(head, _):
        dec[head] = jnp.exp(-rate_ref[base + head] * spans_ref[...])
        return 0

    lax.fori_loop(0, heads, fill, 0)

    ups = [1 + UP_LAG * k for k in range(levels)]
    z_first = ups[-1] + 1
    d_first = max(z_first + Z_LAG * (shards - 1) + 1, chunks - levels)
    downs = [d_first + (levels - 1 - k) + (1 if k == 0 else 0) for k in range(levels)]
    a_first = downs[0] + 1

    def during(c):
        return (c >= 0) & (c < chunks)

    def step(t, _):
        fresh = t < chunks

        @pl.when(fresh & (lax.rem(t, per_group) == 0))
        def _():
            i = lax.div(t, per_group)

            @pl.when(lax.rem(t, per_load) == 0)
            def _():
                for n in range(3):
                    in_copy(n, lax.div(t, per_load)).wait()

            gather(i)

            @pl.when((t < chunks - per_load) & (lax.rem(t, per_load) == per_load - per_group))
            def _():
                for n in range(3):
                    in_copy(n, lax.div(t, per_load) + 1).start()

        @pl.when(fresh)
        def _():
            update(t)

        for k in range(levels):

            @pl.when(during(t - ups[k]))
            def _():
                up(k, t - ups[k])

        cz = t - z_first - Z_LAG * shard

        @pl.when(during(cz))
        def _():
            across(cz)

        for k in range(levels - 1, -1, -1):

            @pl.when(during(t - downs[k]))
            def _():
                down(k, t - downs[k])

        @pl.when(during(t - a_first))
        def _():
            attend(t - a_first)

        return 0

    lax.fori_loop(1, chunks + a_first, step, 0)
    for i in range(max(0, heads // HG - 2), heads // HG):
        row_copy(i).wait()

    def settle(c, _):
        for k in range(levels):
            for j in range(share[k]):
                up_copy(k, c, j).wait_send()
                down_copy(k, c, j, False).wait_send()
        return 0

    lax.fori_loop(0, chunks, settle, 0)
    for i in range(1, seqs):
        fact_copy(i, False).wait_send()

    @pl.when(shard < shards - 1)
    def _():
        def settle_z(c, _):
            z_copy(c, shard + 1).wait_send()
            return 0

        lax.fori_loop(0, chunks, settle_z, 0)


def scan_states(prepared, rate, key, value, query, heads, base, levels, shards, cap, call):
    src, facts, until, since, gap = prepared
    d = key.shape[-1]
    rows = key.shape[2]
    seqs = facts.shape[1]
    total = seqs * cap
    chunks = heads // HC
    vm = pltpu.VMEM
    share = [2 ** (levels - k - 1) for k in range(levels)]
    dma = pltpu.SemaphoreType.DMA
    whole = pl.BlockSpec(memory_space=pltpu.VMEM)
    scalar = pl.BlockSpec(memory_space=pltpu.SMEM)
    away = pl.BlockSpec(memory_space=pl.ANY)
    return pl.pallas_call(
        functools.partial(scan_kernel, levels, shards, seqs, heads, cap, base),
        out_shape=[
            jax.ShapeDtypeStruct((heads // HG, total * HG, d), F32),
            jax.ShapeDtypeStruct((total, d), F32),
        ],
        in_specs=[whole, scalar, scalar, whole, whole, whole, away, away, away],
        out_specs=[away, whole],
        scratch_shapes=[
            vm((seqs, heads, d, d), BF16),
            vm((seqs, heads, d, d), BF16),
            vm((3, total, heads * d), BF16),
            vm((3, total * HG, d), F32),
            vm((rows, HI, d), BF16),
            vm((rows, HI, d), BF16),
            vm((rows, HI, d), BF16),
            dma((3,)),
            dma((2,)),
            vm((seqs,) + facts.shape, F32),
            vm(((2 * levels + 1) * seqs, d), F32),
            vm((heads, (2 * levels + 1) * seqs, d), F32),
            dma((seqs - 1,)),
            dma((seqs - 1,)),
            vm((heads, d, d), F32),
            vm((heads, d, d), F32),
            dma((seqs - 1, chunks)),
            dma((seqs - 1, chunks)),
            dma((seqs - 1, chunks)),
            dma((seqs - 1, chunks)),
            dma((chunks,)),
            dma((chunks,)),
        ]
        + [vm((share[k], heads, d, d), BF16) for k in range(levels)],
        compiler_params=pltpu.CompilerParams(
            collective_id=call, has_side_effects=True, vmem_limit_bytes=67043328
        ),
    )(facts, rate, src, until, since, gap, key, value, query)


def finish_kernel(width, flat_ref, square_ref, gain_ref, mixed_ref, o_ref, scale):
    rows = o_ref.shape[0]

    @pl.when(pl.program_id(0) == 0)
    def _():
        mean = jnp.sum(square_ref[...], axis=1, keepdims=True) * (1.0 / width)
        scale[...] = jnp.broadcast_to(lax.rsqrt(mean + eps_norm), scale.shape)

    gains = [gain_ref[b * HG : (b + 1) * HG, :] for b in range(HI // HG)]

    def body(it, _):
        for e in range(8):
            r = it * 8 + e
            place = flat_ref[0, r]
            factor = scale[pl.ds(place, 1), :]
            here = pl.ds(pl.multiple_of(place * HG, HG), HG)
            parts = [mixed_ref[b, here, :] * factor * gains[b] for b in range(HI // HG)]
            o_ref[r] = jnp.concatenate(parts, axis=0).astype(BF16)
        return 0

    lax.fori_loop(0, rows // 8, body, 0)


def finish(flat, squares, gain, mixed):
    rows = flat.shape[1]
    heads, d = gain.shape
    total = squares.shape[0]
    return pl.pallas_call(
        functools.partial(finish_kernel, heads * d),
        grid=(heads // HI,),
        out_shape=jax.ShapeDtypeStruct((rows, heads, d), BF16),
        in_specs=[
            pl.BlockSpec(memory_space=pltpu.SMEM),
            pl.BlockSpec((total, d), lambda i: (0, 0)),
            pl.BlockSpec((HI, d), lambda i: (i, 0)),
            pl.BlockSpec((HI // HG, total * HG, d), lambda i: (i, 0, 0)),
        ],
        out_specs=pl.BlockSpec((rows, HI, d), lambda i: (0, i, 0)),
        scratch_shapes=[pltpu.VMEM((total, d), F32)],
        compiler_params=pltpu.CompilerParams(vmem_limit_bytes=48 * 1024 * 1024),
    )(flat, squares, gain, mixed)


def per_device(queries, key_rows, value_rows, destination, doc_starts, decay_rate, norm_gain):
    loaders = lax.axis_size("dp")
    shards = lax.axis_size("seq")
    rows, heads, d = queries.shape[2:]
    cap = 3 * rows // (2 * loaders)
    levels = loaders.bit_length() - 1
    src, flat, facts, until, since, gap = prepare(destination, doc_starts, loaders, cap)
    passes = max(1, loaders // 8)
    width = heads // passes
    results = []
    for i in range(passes):
        results.append(
            scan_states(
                (src, facts, until, since, gap),
                decay_rate,
                key_rows,
                value_rows,
                queries,
                width,
                i * width,
                levels,
                shards,
                cap,
                i,
            )
        )
    mixed = results[0][0] if passes == 1 else jnp.concatenate([x[0] for x in results], axis=0)
    squares = sum(x[1] for x in results)
    return finish(flat, squares, norm_gain, mixed)[None, None]


def solution(mesh):
    placed = (
        P("dp", "seq", None, None, None),
        P("dp", "seq", None, None, None),
        P("dp", "seq", None, None, None),
        P("dp", "seq", None),
        P("dp", "seq", None),
        P(),
        P(),
    )
    return jax.shard_map(
        per_device,
        mesh=mesh,
        in_specs=placed,
        out_specs=P("dp", "seq", None, None, None),
        check_vma=False,
    )
```

```python
import functools
import jax
import jax.numpy as jnp
from jax import lax
from jax.experimental import pallas as pl
from jax.experimental.pallas import tpu as pltpu
from jax.sharding import PartitionSpec as P

MESH = pl.DeviceIdType.MESH
F32 = jnp.float32
BF16 = jnp.bfloat16
I32 = jnp.int32
eps_norm = 1e-06
LANES = 128
HG = 8
HI = 16
HC = 2
RB = 64
NEVER = 1e30
UP_LAG = 2
Z_LAG = 2


def prepare(seqs, cap, dest_ref, start_ref, src_ref, flat_ref, fact_ref, until_ref, since_ref, gap_ref):
    rows = dest_ref.shape[-1]
    drow = dest_ref[...]
    srow = start_ref[...]
    ci = lax.broadcasted_iota(I32, (LANES, rows), 1)
    ri = lax.broadcasted_iota(I32, (LANES, rows), 0)
    place = lax.broadcasted_iota(I32, (LANES, LANES), 1)
    rlocal = lax.broadcasted_iota(I32, (LANES, 1), 0)
    slot_row = jnp.zeros((1, rows), I32)
    source = [jnp.zeros((1, LANES), I32) for _ in range(seqs)]
    begins = [jnp.zeros((1, LANES), I32) for _ in range(seqs)]
    for b in range(rows // LANES):
        rb = ri + b * LANES
        dcol = jnp.sum(jnp.where(rb == ci, drow, 0), axis=1, keepdims=True)
        scol = jnp.sum(jnp.where(rb == ci, srow, 0), axis=1, keepdims=True)
        same = jnp.where(dcol == drow, 1, 0)
        slot_col = jnp.sum(jnp.where(ci < rb, same, 0), axis=1, keepdims=True)
        slot_row = slot_row + jnp.sum(jnp.where(rb < ci, same, 0), axis=0, keepdims=True)
        slot_wide = dcol * LANES + slot_col
        rcol = rlocal + b * LANES
        for g in range(seqs):
            hit = slot_wide == place + g * LANES
            source[g] = source[g] + jnp.sum(jnp.where(hit, rcol, 0), axis=0, keepdims=True)
            begins[g] = begins[g] + jnp.sum(jnp.where(hit, scol, 0), axis=0, keepdims=True)
    flat_ref[...] = jnp.clip(drow * cap + slot_row, 0, seqs * cap - 1)
    pi = lax.broadcasted_iota(I32, (cap, LANES), 0)
    pj = lax.broadcasted_iota(I32, (cap, LANES), 1)
    position = pi.astype(F32)
    for g in range(seqs):
        src_ref[:, g * LANES : (g + 1) * LANES] = jnp.clip(source[g], 0, rows - 1)
        begin = begins[g].astype(F32)
        number = jnp.sum(jnp.where(drow == g, 1.0, 0.0), axis=1, keepdims=True)
        doc_end = jnp.sum(begin, axis=1, keepdims=True)
        doc_col = jnp.sum(jnp.where(pj <= pi, begin, 0.0), axis=1, keepdims=True)
        begin_col = jnp.sum(jnp.where(pj == pi, begin, 0.0), axis=1, keepdims=True)
        doc_row = jnp.sum(jnp.where(pi <= pj, begin_col, 0.0), axis=0, keepdims=True)
        here = slice(g * cap, (g + 1) * cap)
        fact_ref[0, g : g + 1, :] = jnp.broadcast_to(number, (1, LANES))
        fact_ref[1, g : g + 1, :] = jnp.broadcast_to(doc_end, (1, LANES))
        ends = (position < number) & (doc_col == doc_end)
        until_ref[here, :] = jnp.where(ends, number - 1.0 - position, NEVER)
        since_ref[here, :] = jnp.where(
            jnp.broadcast_to(doc_col, (cap, LANES)) == 0.0, position + 1.0, NEVER
        )
        keep = (pi >= pj) & (doc_col == doc_row)
        gap_ref[here, :] = jnp.where(keep, (pi - pj).astype(F32), NEVER)


def prep_kernel(seqs, cap, dest_hbm, start_hbm, *refs):
    outs, sems = refs[:6], refs[14]
    dest_ref, start_ref = refs[6:8]
    made = refs[8:14]
    loads = [
        pltpu.make_async_copy(dest_hbm.at[0], dest_ref, sems.at[0]),
        pltpu.make_async_copy(start_hbm.at[0], start_ref, sems.at[1]),
    ]
    for copy in loads:
        copy.start()
    for copy in loads:
        copy.wait()
    prepare(seqs, cap, dest_ref, start_ref, *made)
    stores = [pltpu.make_async_copy(made[n], outs[n], sems.at[2 + n]) for n in range(6)]
    for copy in stores:
        copy.start()
    for copy in stores:
        copy.wait()


def prepared(destination, doc_starts, seqs, cap):
    rows = destination.shape[-1]
    total = seqs * cap
    vm = pltpu.VMEM
    away = pl.BlockSpec(memory_space=pl.ANY)
    shapes = [((1, seqs * LANES), I32), ((1, rows), I32), ((2, seqs, LANES), F32)]
    shapes += [((total, LANES), F32)] * 3
    return pl.pallas_call(
        functools.partial(prep_kernel, seqs, cap),
        out_shape=[jax.ShapeDtypeStruct(*shape) for shape in shapes],
        in_specs=[away] * 2,
        out_specs=[away] * 6,
        scratch_shapes=[vm((1, rows), I32), vm((1, rows), I32)]
        + [vm(*shape) for shape in shapes]
        + [pltpu.SemaphoreType.DMA((8,))],
        compiler_params=pltpu.CompilerParams(vmem_limit_bytes=67043328),
    )(destination, doc_starts)


def scan_kernel(levels, shards, seqs, heads, cap, base, *refs):
    rate_ref, src_ref, flat_ref, fact_ref = refs[:4]
    tables_hbm, sources = refs[4:7], refs[7:10]
    mixed_hbm, square_hbm = refs[10:12]
    until_ref, since_ref, gap_ref, square_ref, small_sem = refs[12:17]
    refs = refs[17:]
    u_ref, out_ref, packed = refs[:3]
    tall = refs[3:6]
    inbuf = refs[6:9]
    in_sem, row_sem, facts, spans_ref, dec, f_s, f_r, total, zin = refs[9:18]
    up_s, up_r, dn_s, dn_r, z_s, z_r = refs[18:24]
    got = refs[24:]
    rows = flat_ref.shape[1]
    d = LANES
    me = lax.axis_index("dp")
    shard = lax.axis_index("seq")
    chunks = heads // HC
    per_group = HG // HC
    per_load = HI // HC
    tables = 2 * levels + 1
    share = [2 ** (levels - k - 1) for k in range(levels)]

    def bit(k):
        return lax.rem(lax.div(me, 2**k), 2)

    def partner(k):
        return me + 2**k - bit(k) * (2 ** (k + 1))

    def low(k):
        return lax.rem(me, 2**k)

    def decay(table, seq, head):
        return dec[head, pl.ds(table * seqs + seq, 1), :]

    def in_copy(n, b):
        return pltpu.make_async_copy(
            sources[n].at[0, 0, :, pl.ds(pl.multiple_of(base + b * HI, HI), HI), :],
            inbuf[n],
            in_sem.at[n],
        )

    small = [
        pltpu.make_async_copy(tables_hbm[n], table, small_sem.at[n])
        for n, table in enumerate((until_ref, since_ref, gap_ref))
    ]
    for copy in small:
        copy.start()
    for n in range(3):
        in_copy(n, 0).start()
    barrier = pltpu.get_barrier_semaphore()
    for i in range(1, seqs):
        peer = lax.rem(me + i, seqs)
        pl.semaphore_signal(barrier, inc=1, device_id=(peer, shard), device_id_type=MESH)

    @pl.when(shard > 0)
    def _():
        pl.semaphore_signal(barrier, inc=1, device_id=(me, shard - 1), device_id_type=MESH)

    @pl.when(shard < shards - 1)
    def _():
        pl.semaphore_signal(barrier, inc=1, device_id=(me, shard + 1), device_id_type=MESH)

    @pl.when(shard == 0)
    def _():
        def clear(i, _):
            zin[pl.ds(i, 1)] = jnp.zeros((1,) + zin.shape[1:], zin.dtype)
            return 0

        lax.fori_loop(0, heads, clear, 0)

    square_ref[...] = jnp.zeros(square_ref.shape, F32)

    def part(c):
        return pl.ds(c * HC, HC)

    def slot(k, j):
        return share[k] - 1 + j

    def up_copy(k, c, j):
        seq = j * 2 ** (k + 1) + (1 - bit(k)) * 2**k + low(k)
        return pltpu.make_async_remote_copy(
            src_ref=u_ref.at[seq, part(c)],
            dst_ref=got[k].at[j, part(c)],
            send_sem=up_s.at[slot(k, j), c],
            recv_sem=up_r.at[slot(k, j), c],
            device_id=(partner(k), shard),
            device_id_type=MESH,
        )

    def down_copy(k, c, j, receive):
        owner = partner(k) if receive else me
        seq = j * 2 ** (k + 1) + lax.rem(owner, 2 ** (k + 1))
        return pltpu.make_async_remote_copy(
            src_ref=got[k].at[j, part(c)],
            dst_ref=out_ref.at[seq, part(c)],
            send_sem=dn_s.at[slot(k, j), c],
            recv_sem=dn_r.at[slot(k, j), c],
            device_id=(partner(k), shard),
            device_id_type=MESH,
        )

    def z_copy(c, target):
        return pltpu.make_async_remote_copy(
            src_ref=total.at[part(c)],
            dst_ref=zin.at[part(c)],
            send_sem=z_s.at[c],
            recv_sem=z_r.at[c],
            device_id=(me, target),
            device_id_type=MESH,
        )

    def row_copy(i):
        return pltpu.make_async_copy(
            tall[2].at[pl.ds(0, rows * HG)], mixed_hbm.at[i], row_sem.at[0]
        )

    def rows_back():
        slots = tall[0].reshape(seqs * cap, HG, d)

        def body(it, _):
            for e in range(16):
                place = flat_ref[0, it * 16 + e]
                target = pl.multiple_of((it * 16 + e) * HG, HG)
                tall[2][pl.ds(target, HG), :] = slots[place]
            return 0

        lax.fori_loop(0, rows // 16, body, 0)

    def gather_side(side):
        steps = cap // 16
        part_heads = slice(side * HG, (side + 1) * HG)

        def body(it, _):
            first = lax.div(it, steps) * LANES + lax.rem(it, steps) * 16
            for e in range(16):
                row = src_ref[0, first + e]
                place = pl.multiple_of((it * 16 + e) * HG, HG)
                for n in range(3):
                    tall[n][pl.ds(place, HG), :] = inbuf[n][row, part_heads, :].astype(F32)
            return 0

        lax.fori_loop(0, seqs * steps, body, 0)

    def gather(i):
        for side in range(HI // HG):

            @pl.when(lax.rem(i, HI // HG) == side)
            def _():
                gather_side(side)

    def update(c):
        def body(g, _):
            here = pl.ds(pl.multiple_of(g * cap, 16), cap)
            until = until_ref[here, :]
            for e in range(HC):
                head = c * HC + e
                j = lax.rem(head, HG)
                cols = pl.ds(pl.multiple_of(head * d, d), d)
                strided = pl.ds(g * cap * HG + j, cap, stride=HG)
                key = tall[0][strided, :]
                value = tall[1][strided, :].astype(BF16)
                weight = jnp.exp(-rate_ref[base + head] * until)
                scaled = (key * weight).astype(BF16)
                packed[0, here, cols] = key.astype(BF16)
                packed[1, here, cols] = value
                packed[2, here, cols] = tall[2][strided, :].astype(BF16)
                change = lax.dot_general(
                    scaled, value, (((0,), (0,)), ((), ())), preferred_element_type=F32
                )
                u_ref[g, head] = change.astype(BF16)
            return 0

        lax.fori_loop(0, seqs, body, 0, unroll=4)
        for j in range(share[0]):
            up_copy(0, c, j).start()

    def up(k, c):
        for j in range(share[k]):
            up_copy(k, c, j).wait_recv()
        first = (bit(k) == 0).astype(F32)

        def body(i, _):
            j, head = lax.div(i, HC), c * HC + lax.rem(i, HC)
            seq = j * 2 ** (k + 1) + low(k + 1)
            own = u_ref[seq, head].astype(F32)
            other = got[k][j, head].astype(F32)
            hi = decay(k, seq, head)
            own_w = first * hi + (1.0 - first)
            other_w = first + (1.0 - first) * hi
            both = own * own_w + other * other_w
            got[k][j, head] = (first * own + (1.0 - first) * other).astype(BF16)
            if k + 1 < levels:
                u_ref[seq, head] = both.astype(BF16)
            else:
                total[head] = both
            return 0

        lax.fori_loop(0, share[k] * HC, body, 0, unroll=2)
        if k + 1 < levels:
            for j in range(share[k + 1]):
                up_copy(k + 1, c, j).start()

    def across(c):
        @pl.when(shard > 0)
        def _():
            z_copy(c, shard).wait_recv()

        def body(i, _):
            head = c * HC + i
            state = zin[head]
            out_ref[me, head] = state.astype(BF16)
            total[head] = state * decay(2 * levels, me, head) + total[head]
            return 0

        lax.fori_loop(0, HC, body, 0)

        @pl.when(shard < shards - 1)
        def _():
            z_copy(c, shard + 1).start()

    def down(k, c):
        if k + 1 < levels:
            for j in range(share[k + 1]):
                down_copy(k + 1, c, j, True).wait_recv()
        first = (bit(k) == 0).astype(F32)

        def body(i, _):
            j, head = lax.div(i, HC), c * HC + lax.rem(i, HC)
            seq = j * 2 ** (k + 1) + low(k + 1)
            start = out_ref[seq, head].astype(F32)
            later = start * decay(levels + k, seq, head) + got[k][j, head].astype(F32)
            out_ref[seq, head] = (first * start + (1.0 - first) * later).astype(BF16)
            got[k][j, head] = (first * later + (1.0 - first) * start).astype(BF16)
            return 0

        lax.fori_loop(0, share[k] * HC, body, 0, unroll=2)
        for j in range(share[k]):
            down_copy(k, c, j, False).start()

    def attend(c):
        i = lax.div(c, per_group)
        for j in range(share[0]):
            down_copy(0, c, j, True).wait_recv()

        def body(g, _):
            here = pl.ds(pl.multiple_of(g * cap, 16), cap)
            gap = gap_ref[here, :cap]
            since = since_ref[here, :]
            squares = square_ref[here, :]
            for e in range(HC):
                head = c * HC + e
                j = lax.rem(head, HG)
                cols = pl.ds(pl.multiple_of(head * d, d), d)
                rate = rate_ref[base + head]
                query = packed[2, here, cols]
                scores = lax.dot_general(
                    query,
                    packed[0, here, cols],
                    (((1,), (1,)), ((), ())),
                    preferred_element_type=F32,
                )
                half = (scores * jnp.exp(-rate * gap)).astype(BF16)
                intra = jnp.dot(half, packed[1, here, cols], preferred_element_type=F32)
                inter = jnp.dot(query, out_ref[g, head], preferred_element_type=F32)
                mixed = intra + inter * jnp.exp(-rate * since)
                tall[0][pl.ds(g * cap * HG + j, cap, stride=HG), :] = mixed
                squares = squares + mixed * mixed
            square_ref[here, :] = squares
            return 0

        lax.fori_loop(0, seqs, body, 0, unroll=4)

        @pl.when(lax.rem(c, per_group) == per_group - 1)
        def _():
            @pl.when(i > 0)
            def _():
                row_copy(i - 1).wait()

            rows_back()
            row_copy(i).start()

    def fact_copy(i, receive):
        owner = lax.rem(me + seqs - i, seqs) if receive else me
        return pltpu.make_async_remote_copy(
            src_ref=fact_ref,
            dst_ref=facts.at[owner],
            send_sem=f_s.at[i - 1],
            recv_sem=f_r.at[i - 1],
            device_id=(lax.rem(me + i, seqs), shard),
            device_id_type=MESH,
        )

    ends = (shard > 0).astype(I32) + (shard < shards - 1).astype(I32)
    pl.semaphore_wait(barrier, seqs - 1 + ends)
    for i in range(1, seqs):
        fact_copy(i, False).start()
    for n in range(3):
        in_copy(n, 0).wait()
    gather_side(0)
    for copy in small:
        copy.wait()
    update(0)
    facts[pl.ds(me, 1)] = fact_ref[...][None]
    for i in range(1, seqs):
        fact_copy(i, True).wait_recv()
    spans = [((me // 2 ** (k + 1) * 2 + 1) * 2**k, 2**k) for k in range(levels)]
    spans += [((me // 2 ** (k + 1) * 2) * 2**k, 2**k) for k in range(levels)]
    spans += [(me * 0, seqs)]
    for table, (begin, size) in enumerate(spans):
        count = jnp.zeros(fact_ref.shape[1:], F32)
        docs = jnp.zeros(fact_ref.shape[1:], F32)
        for loader in range(seqs):
            inside = ((loader >= begin) & (loader < begin + size)).astype(F32)
            count = count + facts[loader, 0] * inside
            docs = docs + facts[loader, 1] * inside
        spans_ref[table * seqs : (table + 1) * seqs, :] = jnp.where(docs == 0.0, count, NEVER)

    def fill(head, _):
        dec[head] = jnp.exp(-rate_ref[base + head] * spans_ref[...])
        return 0

    lax.fori_loop(0, heads, fill, 0)

    ups = [1 + UP_LAG * k for k in range(levels)]
    z_first = ups[-1] + 1
    d_first = max(z_first + Z_LAG * (shards - 1) + 1, chunks - levels)
    downs = [d_first + (levels - 1 - k) + (1 if k == 0 else 0) for k in range(levels)]
    a_first = downs[0] + 1

    def during(c):
        return (c >= 0) & (c < chunks)

    def step(t, _):
        fresh = t < chunks

        @pl.when(fresh & (lax.rem(t, per_group) == 0))
        def _():
            i = lax.div(t, per_group)

            @pl.when(lax.rem(t, per_load) == 0)
            def _():
                for n in range(3):
                    in_copy(n, lax.div(t, per_load)).wait()

            gather(i)

            @pl.when((t < chunks - per_load) & (lax.rem(t, per_load) == per_load - per_group))
            def _():
                for n in range(3):
                    in_copy(n, lax.div(t, per_load) + 1).start()

        @pl.when(fresh)
        def _():
            update(t)

        for k in range(levels):

            @pl.when(during(t - ups[k]))
            def _():
                up(k, t - ups[k])

        cz = t - z_first - Z_LAG * shard

        @pl.when(during(cz))
        def _():
            across(cz)

        for k in range(levels - 1, -1, -1):

            @pl.when(during(t - downs[k]))
            def _():
                down(k, t - downs[k])

        @pl.when(during(t - a_first))
        def _():
            attend(t - a_first)
            settle(t - a_first)

        return 0

    def settle(c):
        for k in range(levels):
            for j in range(share[k]):
                up_copy(k, c, j).wait_send()
                down_copy(k, c, j, False).wait_send()

        @pl.when(shard < shards - 1)
        def _():
            z_copy(c, shard + 1).wait_send()

    lax.fori_loop(1, chunks + a_first, step, 0)
    square_copy = pltpu.make_async_copy(square_ref, square_hbm, small_sem.at[0])
    square_copy.start()
    square_copy.wait()
    row_copy(heads // HG - 1).wait()
    for i in range(1, seqs):
        fact_copy(i, False).wait_send()


def scan_states(rate, tables, key, value, query, heads, base, levels, seqs, shards, cap, call):
    d = key.shape[-1]
    rows = key.shape[2]
    total = seqs * cap
    chunks = heads // HC
    vm = pltpu.VMEM
    share = [2 ** (levels - k - 1) for k in range(levels)]
    dma = pltpu.SemaphoreType.DMA
    away = pl.BlockSpec(memory_space=pl.ANY)
    whole = pl.BlockSpec(memory_space=pltpu.VMEM)
    scalar = pl.BlockSpec(memory_space=pltpu.SMEM)
    return pl.pallas_call(
        functools.partial(scan_kernel, levels, shards, seqs, heads, cap, base),
        out_shape=[
            jax.ShapeDtypeStruct((heads // HG, rows * HG, d), F32),
            jax.ShapeDtypeStruct((total, d), F32),
        ],
        in_specs=[scalar, scalar, scalar, whole] + [away] * 6,
        out_specs=[away, away],
        scratch_shapes=[
            vm((total, LANES), F32),
            vm((total, LANES), F32),
            vm((total, LANES), F32),
            vm((total, d), F32),
            dma((3,)),
            vm((seqs, heads, d, d), BF16),
            vm((seqs, heads, d, d), BF16),
            vm((3, total, heads * d), BF16),
            vm((total * HG, d), F32),
            vm((total * HG, d), F32),
            vm((total * HG, d), F32),
            vm((rows, HI, d), BF16),
            vm((rows, HI, d), BF16),
            vm((rows, HI, d), BF16),
            dma((3,)),
            dma((1,)),
            vm((seqs, 2, seqs, LANES), F32),
            vm(((2 * levels + 1) * seqs, d), F32),
            vm((heads, (2 * levels + 1) * seqs, d), F32),
            dma((seqs - 1,)),
            dma((seqs - 1,)),
            vm((heads, d, d), F32),
            vm((heads, d, d), F32),
            dma((seqs - 1, chunks)),
            dma((seqs - 1, chunks)),
            dma((seqs - 1, chunks)),
            dma((seqs - 1, chunks)),
            dma((chunks,)),
            dma((chunks,)),
        ]
        + [vm((share[k], heads, d, d), BF16) for k in range(levels)],
        compiler_params=pltpu.CompilerParams(
            collective_id=call, has_side_effects=True, vmem_limit_bytes=67043328
        ),
    )(rate, *tables, key, value, query)


def finish_kernel(width, flat_ref, square_ref, gain_ref, mixed_ref, o_ref, scale):
    block = pl.program_id(0)

    @pl.when(block == 0)
    def _():
        mean = jnp.sum(square_ref[...], axis=1, keepdims=True) * (1.0 / width)
        scale[...] = jnp.broadcast_to(lax.rsqrt(mean + eps_norm), scale.shape)

    groups = mixed_ref.shape[0]
    gains = [gain_ref[b * HG : (b + 1) * HG, :] for b in range(groups)]

    def body(it, _):
        for e in range(16):
            r = it * 16 + e
            factor = scale[pl.ds(flat_ref[0, block * RB + r], 1), :]
            here = pl.ds(pl.multiple_of(r * HG, HG), HG)
            parts = [mixed_ref[b, here, :] * factor * gains[b] for b in range(groups)]
            o_ref[r] = jnp.concatenate(parts, axis=0).astype(BF16)
        return 0

    lax.fori_loop(0, RB // 16, body, 0)


def finish(flat, squares, gain, mixed):
    rows = flat.shape[1]
    heads, d = gain.shape
    total = squares.shape[0]
    return pl.pallas_call(
        functools.partial(finish_kernel, heads * d),
        grid=(rows // RB,),
        out_shape=jax.ShapeDtypeStruct((rows, heads, d), BF16),
        in_specs=[
            pl.BlockSpec(memory_space=pltpu.SMEM),
            pl.BlockSpec((total, d), lambda i: (0, 0)),
            pl.BlockSpec((heads, d), lambda i: (0, 0)),
            pl.BlockSpec((heads // HG, RB * HG, d), lambda i: (0, i, 0)),
        ],
        out_specs=pl.BlockSpec((RB, heads, d), lambda i: (i, 0, 0)),
        scratch_shapes=[pltpu.VMEM((total, d), F32)],
        compiler_params=pltpu.CompilerParams(vmem_limit_bytes=67043328),
    )(flat, squares, gain, mixed)


def per_device(queries, key_rows, value_rows, destination, doc_starts, decay_rate, norm_gain):
    loaders = lax.axis_size("dp")
    shards = lax.axis_size("seq")
    rows, heads, d = queries.shape[2:]
    cap = 3 * rows // (2 * loaders)
    levels = loaders.bit_length() - 1
    tables = prepared(destination, doc_starts, loaders, cap)
    passes = max(1, loaders // 8)
    width = heads // passes
    results = []
    for i in range(passes):
        results.append(
            scan_states(
                decay_rate,
                tables,
                key_rows,
                value_rows,
                queries,
                width,
                i * width,
                levels,
                loaders,
                shards,
                cap,
                i,
            )
        )
    mixed = results[0][0] if passes == 1 else jnp.concatenate([x[0] for x in results], axis=0)
    squares = sum(x[1] for x in results[1:]) + results[0][1] if passes > 1 else results[0][1]
    return finish(tables[1], squares, norm_gain, mixed)[None, None]


def solution(mesh):
    placed = (
        P("dp", "seq", None, None, None),
        P("dp", "seq", None, None, None),
        P("dp", "seq", None, None, None),
        P("dp", "seq", None),
        P("dp", "seq", None),
        P(),
        P(),
    )
    return jax.shard_map(
        per_device,
        mesh=mesh,
        in_specs=placed,
        out_specs=P("dp", "seq", None, None, None),
        check_vma=False,
    )
```

```python
import functools
import jax
import jax.numpy as jnp
from jax import lax
from jax.experimental import pallas as pl
from jax.experimental.pallas import tpu as pltpu
from jax.sharding import PartitionSpec as P

MESH = pl.DeviceIdType.MESH
F32 = jnp.float32
BF16 = jnp.bfloat16
I32 = jnp.int32
eps_norm = 1e-06
LANES = 128
HG = 8
HI = 16
HC = 2
RB = 64
NEVER = 1e30
UP_LAG = 2
Z_LAG = 2


def prepare(seqs, cap, dest_ref, start_ref, src_ref, flat_ref, fact_ref, until_ref, since_ref, gap_ref):
    rows = dest_ref.shape[-1]
    drow = dest_ref[...]
    srow = start_ref[...]
    ci = lax.broadcasted_iota(I32, (LANES, rows), 1)
    ri = lax.broadcasted_iota(I32, (LANES, rows), 0)
    place = lax.broadcasted_iota(I32, (LANES, LANES), 1)
    rlocal = lax.broadcasted_iota(I32, (LANES, 1), 0)
    slot_row = jnp.zeros((1, rows), I32)
    source = [jnp.zeros((1, LANES), I32) for _ in range(seqs)]
    begins = [jnp.zeros((1, LANES), I32) for _ in range(seqs)]
    for b in range(rows // LANES):
        rb = ri + b * LANES
        dcol = jnp.sum(jnp.where(rb == ci, drow, 0), axis=1, keepdims=True)
        scol = jnp.sum(jnp.where(rb == ci, srow, 0), axis=1, keepdims=True)
        same = jnp.where(dcol == drow, 1, 0)
        slot_col = jnp.sum(jnp.where(ci < rb, same, 0), axis=1, keepdims=True)
        slot_row = slot_row + jnp.sum(jnp.where(rb < ci, same, 0), axis=0, keepdims=True)
        slot_wide = dcol * LANES + slot_col
        rcol = rlocal + b * LANES
        for g in range(seqs):
            hit = slot_wide == place + g * LANES
            source[g] = source[g] + jnp.sum(jnp.where(hit, rcol, 0), axis=0, keepdims=True)
            begins[g] = begins[g] + jnp.sum(jnp.where(hit, scol, 0), axis=0, keepdims=True)
    flat_ref[...] = jnp.clip(drow * cap + slot_row, 0, seqs * cap - 1)
    pi = lax.broadcasted_iota(I32, (cap, LANES), 0)
    pj = lax.broadcasted_iota(I32, (cap, LANES), 1)
    position = pi.astype(F32)
    for g in range(seqs):
        src_ref[:, g * LANES : (g + 1) * LANES] = jnp.clip(source[g], 0, rows - 1)
        begin = begins[g].astype(F32)
        number = jnp.sum(jnp.where(drow == g, 1.0, 0.0), axis=1, keepdims=True)
        doc_end = jnp.sum(begin, axis=1, keepdims=True)
        doc_col = jnp.sum(jnp.where(pj <= pi, begin, 0.0), axis=1, keepdims=True)
        begin_col = jnp.sum(jnp.where(pj == pi, begin, 0.0), axis=1, keepdims=True)
        doc_row = jnp.sum(jnp.where(pi <= pj, begin_col, 0.0), axis=0, keepdims=True)
        here = slice(g * cap, (g + 1) * cap)
        fact_ref[0, g : g + 1, :] = jnp.broadcast_to(number, (1, LANES))
        fact_ref[1, g : g + 1, :] = jnp.broadcast_to(doc_end, (1, LANES))
        ends = (position < number) & (doc_col == doc_end)
        until_ref[here, :] = jnp.where(ends, number - 1.0 - position, NEVER)
        since_ref[here, :] = jnp.where(
            jnp.broadcast_to(doc_col, (cap, LANES)) == 0.0, position + 1.0, NEVER
        )
        keep = (pi >= pj) & (doc_col == doc_row)
        gap_ref[here, :] = jnp.where(keep, (pi - pj).astype(F32), NEVER)


def scan_kernel(levels, shards, seqs, heads, cap, base, *refs):
    rate_ref, dest_hbm, start_hbm = refs[:3]
    sources = refs[3:6]
    mixed_hbm, square_hbm, flat_hbm = refs[6:9]
    src_ref, flat_ref, dest_ref, start_ref, src_row, flat_row = refs[9:15]
    fact_ref, until_ref, since_ref, gap_ref, square_ref, small_sem = refs[15:21]
    refs = refs[21:]
    u_ref, out_ref, packed = refs[:3]
    tall = refs[3:6]
    inbuf = refs[6:9]
    in_sem, row_sem, facts, spans_ref, dec, f_s, f_r, total, zin = refs[9:18]
    up_s, up_r, dn_s, dn_r, z_s, z_r = refs[18:24]
    got = refs[24:]
    rows = flat_ref.shape[1]
    d = LANES
    me = lax.axis_index("dp")
    shard = lax.axis_index("seq")
    chunks = heads // HC
    per_group = HG // HC
    per_load = HI // HC
    tables = 2 * levels + 1
    share = [2 ** (levels - k - 1) for k in range(levels)]

    def bit(k):
        return lax.rem(lax.div(me, 2**k), 2)

    def partner(k):
        return me + 2**k - bit(k) * (2 ** (k + 1))

    def low(k):
        return lax.rem(me, 2**k)

    def decay(table, seq, head):
        return dec[head, pl.ds(table * seqs + seq, 1), :]

    def in_copy(n, b):
        return pltpu.make_async_copy(
            sources[n].at[0, 0, :, pl.ds(pl.multiple_of(base + b * HI, HI), HI), :],
            inbuf[n],
            in_sem.at[n],
        )

    loads = [
        pltpu.make_async_copy(dest_hbm.at[0], dest_ref, small_sem.at[0]),
        pltpu.make_async_copy(start_hbm.at[0], start_ref, small_sem.at[1]),
    ]
    moves = [
        pltpu.make_async_copy(src_row, src_ref, small_sem.at[2]),
        pltpu.make_async_copy(flat_row, flat_ref, small_sem.at[3]),
        pltpu.make_async_copy(flat_row, flat_hbm, small_sem.at[4]),
    ]
    for copy in loads:
        copy.start()
    for n in range(3):
        in_copy(n, 0).start()
    barrier = pltpu.get_barrier_semaphore()
    for i in range(1, seqs):
        peer = lax.rem(me + i, seqs)
        pl.semaphore_signal(barrier, inc=1, device_id=(peer, shard), device_id_type=MESH)

    @pl.when(shard > 0)
    def _():
        pl.semaphore_signal(barrier, inc=1, device_id=(me, shard - 1), device_id_type=MESH)

    @pl.when(shard < shards - 1)
    def _():
        pl.semaphore_signal(barrier, inc=1, device_id=(me, shard + 1), device_id_type=MESH)

    @pl.when(shard == 0)
    def _():
        def clear(i, _):
            zin[pl.ds(i, 1)] = jnp.zeros((1,) + zin.shape[1:], zin.dtype)
            return 0

        lax.fori_loop(0, heads, clear, 0)

    square_ref[...] = jnp.zeros(square_ref.shape, F32)
    for copy in loads:
        copy.wait()
    prepare(
        seqs, cap, dest_ref, start_ref, src_row, flat_row, fact_ref, until_ref, since_ref, gap_ref
    )
    for copy in moves:
        copy.start()

    def part(c):
        return pl.ds(c * HC, HC)

    def slot(k, j):
        return share[k] - 1 + j

    def up_copy(k, c, j):
        seq = j * 2 ** (k + 1) + (1 - bit(k)) * 2**k + low(k)
        return pltpu.make_async_remote_copy(
            src_ref=u_ref.at[seq, part(c)],
            dst_ref=got[k].at[j, part(c)],
            send_sem=up_s.at[slot(k, j), c],
            recv_sem=up_r.at[slot(k, j), c],
            device_id=(partner(k), shard),
            device_id_type=MESH,
        )

    def down_copy(k, c, j, receive):
        owner = partner(k) if receive else me
        seq = j * 2 ** (k + 1) + lax.rem(owner, 2 ** (k + 1))
        return pltpu.make_async_remote_copy(
            src_ref=got[k].at[j, part(c)],
            dst_ref=out_ref.at[seq, part(c)],
            send_sem=dn_s.at[slot(k, j), c],
            recv_sem=dn_r.at[slot(k, j), c],
            device_id=(partner(k), shard),
            device_id_type=MESH,
        )

    def z_copy(c, target):
        return pltpu.make_async_remote_copy(
            src_ref=total.at[part(c)],
            dst_ref=zin.at[part(c)],
            send_sem=z_s.at[c],
            recv_sem=z_r.at[c],
            device_id=(me, target),
            device_id_type=MESH,
        )

    def row_copy(i):
        return pltpu.make_async_copy(
            tall[2].at[pl.ds(0, rows * HG)], mixed_hbm.at[i], row_sem.at[0]
        )

    def rows_back():
        slots = tall[0].reshape(seqs * cap, HG, d)

        def body(it, _):
            for e in range(16):
                place = flat_ref[0, it * 16 + e]
                target = pl.multiple_of((it * 16 + e) * HG, HG)
                tall[2][pl.ds(target, HG), :] = slots[place]
            return 0

        lax.fori_loop(0, rows // 16, body, 0)

    def gather_side(side):
        steps = cap // 16
        part_heads = slice(side * HG, (side + 1) * HG)

        def body(it, _):
            first = lax.div(it, steps) * LANES + lax.rem(it, steps) * 16
            for e in range(16):
                row = src_ref[0, first + e]
                place = pl.multiple_of((it * 16 + e) * HG, HG)
                for n in range(3):
                    tall[n][pl.ds(place, HG), :] = inbuf[n][row, part_heads, :].astype(F32)
            return 0

        lax.fori_loop(0, seqs * steps, body, 0)

    def gather(i):
        for side in range(HI // HG):

            @pl.when(lax.rem(i, HI // HG) == side)
            def _():
                gather_side(side)

    def update(c):
        def body(g, _):
            here = pl.ds(pl.multiple_of(g * cap, 16), cap)
            until = until_ref[here, :]
            for e in range(HC):
                head = c * HC + e
                j = lax.rem(head, HG)
                cols = pl.ds(pl.multiple_of(head * d, d), d)
                strided = pl.ds(g * cap * HG + j, cap, stride=HG)
                key = tall[0][strided, :]
                value = tall[1][strided, :].astype(BF16)
                weight = jnp.exp(-rate_ref[base + head] * until)
                scaled = (key * weight).astype(BF16)
                packed[0, here, cols] = key.astype(BF16)
                packed[1, here, cols] = value
                packed[2, here, cols] = tall[2][strided, :].astype(BF16)
                change = lax.dot_general(
                    scaled, value, (((0,), (0,)), ((), ())), preferred_element_type=F32
                )
                u_ref[g, head] = change.astype(BF16)
            return 0

        lax.fori_loop(0, seqs, body, 0, unroll=4)
        for j in range(share[0]):
            up_copy(0, c, j).start()

    def up(k, c):
        for j in range(share[k]):
            up_copy(k, c, j).wait_recv()
        first = (bit(k) == 0).astype(F32)

        def body(i, _):
            j, head = lax.div(i, HC), c * HC + lax.rem(i, HC)
            seq = j * 2 ** (k + 1) + low(k + 1)
            own = u_ref[seq, head].astype(F32)
            other = got[k][j, head].astype(F32)
            hi = decay(k, seq, head)
            own_w = first * hi + (1.0 - first)
            other_w = first + (1.0 - first) * hi
            both = own * own_w + other * other_w
            got[k][j, head] = (first * own + (1.0 - first) * other).astype(BF16)
            if k + 1 < levels:
                u_ref[seq, head] = both.astype(BF16)
            else:
                total[head] = both
            return 0

        lax.fori_loop(0, share[k] * HC, body, 0, unroll=2)
        if k + 1 < levels:
            for j in range(share[k + 1]):
                up_copy(k + 1, c, j).start()

    def across(c):
        @pl.when(shard > 0)
        def _():
            z_copy(c, shard).wait_recv()

        def body(i, _):
            head = c * HC + i
            state = zin[head]
            out_ref[me, head] = state.astype(BF16)
            total[head] = state * decay(2 * levels, me, head) + total[head]
            return 0

        lax.fori_loop(0, HC, body, 0)

        @pl.when(shard < shards - 1)
        def _():
            z_copy(c, shard + 1).start()

    def down(k, c):
        if k + 1 < levels:
            for j in range(share[k + 1]):
                down_copy(k + 1, c, j, True).wait_recv()
        first = (bit(k) == 0).astype(F32)

        def body(i, _):
            j, head = lax.div(i, HC), c * HC + lax.rem(i, HC)
            seq = j * 2 ** (k + 1) + low(k + 1)
            start = out_ref[seq, head].astype(F32)
            later = start * decay(levels + k, seq, head) + got[k][j, head].astype(F32)
            out_ref[seq, head] = (first * start + (1.0 - first) * later).astype(BF16)
            got[k][j, head] = (first * later + (1.0 - first) * start).astype(BF16)
            return 0

        lax.fori_loop(0, share[k] * HC, body, 0, unroll=2)
        for j in range(share[k]):
            down_copy(k, c, j, False).start()

    def attend(c):
        i = lax.div(c, per_group)
        for j in range(share[0]):
            down_copy(0, c, j, True).wait_recv()

        def body(g, _):
            here = pl.ds(pl.multiple_of(g * cap, 16), cap)
            gap = gap_ref[here, :cap]
            since = since_ref[here, :]
            squares = square_ref[here, :]
            for e in range(HC):
                head = c * HC + e
                j = lax.rem(head, HG)
                cols = pl.ds(pl.multiple_of(head * d, d), d)
                rate = rate_ref[base + head]
                query = packed[2, here, cols]
                scores = lax.dot_general(
                    query,
                    packed[0, here, cols],
                    (((1,), (1,)), ((), ())),
                    preferred_element_type=F32,
                )
                half = (scores * jnp.exp(-rate * gap)).astype(BF16)
                intra = jnp.dot(half, packed[1, here, cols], preferred_element_type=F32)
                inter = jnp.dot(query, out_ref[g, head], preferred_element_type=F32)
                mixed = intra + inter * jnp.exp(-rate * since)
                tall[0][pl.ds(g * cap * HG + j, cap, stride=HG), :] = mixed
                squares = squares + mixed * mixed
            square_ref[here, :] = squares
            return 0

        lax.fori_loop(0, seqs, body, 0, unroll=4)

        @pl.when(lax.rem(c, per_group) == per_group - 1)
        def _():
            @pl.when(i > 0)
            def _():
                row_copy(i - 1).wait()

            rows_back()
            row_copy(i).start()

    def fact_copy(i, receive):
        owner = lax.rem(me + seqs - i, seqs) if receive else me
        return pltpu.make_async_remote_copy(
            src_ref=fact_ref,
            dst_ref=facts.at[owner],
            send_sem=f_s.at[i - 1],
            recv_sem=f_r.at[i - 1],
            device_id=(lax.rem(me + i, seqs), shard),
            device_id_type=MESH,
        )

    ends = (shard > 0).astype(I32) + (shard < shards - 1).astype(I32)
    pl.semaphore_wait(barrier, seqs - 1 + ends)
    for i in range(1, seqs):
        fact_copy(i, False).start()
    for copy in moves:
        copy.wait()
    for n in range(3):
        in_copy(n, 0).wait()
    gather_side(0)
    update(0)
    facts[pl.ds(me, 1)] = fact_ref[...][None]
    for i in range(1, seqs):
        fact_copy(i, True).wait_recv()
    spans = [((me // 2 ** (k + 1) * 2 + 1) * 2**k, 2**k) for k in range(levels)]
    spans += [((me // 2 ** (k + 1) * 2) * 2**k, 2**k) for k in range(levels)]
    spans += [(me * 0, seqs)]
    for table, (begin, size) in enumerate(spans):
        count = jnp.zeros(fact_ref.shape[1:], F32)
        docs = jnp.zeros(fact_ref.shape[1:], F32)
        for loader in range(seqs):
            inside = ((loader >= begin) & (loader < begin + size)).astype(F32)
            count = count + facts[loader, 0] * inside
            docs = docs + facts[loader, 1] * inside
        spans_ref[table * seqs : (table + 1) * seqs, :] = jnp.where(docs == 0.0, count, NEVER)

    def fill(head, _):
        dec[head] = jnp.exp(-rate_ref[base + head] * spans_ref[...])
        return 0

    lax.fori_loop(0, heads, fill, 0)

    ups = [1 + UP_LAG * k for k in range(levels)]
    z_first = ups[-1] + 1
    d_first = max(z_first + Z_LAG * (shards - 1) + 1, chunks - levels)
    downs = [d_first + (levels - 1 - k) + (1 if k == 0 else 0) for k in range(levels)]
    a_first = downs[0] + 1

    def during(c):
        return (c >= 0) & (c < chunks)

    def step(t, _):
        fresh = t < chunks

        @pl.when(fresh & (lax.rem(t, per_group) == 0))
        def _():
            i = lax.div(t, per_group)

            @pl.when(lax.rem(t, per_load) == 0)
            def _():
                for n in range(3):
                    in_copy(n, lax.div(t, per_load)).wait()

            gather(i)

            @pl.when((t < chunks - per_load) & (lax.rem(t, per_load) == per_load - per_group))
            def _():
                for n in range(3):
                    in_copy(n, lax.div(t, per_load) + 1).start()

        @pl.when(fresh)
        def _():
            update(t)

        for k in range(levels):

            @pl.when(during(t - ups[k]))
            def _():
                up(k, t - ups[k])

        cz = t - z_first - Z_LAG * shard

        @pl.when(during(cz))
        def _():
            across(cz)

        for k in range(levels - 1, -1, -1):

            @pl.when(during(t - downs[k]))
            def _():
                down(k, t - downs[k])

        @pl.when(during(t - a_first))
        def _():
            attend(t - a_first)
            settle(t - a_first)

        return 0

    def settle(c):
        for k in range(levels):
            for j in range(share[k]):
                up_copy(k, c, j).wait_send()
                down_copy(k, c, j, False).wait_send()

        @pl.when(shard < shards - 1)
        def _():
            z_copy(c, shard + 1).wait_send()

    lax.fori_loop(1, chunks + a_first, step, 0)
    square_copy = pltpu.make_async_copy(square_ref, square_hbm, small_sem.at[0])
    square_copy.start()
    square_copy.wait()
    row_copy(heads // HG - 1).wait()
    for i in range(1, seqs):
        fact_copy(i, False).wait_send()


def scan_states(rate, destination, doc_starts, key, value, query, heads, base, levels, seqs, shards, cap, call):
    d = key.shape[-1]
    rows = key.shape[2]
    total = seqs * cap
    chunks = heads // HC
    vm = pltpu.VMEM
    share = [2 ** (levels - k - 1) for k in range(levels)]
    dma = pltpu.SemaphoreType.DMA
    away = pl.BlockSpec(memory_space=pl.ANY)
    scalar = pl.BlockSpec(memory_space=pltpu.SMEM)
    return pl.pallas_call(
        functools.partial(scan_kernel, levels, shards, seqs, heads, cap, base),
        out_shape=[
            jax.ShapeDtypeStruct((heads // HG, rows * HG, d), F32),
            jax.ShapeDtypeStruct((total, d), F32),
            jax.ShapeDtypeStruct((1, rows), I32),
        ],
        in_specs=[scalar] + [away] * 5,
        out_specs=[away] * 3,
        scratch_shapes=[
            pltpu.SMEM((1, seqs * LANES), I32),
            pltpu.SMEM((1, rows), I32),
            vm((1, rows), I32),
            vm((1, rows), I32),
            vm((1, seqs * LANES), I32),
            vm((1, rows), I32),
            vm((2, seqs, LANES), F32),
            vm((total, LANES), F32),
            vm((total, LANES), F32),
            vm((total, LANES), F32),
            vm((total, d), F32),
            dma((5,)),
            vm((seqs, heads, d, d), BF16),
            vm((seqs, heads, d, d), BF16),
            vm((3, total, heads * d), BF16),
            vm((total * HG, d), F32),
            vm((total * HG, d), F32),
            vm((total * HG, d), F32),
            vm((rows, HI, d), BF16),
            vm((rows, HI, d), BF16),
            vm((rows, HI, d), BF16),
            dma((3,)),
            dma((1,)),
            vm((seqs, 2, seqs, LANES), F32),
            vm(((2 * levels + 1) * seqs, d), F32),
            vm((heads, (2 * levels + 1) * seqs, d), F32),
            dma((seqs - 1,)),
            dma((seqs - 1,)),
            vm((heads, d, d), F32),
            vm((heads, d, d), F32),
            dma((seqs - 1, chunks)),
            dma((seqs - 1, chunks)),
            dma((seqs - 1, chunks)),
            dma((seqs - 1, chunks)),
            dma((chunks,)),
            dma((chunks,)),
        ]
        + [vm((share[k], heads, d, d), BF16) for k in range(levels)],
        compiler_params=pltpu.CompilerParams(
            collective_id=call, has_side_effects=True, vmem_limit_bytes=67043328
        ),
    )(rate, destination, doc_starts, key, value, query)


def finish_kernel(width, flat_ref, square_ref, gain_ref, mixed_ref, o_ref, scale):
    block = pl.program_id(0)

    @pl.when(block == 0)
    def _():
        mean = jnp.sum(square_ref[...], axis=1, keepdims=True) * (1.0 / width)
        scale[...] = jnp.broadcast_to(lax.rsqrt(mean + eps_norm), scale.shape)

    groups = mixed_ref.shape[0]
    gains = [gain_ref[b * HG : (b + 1) * HG, :] for b in range(groups)]

    def body(it, _):
        for e in range(16):
            r = it * 16 + e
            factor = scale[pl.ds(flat_ref[0, block * RB + r], 1), :]
            here = pl.ds(pl.multiple_of(r * HG, HG), HG)
            parts = [mixed_ref[b, here, :] * factor * gains[b] for b in range(groups)]
            o_ref[r] = jnp.concatenate(parts, axis=0).astype(BF16)
        return 0

    lax.fori_loop(0, RB // 16, body, 0)


def finish(flat, squares, gain, mixed):
    rows = flat.shape[1]
    heads, d = gain.shape
    total = squares.shape[0]
    return pl.pallas_call(
        functools.partial(finish_kernel, heads * d),
        grid=(rows // RB,),
        out_shape=jax.ShapeDtypeStruct((rows, heads, d), BF16),
        in_specs=[
            pl.BlockSpec(memory_space=pltpu.SMEM),
            pl.BlockSpec((total, d), lambda i: (0, 0)),
            pl.BlockSpec((heads, d), lambda i: (0, 0)),
            pl.BlockSpec((heads // HG, RB * HG, d), lambda i: (0, i, 0)),
        ],
        out_specs=pl.BlockSpec((RB, heads, d), lambda i: (i, 0, 0)),
        scratch_shapes=[pltpu.VMEM((total, d), F32)],
        compiler_params=pltpu.CompilerParams(vmem_limit_bytes=67043328),
    )(flat, squares, gain, mixed)


def per_device(queries, key_rows, value_rows, destination, doc_starts, decay_rate, norm_gain):
    loaders = lax.axis_size("dp")
    shards = lax.axis_size("seq")
    rows, heads, d = queries.shape[2:]
    cap = 3 * rows // (2 * loaders)
    levels = loaders.bit_length() - 1
    passes = max(1, loaders // 8)
    width = heads // passes
    results = []
    for i in range(passes):
        results.append(
            scan_states(
                decay_rate,
                destination,
                doc_starts,
                key_rows,
                value_rows,
                queries,
                width,
                i * width,
                levels,
                loaders,
                shards,
                cap,
                i,
            )
        )
    mixed = results[0][0] if passes == 1 else jnp.concatenate([x[0] for x in results], axis=0)
    squares = sum(x[1] for x in results[1:]) + results[0][1] if passes > 1 else results[0][1]
    return finish(results[0][2], squares, norm_gain, mixed)[None, None]


def solution(mesh):
    placed = (
        P("dp", "seq", None, None, None),
        P("dp", "seq", None, None, None),
        P("dp", "seq", None, None, None),
        P("dp", "seq", None),
        P("dp", "seq", None),
        P(),
        P(),
    )
    return jax.shard_map(
        per_device,
        mesh=mesh,
        in_specs=placed,
        out_specs=P("dp", "seq", None, None, None),
        check_vma=False,
    )
```

```python
import functools
import jax
import jax.numpy as jnp
from jax import lax
from jax.experimental import pallas as pl
from jax.experimental.pallas import tpu as pltpu
from jax.sharding import PartitionSpec as P

MESH = pl.DeviceIdType.MESH
F32 = jnp.float32
BF16 = jnp.bfloat16
I32 = jnp.int32
eps_norm = 1e-06
LANES = 128
HG = 8
HI = 16
HC = 2
RB = 256
NEVER = 1e30
UP_LAG = 2
Z_LAG = 2


def prepare(seqs, cap, dest_ref, start_ref, src_ref, flat_ref, fact_ref, until_ref, since_ref, gap_ref):
    rows = dest_ref.shape[-1]
    drow = dest_ref[...]
    srow = start_ref[...]
    ci = lax.broadcasted_iota(I32, (LANES, rows), 1)
    ri = lax.broadcasted_iota(I32, (LANES, rows), 0)
    place = lax.broadcasted_iota(I32, (LANES, LANES), 1)
    rlocal = lax.broadcasted_iota(I32, (LANES, 1), 0)
    slot_row = jnp.zeros((1, rows), I32)
    source = [jnp.zeros((1, LANES), I32) for _ in range(seqs)]
    begins = [jnp.zeros((1, LANES), I32) for _ in range(seqs)]
    for b in range(rows // LANES):
        rb = ri + b * LANES
        dcol = jnp.sum(jnp.where(rb == ci, drow, 0), axis=1, keepdims=True)
        scol = jnp.sum(jnp.where(rb == ci, srow, 0), axis=1, keepdims=True)
        same = jnp.where(dcol == drow, 1, 0)
        slot_col = jnp.sum(jnp.where(ci < rb, same, 0), axis=1, keepdims=True)
        slot_row = slot_row + jnp.sum(jnp.where(rb < ci, same, 0), axis=0, keepdims=True)
        slot_wide = dcol * LANES + slot_col
        rcol = rlocal + b * LANES
        for g in range(seqs):
            hit = slot_wide == place + g * LANES
            source[g] = source[g] + jnp.sum(jnp.where(hit, rcol, 0), axis=0, keepdims=True)
            begins[g] = begins[g] + jnp.sum(jnp.where(hit, scol, 0), axis=0, keepdims=True)
    flat_ref[...] = jnp.clip(drow * cap + slot_row, 0, seqs * cap - 1)
    pi = lax.broadcasted_iota(I32, (cap, LANES), 0)
    pj = lax.broadcasted_iota(I32, (cap, LANES), 1)
    position = pi.astype(F32)
    for g in range(seqs):
        src_ref[:, g * LANES : (g + 1) * LANES] = jnp.clip(source[g], 0, rows - 1)
        begin = begins[g].astype(F32)
        number = jnp.sum(jnp.where(drow == g, 1.0, 0.0), axis=1, keepdims=True)
        doc_end = jnp.sum(begin, axis=1, keepdims=True)
        doc_col = jnp.sum(jnp.where(pj <= pi, begin, 0.0), axis=1, keepdims=True)
        begin_col = jnp.sum(jnp.where(pj == pi, begin, 0.0), axis=1, keepdims=True)
        doc_row = jnp.sum(jnp.where(pi <= pj, begin_col, 0.0), axis=0, keepdims=True)
        here = slice(g * cap, (g + 1) * cap)
        fact_ref[0, g : g + 1, :] = jnp.broadcast_to(number, (1, LANES))
        fact_ref[1, g : g + 1, :] = jnp.broadcast_to(doc_end, (1, LANES))
        ends = (position < number) & (doc_col == doc_end)
        until_ref[here, :] = jnp.where(ends, number - 1.0 - position, NEVER)
        since_ref[here, :] = jnp.where(
            jnp.broadcast_to(doc_col, (cap, LANES)) == 0.0, position + 1.0, NEVER
        )
        keep = (pi >= pj) & (doc_col == doc_row)
        gap_ref[here, :] = jnp.where(keep, (pi - pj).astype(F32), NEVER)


def scan_kernel(levels, shards, seqs, heads, cap, base, *refs):
    rate_ref, dest_hbm, start_hbm = refs[:3]
    sources = refs[3:6]
    mixed_hbm, square_hbm, flat_hbm = refs[6:9]
    src_ref, flat_ref, dest_ref, start_ref, src_row, flat_row = refs[9:15]
    fact_ref, until_ref, since_ref, gap_ref, square_ref, small_sem = refs[15:21]
    refs = refs[21:]
    u_ref, out_ref, packed = refs[:3]
    tall = refs[3:6]
    inbuf = refs[6:9]
    in_sem, row_sem, facts, spans_ref, dec, f_s, f_r, total, zin = refs[9:18]
    up_s, up_r, dn_s, dn_r, z_s, z_r = refs[18:24]
    got = refs[24:]
    rows = flat_ref.shape[1]
    d = LANES
    me = lax.axis_index("dp")
    shard = lax.axis_index("seq")
    chunks = heads // HC
    per_group = HG // HC
    per_load = HI // HC
    tables = 2 * levels + 1
    share = [2 ** (levels - k - 1) for k in range(levels)]

    def bit(k):
        return lax.rem(lax.div(me, 2**k), 2)

    def partner(k):
        return me + 2**k - bit(k) * (2 ** (k + 1))

    def low(k):
        return lax.rem(me, 2**k)

    def decay(table, seq, head):
        return dec[head, pl.ds(table * seqs + seq, 1), :]

    def in_copy(n, b):
        return pltpu.make_async_copy(
            sources[n].at[0, 0, :, pl.ds(pl.multiple_of(base + b * HI, HI), HI), :],
            inbuf[n],
            in_sem.at[n],
        )

    loads = [
        pltpu.make_async_copy(dest_hbm.at[0], dest_ref, small_sem.at[0]),
        pltpu.make_async_copy(start_hbm.at[0], start_ref, small_sem.at[1]),
    ]
    moves = [
        pltpu.make_async_copy(src_row, src_ref, small_sem.at[2]),
        pltpu.make_async_copy(flat_row, flat_ref, small_sem.at[3]),
        pltpu.make_async_copy(flat_row, flat_hbm, small_sem.at[4]),
    ]
    for copy in loads:
        copy.start()
    for n in range(3):
        in_copy(n, 0).start()
    barrier = pltpu.get_barrier_semaphore()
    for i in range(1, seqs):
        peer = lax.rem(me + i, seqs)
        pl.semaphore_signal(barrier, inc=1, device_id=(peer, shard), device_id_type=MESH)

    @pl.when(shard > 0)
    def _():
        pl.semaphore_signal(barrier, inc=1, device_id=(me, shard - 1), device_id_type=MESH)

    @pl.when(shard < shards - 1)
    def _():
        pl.semaphore_signal(barrier, inc=1, device_id=(me, shard + 1), device_id_type=MESH)

    @pl.when(shard == 0)
    def _():
        def clear(i, _):
            zin[pl.ds(i, 1)] = jnp.zeros((1,) + zin.shape[1:], zin.dtype)
            return 0

        lax.fori_loop(0, heads, clear, 0)

    square_ref[...] = jnp.zeros(square_ref.shape, F32)
    for copy in loads:
        copy.wait()
    prepare(
        seqs, cap, dest_ref, start_ref, src_row, flat_row, fact_ref, until_ref, since_ref, gap_ref
    )
    for copy in moves:
        copy.start()

    def part(c):
        return pl.ds(c * HC, HC)

    def slot(k, j):
        return share[k] - 1 + j

    def up_copy(k, c, j):
        seq = j * 2 ** (k + 1) + (1 - bit(k)) * 2**k + low(k)
        return pltpu.make_async_remote_copy(
            src_ref=u_ref.at[seq, part(c)],
            dst_ref=got[k].at[j, part(c)],
            send_sem=up_s.at[slot(k, j), c],
            recv_sem=up_r.at[slot(k, j), c],
            device_id=(partner(k), shard),
            device_id_type=MESH,
        )

    def down_copy(k, c, j, receive):
        owner = partner(k) if receive else me
        seq = j * 2 ** (k + 1) + lax.rem(owner, 2 ** (k + 1))
        return pltpu.make_async_remote_copy(
            src_ref=got[k].at[j, part(c)],
            dst_ref=out_ref.at[seq, part(c)],
            send_sem=dn_s.at[slot(k, j), c],
            recv_sem=dn_r.at[slot(k, j), c],
            device_id=(partner(k), shard),
            device_id_type=MESH,
        )

    def z_copy(c, target):
        return pltpu.make_async_remote_copy(
            src_ref=total.at[part(c)],
            dst_ref=zin.at[part(c)],
            send_sem=z_s.at[c],
            recv_sem=z_r.at[c],
            device_id=(me, target),
            device_id_type=MESH,
        )

    def row_copy(i):
        return pltpu.make_async_copy(
            tall[2].at[pl.ds(0, rows * HG)], mixed_hbm.at[i], row_sem.at[0]
        )

    def rows_back():
        slots = tall[0].reshape(seqs * cap, HG, d)

        def body(it, _):
            for e in range(16):
                place = flat_ref[0, it * 16 + e]
                target = pl.multiple_of((it * 16 + e) * HG, HG)
                tall[2][pl.ds(target, HG), :] = slots[place]
            return 0

        lax.fori_loop(0, rows // 16, body, 0)

    def gather_side(side):
        steps = cap // 16
        part_heads = slice(side * HG, (side + 1) * HG)

        def body(it, _):
            first = lax.div(it, steps) * LANES + lax.rem(it, steps) * 16
            for e in range(16):
                row = src_ref[0, first + e]
                place = pl.multiple_of((it * 16 + e) * HG, HG)
                for n in range(3):
                    tall[n][pl.ds(place, HG), :] = inbuf[n][row, part_heads, :].astype(F32)
            return 0

        lax.fori_loop(0, seqs * steps, body, 0)

    def gather(i):
        for side in range(HI // HG):

            @pl.when(lax.rem(i, HI // HG) == side)
            def _():
                gather_side(side)

    def update(c):
        def body(g, _):
            here = pl.ds(pl.multiple_of(g * cap, 16), cap)
            until = until_ref[here, :]
            for e in range(HC):
                head = c * HC + e
                j = lax.rem(head, HG)
                cols = pl.ds(pl.multiple_of(head * d, d), d)
                strided = pl.ds(g * cap * HG + j, cap, stride=HG)
                key = tall[0][strided, :]
                value = tall[1][strided, :].astype(BF16)
                weight = jnp.exp(-rate_ref[base + head] * until)
                scaled = (key * weight).astype(BF16)
                packed[0, here, cols] = key.astype(BF16)
                packed[1, here, cols] = value
                packed[2, here, cols] = tall[2][strided, :].astype(BF16)
                change = lax.dot_general(
                    scaled, value, (((0,), (0,)), ((), ())), preferred_element_type=F32
                )
                u_ref[g, head] = change.astype(BF16)
            return 0

        lax.fori_loop(0, seqs, body, 0, unroll=4)
        for j in range(share[0]):
            up_copy(0, c, j).start()

    def up(k, c):
        for j in range(share[k]):
            up_copy(k, c, j).wait_recv()
        first = (bit(k) == 0).astype(F32)

        def body(i, _):
            j, head = lax.div(i, HC), c * HC + lax.rem(i, HC)
            seq = j * 2 ** (k + 1) + low(k + 1)
            own = u_ref[seq, head].astype(F32)
            other = got[k][j, head].astype(F32)
            hi = decay(k, seq, head)
            own_w = first * hi + (1.0 - first)
            other_w = first + (1.0 - first) * hi
            both = own * own_w + other * other_w
            got[k][j, head] = (first * own + (1.0 - first) * other).astype(BF16)
            if k + 1 < levels:
                u_ref[seq, head] = both.astype(BF16)
            else:
                total[head] = both
            return 0

        lax.fori_loop(0, share[k] * HC, body, 0, unroll=2)
        if k + 1 < levels:
            for j in range(share[k + 1]):
                up_copy(k + 1, c, j).start()

    def across(c):
        @pl.when(shard > 0)
        def _():
            z_copy(c, shard).wait_recv()

        def body(i, _):
            head = c * HC + i
            state = zin[head]
            out_ref[me, head] = state.astype(BF16)
            total[head] = state * decay(2 * levels, me, head) + total[head]
            return 0

        lax.fori_loop(0, HC, body, 0)

        @pl.when(shard < shards - 1)
        def _():
            z_copy(c, shard + 1).start()

    def down(k, c):
        if k + 1 < levels:
            for j in range(share[k + 1]):
                down_copy(k + 1, c, j, True).wait_recv()
        first = (bit(k) == 0).astype(F32)

        def body(i, _):
            j, head = lax.div(i, HC), c * HC + lax.rem(i, HC)
            seq = j * 2 ** (k + 1) + low(k + 1)
            start = out_ref[seq, head].astype(F32)
            later = start * decay(levels + k, seq, head) + got[k][j, head].astype(F32)
            out_ref[seq, head] = (first * start + (1.0 - first) * later).astype(BF16)
            got[k][j, head] = (first * later + (1.0 - first) * start).astype(BF16)
            return 0

        lax.fori_loop(0, share[k] * HC, body, 0, unroll=2)
        for j in range(share[k]):
            down_copy(k, c, j, False).start()

    def attend(c):
        i = lax.div(c, per_group)
        for j in range(share[0]):
            down_copy(0, c, j, True).wait_recv()

        def body(g, _):
            here = pl.ds(pl.multiple_of(g * cap, 16), cap)
            gap = gap_ref[here, :cap]
            since = since_ref[here, :]
            squares = square_ref[here, :]
            for e in range(HC):
                head = c * HC + e
                j = lax.rem(head, HG)
                cols = pl.ds(pl.multiple_of(head * d, d), d)
                rate = rate_ref[base + head]
                query = packed[2, here, cols]
                scores = lax.dot_general(
                    query,
                    packed[0, here, cols],
                    (((1,), (1,)), ((), ())),
                    preferred_element_type=F32,
                )
                half = (scores * jnp.exp(-rate * gap)).astype(BF16)
                intra = jnp.dot(half, packed[1, here, cols], preferred_element_type=F32)
                inter = jnp.dot(query, out_ref[g, head], preferred_element_type=F32)
                mixed = intra + inter * jnp.exp(-rate * since)
                tall[0][pl.ds(g * cap * HG + j, cap, stride=HG), :] = mixed
                squares = squares + mixed * mixed
            square_ref[here, :] = squares
            return 0

        lax.fori_loop(0, seqs, body, 0, unroll=4)

        @pl.when(lax.rem(c, per_group) == per_group - 1)
        def _():
            @pl.when(i > 0)
            def _():
                row_copy(i - 1).wait()

            rows_back()
            row_copy(i).start()

    def fact_copy(i, receive):
        owner = lax.rem(me + seqs - i, seqs) if receive else me
        return pltpu.make_async_remote_copy(
            src_ref=fact_ref,
            dst_ref=facts.at[owner],
            send_sem=f_s.at[i - 1],
            recv_sem=f_r.at[i - 1],
            device_id=(lax.rem(me + i, seqs), shard),
            device_id_type=MESH,
        )

    ends = (shard > 0).astype(I32) + (shard < shards - 1).astype(I32)
    pl.semaphore_wait(barrier, seqs - 1 + ends)
    for i in range(1, seqs):
        fact_copy(i, False).start()
    for copy in moves:
        copy.wait()
    for n in range(3):
        in_copy(n, 0).wait()
    gather_side(0)
    update(0)
    facts[pl.ds(me, 1)] = fact_ref[...][None]
    for i in range(1, seqs):
        fact_copy(i, True).wait_recv()
    spans = [((me // 2 ** (k + 1) * 2 + 1) * 2**k, 2**k) for k in range(levels)]
    spans += [((me // 2 ** (k + 1) * 2) * 2**k, 2**k) for k in range(levels)]
    spans += [(me * 0, seqs)]
    for table, (begin, size) in enumerate(spans):
        count = jnp.zeros(fact_ref.shape[1:], F32)
        docs = jnp.zeros(fact_ref.shape[1:], F32)
        for loader in range(seqs):
            inside = ((loader >= begin) & (loader < begin + size)).astype(F32)
            count = count + facts[loader, 0] * inside
            docs = docs + facts[loader, 1] * inside
        spans_ref[table * seqs : (table + 1) * seqs, :] = jnp.where(docs == 0.0, count, NEVER)

    def fill(head, _):
        dec[head] = jnp.exp(-rate_ref[base + head] * spans_ref[...])
        return 0

    lax.fori_loop(0, heads, fill, 0)

    ups = [1 + UP_LAG * k for k in range(levels)]
    z_first = ups[-1] + 1
    d_first = max(z_first + Z_LAG * (shards - 1) + 1, chunks - levels - 2)
    downs = [d_first + 2 * (levels - 1 - k) + (1 if k == 0 else 0) for k in range(levels)]
    a_first = downs[0] + 1

    def during(c):
        return (c >= 0) & (c < chunks)

    def step(t, _):
        fresh = t < chunks

        @pl.when(fresh & (lax.rem(t, per_group) == 0))
        def _():
            i = lax.div(t, per_group)

            @pl.when(lax.rem(t, per_load) == 0)
            def _():
                for n in range(3):
                    in_copy(n, lax.div(t, per_load)).wait()

            gather(i)

            @pl.when((t < chunks - per_load) & (lax.rem(t, per_load) == per_load - per_group))
            def _():
                for n in range(3):
                    in_copy(n, lax.div(t, per_load) + 1).start()

        @pl.when(fresh)
        def _():
            update(t)

        for k in range(levels):

            @pl.when(during(t - ups[k]))
            def _():
                up(k, t - ups[k])

        cz = t - z_first - Z_LAG * shard

        @pl.when(during(cz))
        def _():
            across(cz)

        for k in range(levels - 1, -1, -1):

            @pl.when(during(t - downs[k]))
            def _():
                down(k, t - downs[k])

        @pl.when(during(t - a_first))
        def _():
            attend(t - a_first)
            settle(t - a_first)

        return 0

    def settle(c):
        for k in range(levels):
            for j in range(share[k]):
                up_copy(k, c, j).wait_send()
                down_copy(k, c, j, False).wait_send()

        @pl.when(shard < shards - 1)
        def _():
            z_copy(c, shard + 1).wait_send()

    lax.fori_loop(1, chunks + a_first, step, 0)
    square_copy = pltpu.make_async_copy(square_ref, square_hbm, small_sem.at[0])
    square_copy.start()
    square_copy.wait()
    row_copy(heads // HG - 1).wait()
    for i in range(1, seqs):
        fact_copy(i, False).wait_send()


def scan_states(rate, destination, doc_starts, key, value, query, heads, base, levels, seqs, shards, cap, call):
    d = key.shape[-1]
    rows = key.shape[2]
    total = seqs * cap
    chunks = heads // HC
    vm = pltpu.VMEM
    share = [2 ** (levels - k - 1) for k in range(levels)]
    dma = pltpu.SemaphoreType.DMA
    away = pl.BlockSpec(memory_space=pl.ANY)
    scalar = pl.BlockSpec(memory_space=pltpu.SMEM)
    return pl.pallas_call(
        functools.partial(scan_kernel, levels, shards, seqs, heads, cap, base),
        out_shape=[
            jax.ShapeDtypeStruct((heads // HG, rows * HG, d), F32),
            jax.ShapeDtypeStruct((total, d), F32),
            jax.ShapeDtypeStruct((1, rows), I32),
        ],
        in_specs=[scalar] + [away] * 5,
        out_specs=[away] * 3,
        scratch_shapes=[
            pltpu.SMEM((1, seqs * LANES), I32),
            pltpu.SMEM((1, rows), I32),
            vm((1, rows), I32),
            vm((1, rows), I32),
            vm((1, seqs * LANES), I32),
            vm((1, rows), I32),
            vm((2, seqs, LANES), F32),
            vm((total, LANES), F32),
            vm((total, LANES), F32),
            vm((total, LANES), F32),
            vm((total, d), F32),
            dma((5,)),
            vm((seqs, heads, d, d), BF16),
            vm((seqs, heads, d, d), BF16),
            vm((3, total, heads * d), BF16),
            vm((total * HG, d), F32),
            vm((total * HG, d), F32),
            vm((total * HG, d), F32),
            vm((rows, HI, d), BF16),
            vm((rows, HI, d), BF16),
            vm((rows, HI, d), BF16),
            dma((3,)),
            dma((1,)),
            vm((seqs, 2, seqs, LANES), F32),
            vm(((2 * levels + 1) * seqs, d), F32),
            vm((heads, (2 * levels + 1) * seqs, d), F32),
            dma((seqs - 1,)),
            dma((seqs - 1,)),
            vm((heads, d, d), F32),
            vm((heads, d, d), F32),
            dma((seqs - 1, chunks)),
            dma((seqs - 1, chunks)),
            dma((seqs - 1, chunks)),
            dma((seqs - 1, chunks)),
            dma((chunks,)),
            dma((chunks,)),
        ]
        + [vm((share[k], heads, d, d), BF16) for k in range(levels)],
        compiler_params=pltpu.CompilerParams(
            collective_id=call, has_side_effects=True, vmem_limit_bytes=67043328
        ),
    )(rate, destination, doc_starts, key, value, query)


def finish_kernel(width, flat_ref, square_ref, gain_ref, mixed_ref, o_ref, scale):
    block = pl.program_id(0)

    @pl.when(block == 0)
    def _():
        mean = jnp.sum(square_ref[...], axis=1, keepdims=True) * (1.0 / width)
        scale[...] = jnp.broadcast_to(lax.rsqrt(mean + eps_norm), scale.shape)

    groups = mixed_ref.shape[0]
    gains = [gain_ref[b * HG : (b + 1) * HG, :] for b in range(groups)]

    def body(it, _):
        for e in range(16):
            r = it * 16 + e
            factor = scale[pl.ds(flat_ref[0, block * RB + r], 1), :]
            here = pl.ds(pl.multiple_of(r * HG, HG), HG)
            parts = [mixed_ref[b, here, :] * factor * gains[b] for b in range(groups)]
            o_ref[r] = jnp.concatenate(parts, axis=0).astype(BF16)
        return 0

    lax.fori_loop(0, RB // 16, body, 0)


def finish(flat, squares, gain, mixed):
    rows = flat.shape[1]
    heads, d = gain.shape
    total = squares.shape[0]
    return pl.pallas_call(
        functools.partial(finish_kernel, heads * d),
        grid=(rows // RB,),
        out_shape=jax.ShapeDtypeStruct((rows, heads, d), BF16),
        in_specs=[
            pl.BlockSpec(memory_space=pltpu.SMEM),
            pl.BlockSpec((total, d), lambda i: (0, 0)),
            pl.BlockSpec((heads, d), lambda i: (0, 0)),
            pl.BlockSpec((heads // HG, RB * HG, d), lambda i: (0, i, 0)),
        ],
        out_specs=pl.BlockSpec((RB, heads, d), lambda i: (i, 0, 0)),
        scratch_shapes=[pltpu.VMEM((total, d), F32)],
        compiler_params=pltpu.CompilerParams(vmem_limit_bytes=67043328),
    )(flat, squares, gain, mixed)


def per_device(queries, key_rows, value_rows, destination, doc_starts, decay_rate, norm_gain):
    loaders = lax.axis_size("dp")
    shards = lax.axis_size("seq")
    rows, heads, d = queries.shape[2:]
    cap = 3 * rows // (2 * loaders)
    levels = loaders.bit_length() - 1
    passes = max(1, loaders // 8)
    width = heads // passes
    results = []
    for i in range(passes):
        results.append(
            scan_states(
                decay_rate,
                destination,
                doc_starts,
                key_rows,
                value_rows,
                queries,
                width,
                i * width,
                levels,
                loaders,
                shards,
                cap,
                i,
            )
        )
    mixed = results[0][0] if passes == 1 else jnp.concatenate([x[0] for x in results], axis=0)
    squares = sum(x[1] for x in results[1:]) + results[0][1] if passes > 1 else results[0][1]
    return finish(results[0][2], squares, norm_gain, mixed)[None, None]


def solution(mesh):
    placed = (
        P("dp", "seq", None, None, None),
        P("dp", "seq", None, None, None),
        P("dp", "seq", None, None, None),
        P("dp", "seq", None),
        P("dp", "seq", None),
        P(),
        P(),
    )
    return jax.shard_map(
        per_device,
        mesh=mesh,
        in_specs=placed,
        out_specs=P("dp", "seq", None, None, None),
        check_vma=False,
    )
```

```python
import functools
import jax
import jax.numpy as jnp
from jax import lax
from jax.experimental import pallas as pl
from jax.experimental.pallas import tpu as pltpu
from jax.sharding import PartitionSpec as P

MESH = pl.DeviceIdType.MESH
F32 = jnp.float32
BF16 = jnp.bfloat16
I32 = jnp.int32
eps_norm = 1e-06
LANES = 128
HG = 8
HI = 16
HC = 2
PARTS = 4
PIECES = 4
NEVER = 1e30
UP_LAG = 2
Z_LAG = 2


def prepare(seqs, cap, dest_ref, start_ref, src_ref, flat_ref, fact_ref, until_ref, since_ref, gap_ref):
    rows = dest_ref.shape[-1]
    drow = dest_ref[...]
    srow = start_ref[...]
    ci = lax.broadcasted_iota(I32, (LANES, rows), 1)
    ri = lax.broadcasted_iota(I32, (LANES, rows), 0)
    place = lax.broadcasted_iota(I32, (LANES, LANES), 1)
    rlocal = lax.broadcasted_iota(I32, (LANES, 1), 0)
    slot_row = jnp.zeros((1, rows), I32)
    source = [jnp.zeros((1, LANES), I32) for _ in range(seqs)]
    begins = [jnp.zeros((1, LANES), I32) for _ in range(seqs)]
    for b in range(rows // LANES):
        rb = ri + b * LANES
        dcol = jnp.sum(jnp.where(rb == ci, drow, 0), axis=1, keepdims=True)
        scol = jnp.sum(jnp.where(rb == ci, srow, 0), axis=1, keepdims=True)
        same = jnp.where(dcol == drow, 1, 0)
        slot_col = jnp.sum(jnp.where(ci < rb, same, 0), axis=1, keepdims=True)
        slot_row = slot_row + jnp.sum(jnp.where(rb < ci, same, 0), axis=0, keepdims=True)
        slot_wide = dcol * LANES + slot_col
        rcol = rlocal + b * LANES
        for g in range(seqs):
            hit = slot_wide == place + g * LANES
            source[g] = source[g] + jnp.sum(jnp.where(hit, rcol, 0), axis=0, keepdims=True)
            begins[g] = begins[g] + jnp.sum(jnp.where(hit, scol, 0), axis=0, keepdims=True)
    flat_ref[...] = jnp.clip(drow * cap + slot_row, 0, seqs * cap - 1)
    pi = lax.broadcasted_iota(I32, (cap, LANES), 0)
    pj = lax.broadcasted_iota(I32, (cap, LANES), 1)
    position = pi.astype(F32)
    for g in range(seqs):
        src_ref[:, g * LANES : (g + 1) * LANES] = jnp.clip(source[g], 0, rows - 1)
        begin = begins[g].astype(F32)
        number = jnp.sum(jnp.where(drow == g, 1.0, 0.0), axis=1, keepdims=True)
        doc_end = jnp.sum(begin, axis=1, keepdims=True)
        doc_col = jnp.sum(jnp.where(pj <= pi, begin, 0.0), axis=1, keepdims=True)
        begin_col = jnp.sum(jnp.where(pj == pi, begin, 0.0), axis=1, keepdims=True)
        doc_row = jnp.sum(jnp.where(pi <= pj, begin_col, 0.0), axis=0, keepdims=True)
        here = slice(g * cap, (g + 1) * cap)
        fact_ref[0, g : g + 1, :] = jnp.broadcast_to(number, (1, LANES))
        fact_ref[1, g : g + 1, :] = jnp.broadcast_to(doc_end, (1, LANES))
        ends = (position < number) & (doc_col == doc_end)
        until_ref[here, :] = jnp.where(ends, number - 1.0 - position, NEVER)
        since_ref[here, :] = jnp.where(
            jnp.broadcast_to(doc_col, (cap, LANES)) == 0.0, position + 1.0, NEVER
        )
        keep = (pi >= pj) & (doc_col == doc_row)
        gap_ref[here, :] = jnp.where(keep, (pi - pj).astype(F32), NEVER)


def scan_kernel(levels, shards, seqs, heads, cap, base, *refs):
    rate_hbm, dest_hbm, start_hbm = refs[:3]
    sources = refs[3:6]
    mixed_hbm, square_hbm, flat_hbm = refs[6:9]
    rate_ref, src_ref, flat_ref, dest_ref, start_ref, src_row, flat_row = refs[9:16]
    fact_ref, until_ref, since_ref, gap_ref, square_ref, small_sem = refs[16:22]
    refs = refs[22:]
    u_ref, out_ref, packed = refs[:3]
    tall = refs[3:6]
    inbuf = refs[6:9]
    in_sem, row_sem, facts, spans_ref, dec, f_s, f_r, total, zin = refs[9:18]
    up_s, up_r, dn_s, dn_r, z_s, z_r = refs[18:24]
    got = refs[24:]
    rows = flat_ref.shape[1]
    d = LANES
    me = lax.axis_index("dp")
    shard = lax.axis_index("seq")
    chunks = heads // HC
    per_group = HG // HC
    per_load = HI // HC
    tables = 2 * levels + 1
    share = [2 ** (levels - k - 1) for k in range(levels)]

    def bit(k):
        return lax.rem(lax.div(me, 2**k), 2)

    def partner(k):
        return me + 2**k - bit(k) * (2 ** (k + 1))

    def low(k):
        return lax.rem(me, 2**k)

    def decay(table, seq, head):
        return dec[head, pl.ds(table * seqs + seq, 1), :]

    def in_copy(n, b):
        return pltpu.make_async_copy(
            sources[n].at[0, 0, :, pl.ds(pl.multiple_of(base + b * HI, HI), HI), :],
            inbuf[n],
            in_sem.at[n],
        )

    loads = [
        pltpu.make_async_copy(dest_hbm.at[0], dest_ref, small_sem.at[0]),
        pltpu.make_async_copy(start_hbm.at[0], start_ref, small_sem.at[1]),
        pltpu.make_async_copy(rate_hbm, rate_ref, small_sem.at[5]),
    ]
    moves = [
        pltpu.make_async_copy(src_row, src_ref, small_sem.at[2]),
        pltpu.make_async_copy(flat_row, flat_ref, small_sem.at[3]),
        pltpu.make_async_copy(flat_row, flat_hbm, small_sem.at[4]),
    ]
    barrier = pltpu.get_barrier_semaphore()
    for i in range(1, seqs):
        peer = lax.rem(me + i, seqs)
        pl.semaphore_signal(barrier, inc=1, device_id=(peer, shard), device_id_type=MESH)

    @pl.when(shard > 0)
    def _():
        pl.semaphore_signal(barrier, inc=1, device_id=(me, shard - 1), device_id_type=MESH)

    @pl.when(shard < shards - 1)
    def _():
        pl.semaphore_signal(barrier, inc=1, device_id=(me, shard + 1), device_id_type=MESH)

    for copy in loads:
        copy.start()
    for n in range(3):
        in_copy(n, 0).start()
    @pl.when(shard == 0)
    def _():
        def clear(i, _):
            zin[pl.ds(i, 1)] = jnp.zeros((1,) + zin.shape[1:], zin.dtype)
            return 0

        lax.fori_loop(0, heads, clear, 0)

    square_ref[...] = jnp.zeros(square_ref.shape, F32)
    for copy in loads:
        copy.wait()
    prepare(
        seqs, cap, dest_ref, start_ref, src_row, flat_row, fact_ref, until_ref, since_ref, gap_ref
    )
    for copy in moves:
        copy.start()

    def part(c):
        return pl.ds(c * HC, HC)

    def slot(k, j):
        return share[k] - 1 + j

    def up_copy(k, c, j):
        seq = j * 2 ** (k + 1) + (1 - bit(k)) * 2**k + low(k)
        return pltpu.make_async_remote_copy(
            src_ref=u_ref.at[seq, part(c)],
            dst_ref=got[k].at[j, part(c)],
            send_sem=up_s.at[slot(k, j), c],
            recv_sem=up_r.at[slot(k, j), c],
            device_id=(partner(k), shard),
            device_id_type=MESH,
        )

    def down_copy(k, c, j, receive):
        owner = partner(k) if receive else me
        seq = j * 2 ** (k + 1) + lax.rem(owner, 2 ** (k + 1))
        return pltpu.make_async_remote_copy(
            src_ref=got[k].at[j, part(c)],
            dst_ref=out_ref.at[seq, part(c)],
            send_sem=dn_s.at[slot(k, j), c],
            recv_sem=dn_r.at[slot(k, j), c],
            device_id=(partner(k), shard),
            device_id_type=MESH,
        )

    def z_copy(c, target):
        return pltpu.make_async_remote_copy(
            src_ref=total.at[part(c)],
            dst_ref=zin.at[part(c)],
            send_sem=z_s.at[c],
            recv_sem=z_r.at[c],
            device_id=(me, target),
            device_id_type=MESH,
        )

    def row_copy(i, p):
        here = pl.ds(p * (rows * HG // PIECES), rows * HG // PIECES)
        return pltpu.make_async_copy(
            tall[2].at[here], mixed_hbm.at[i, here], row_sem.at[p]
        )

    def rows_back(p):
        slots = tall[0].reshape(seqs * cap, HG, d)
        steps = rows // PIECES // 16

        def body(it, _):
            first = (p * steps + it) * 16
            found = [slots[flat_ref[0, first + e]] for e in range(16)]
            for e in range(16):
                target = pl.multiple_of((first + e) * HG, HG)
                tall[2][pl.ds(target, HG), :] = found[e]
            return 0

        lax.fori_loop(0, steps, body, 0)

    def square_copy():
        return pltpu.make_async_copy(square_ref, square_hbm, small_sem.at[0])

    def gather_side(side):
        steps = cap // 16
        part_heads = slice(side * HG, (side + 1) * HG)

        def body(it, _):
            first = lax.div(it, steps) * LANES + lax.rem(it, steps) * 16
            for half in range(0, 16, 8):
                found = [
                    [inbuf[n][src_ref[0, first + half + e], part_heads, :].astype(F32) for n in range(3)]
                    for e in range(8)
                ]
                for e in range(8):
                    place = pl.multiple_of((it * 16 + half + e) * HG, HG)
                    for n in range(3):
                        tall[n][pl.ds(place, HG), :] = found[e][n]
            return 0

        lax.fori_loop(0, seqs * steps, body, 0)

    def gather(i):
        for side in range(HI // HG):

            @pl.when(lax.rem(i, HI // HG) == side)
            def _():
                gather_side(side)

    def update(c):
        def body(g, _):
            here = pl.ds(pl.multiple_of(g * cap, 16), cap)
            until = until_ref[here, :]
            for e in range(HC):
                head = c * HC + e
                j = lax.rem(head, HG)
                cols = pl.ds(pl.multiple_of(head * d, d), d)
                strided = pl.ds(g * cap * HG + j, cap, stride=HG)
                key = tall[0][strided, :]
                value = tall[1][strided, :].astype(BF16)
                weight = jnp.exp(-rate_ref[base + head] * until)
                scaled = (key * weight).astype(BF16)
                packed[0, here, cols] = key.astype(BF16)
                packed[1, here, cols] = value
                packed[2, here, cols] = tall[2][strided, :].astype(BF16)
                change = lax.dot_general(
                    scaled, value, (((0,), (0,)), ((), ())), preferred_element_type=F32
                )
                u_ref[g, head] = change.astype(BF16)
            return 0

        lax.fori_loop(0, seqs, body, 0, unroll=4)
        for j in range(share[0]):
            up_copy(0, c, j).start()

    def up(k, c):
        for j in range(share[k]):
            up_copy(k, c, j).wait_recv()
        first = (bit(k) == 0).astype(F32)

        def body(i, _):
            j, head = lax.div(i, HC), c * HC + lax.rem(i, HC)
            seq = j * 2 ** (k + 1) + low(k + 1)
            own = u_ref[seq, head].astype(F32)
            other = got[k][j, head].astype(F32)
            hi = decay(k, seq, head)
            own_w = first * hi + (1.0 - first)
            other_w = first + (1.0 - first) * hi
            both = own * own_w + other * other_w
            got[k][j, head] = (first * own + (1.0 - first) * other).astype(BF16)
            if k + 1 < levels:
                u_ref[seq, head] = both.astype(BF16)
            else:
                total[head] = both
            return 0

        lax.fori_loop(0, share[k] * HC, body, 0, unroll=2)
        if k + 1 < levels:
            for j in range(share[k + 1]):
                up_copy(k + 1, c, j).start()

    def across(c):
        @pl.when(shard > 0)
        def _():
            z_copy(c, shard).wait_recv()

        def body(i, _):
            head = c * HC + i
            state = zin[head]
            out_ref[me, head] = state.astype(BF16)
            total[head] = state * decay(2 * levels, me, head) + total[head]
            return 0

        lax.fori_loop(0, HC, body, 0)

        @pl.when(shard < shards - 1)
        def _():
            z_copy(c, shard + 1).start()

    def down(k, c):
        if k + 1 < levels:
            for j in range(share[k + 1]):
                down_copy(k + 1, c, j, True).wait_recv()
        first = (bit(k) == 0).astype(F32)

        def body(i, _):
            j, head = lax.div(i, HC), c * HC + lax.rem(i, HC)
            seq = j * 2 ** (k + 1) + low(k + 1)
            start = out_ref[seq, head].astype(F32)
            later = start * decay(levels + k, seq, head) + got[k][j, head].astype(F32)
            out_ref[seq, head] = (first * start + (1.0 - first) * later).astype(BF16)
            got[k][j, head] = (first * later + (1.0 - first) * start).astype(BF16)
            return 0

        lax.fori_loop(0, share[k] * HC, body, 0, unroll=2)
        for j in range(share[k]):
            down_copy(k, c, j, False).start()

    def attend(c):
        i = lax.div(c, per_group)
        for j in range(share[0]):
            down_copy(0, c, j, True).wait_recv()

        def body(g, _):
            here = pl.ds(pl.multiple_of(g * cap, 16), cap)
            gap = gap_ref[here, :cap]
            since = since_ref[here, :]
            squares = square_ref[here, :]
            for e in range(HC):
                head = c * HC + e
                j = lax.rem(head, HG)
                cols = pl.ds(pl.multiple_of(head * d, d), d)
                rate = rate_ref[base + head]
                query = packed[2, here, cols]
                scores = lax.dot_general(
                    query,
                    packed[0, here, cols],
                    (((1,), (1,)), ((), ())),
                    preferred_element_type=F32,
                )
                half = (scores * jnp.exp(-rate * gap)).astype(BF16)
                intra = jnp.dot(half, packed[1, here, cols], preferred_element_type=F32)
                inter = jnp.dot(query, out_ref[g, head], preferred_element_type=F32)
                mixed = intra + inter * jnp.exp(-rate * since)
                tall[0][pl.ds(g * cap * HG + j, cap, stride=HG), :] = mixed
                squares = squares + mixed * mixed
            square_ref[here, :] = squares
            return 0

        lax.fori_loop(0, seqs, body, 0, unroll=4)

        @pl.when(lax.rem(c, per_group) == per_group - 1)
        def _():
            @pl.when(c == chunks - 1)
            def _():
                square_copy().start()

            for p in range(PIECES):

                @pl.when(i > 0)
                def _():
                    row_copy(i - 1, p).wait()

                rows_back(p)
                row_copy(i, p).start()

    def fact_copy(i, receive):
        owner = lax.rem(me + seqs - i, seqs) if receive else me
        return pltpu.make_async_remote_copy(
            src_ref=fact_ref,
            dst_ref=facts.at[owner],
            send_sem=f_s.at[i - 1],
            recv_sem=f_r.at[i - 1],
            device_id=(lax.rem(me + i, seqs), shard),
            device_id_type=MESH,
        )

    ends = (shard > 0).astype(I32) + (shard < shards - 1).astype(I32)
    pl.semaphore_wait(barrier, seqs - 1 + ends)
    for i in range(1, seqs):
        fact_copy(i, False).start()
    for copy in moves:
        copy.wait()
    for n in range(3):
        in_copy(n, 0).wait()
    gather_side(0)
    update(0)
    facts[pl.ds(me, 1)] = fact_ref[...][None]
    for i in range(1, seqs):
        fact_copy(i, True).wait_recv()
    spans = [((me // 2 ** (k + 1) * 2 + 1) * 2**k, 2**k) for k in range(levels)]
    spans += [((me // 2 ** (k + 1) * 2) * 2**k, 2**k) for k in range(levels)]
    spans += [(me * 0, seqs)]
    for table, (begin, size) in enumerate(spans):
        count = jnp.zeros(fact_ref.shape[1:], F32)
        docs = jnp.zeros(fact_ref.shape[1:], F32)
        for loader in range(seqs):
            inside = ((loader >= begin) & (loader < begin + size)).astype(F32)
            count = count + facts[loader, 0] * inside
            docs = docs + facts[loader, 1] * inside
        spans_ref[table * seqs : (table + 1) * seqs, :] = jnp.where(docs == 0.0, count, NEVER)

    def fill(head, _):
        dec[head] = jnp.exp(-rate_ref[base + head] * spans_ref[...])
        return 0

    lax.fori_loop(0, heads, fill, 0)

    ups = [1 + UP_LAG * k for k in range(levels)]
    z_first = ups[-1] + 1
    d_first = max(z_first + Z_LAG * (shards - 1) + 1, chunks - levels - 2)
    downs = [d_first + 2 * (levels - 1 - k) + (1 if k == 0 else 0) for k in range(levels)]
    a_first = downs[0] + 1

    def during(c):
        return (c >= 0) & (c < chunks)

    def step(t, _):
        fresh = t < chunks

        @pl.when(fresh & (lax.rem(t, per_group) == 0))
        def _():
            i = lax.div(t, per_group)

            @pl.when(lax.rem(t, per_load) == 0)
            def _():
                for n in range(3):
                    in_copy(n, lax.div(t, per_load)).wait()

            gather(i)

            @pl.when((t < chunks - per_load) & (lax.rem(t, per_load) == per_load - per_group))
            def _():
                for n in range(3):
                    in_copy(n, lax.div(t, per_load) + 1).start()

        @pl.when(fresh)
        def _():
            update(t)

        for k in range(levels):

            @pl.when(during(t - ups[k]))
            def _():
                up(k, t - ups[k])

        cz = t - z_first - Z_LAG * shard

        @pl.when(during(cz))
        def _():
            across(cz)

        for k in range(levels - 1, -1, -1):

            @pl.when(during(t - downs[k]))
            def _():
                down(k, t - downs[k])

        @pl.when(during(t - a_first))
        def _():
            attend(t - a_first)
            settle(t - a_first)

        return 0

    def settle(c):
        for k in range(levels):
            for j in range(share[k]):
                up_copy(k, c, j).wait_send()
                down_copy(k, c, j, False).wait_send()

        @pl.when(shard < shards - 1)
        def _():
            z_copy(c, shard + 1).wait_send()

    lax.fori_loop(1, chunks + a_first, step, 0)
    square_copy().wait()
    for p in range(PIECES):
        row_copy(heads // HG - 1, p).wait()
    for i in range(1, seqs):
        fact_copy(i, False).wait_send()


def scan_states(rate, destination, doc_starts, key, value, query, heads, base, levels, seqs, shards, cap, call):
    d = key.shape[-1]
    rows = key.shape[2]
    total = seqs * cap
    chunks = heads // HC
    vm = pltpu.VMEM
    share = [2 ** (levels - k - 1) for k in range(levels)]
    dma = pltpu.SemaphoreType.DMA
    away = pl.BlockSpec(memory_space=pl.ANY)
    return pl.pallas_call(
        functools.partial(scan_kernel, levels, shards, seqs, heads, cap, base),
        out_shape=[
            jax.ShapeDtypeStruct((heads // HG, rows * HG, d), F32),
            jax.ShapeDtypeStruct((total, d), F32),
            jax.ShapeDtypeStruct((1, rows), I32),
        ],
        in_specs=[away] * 6,
        out_specs=[away] * 3,
        scratch_shapes=[
            pltpu.SMEM(rate.shape, F32),
            pltpu.SMEM((1, seqs * LANES), I32),
            pltpu.SMEM((1, rows), I32),
            vm((1, rows), I32),
            vm((1, rows), I32),
            vm((1, seqs * LANES), I32),
            vm((1, rows), I32),
            vm((2, seqs, LANES), F32),
            vm((total, LANES), F32),
            vm((total, LANES), F32),
            vm((total, LANES), F32),
            vm((total, d), F32),
            dma((6,)),
            vm((seqs, heads, d, d), BF16),
            vm((seqs, heads, d, d), BF16),
            vm((3, total, heads * d), BF16),
            vm((total * HG, d), F32),
            vm((total * HG, d), F32),
            vm((total * HG, d), F32),
            vm((rows, HI, d), BF16),
            vm((rows, HI, d), BF16),
            vm((rows, HI, d), BF16),
            dma((3,)),
            dma((PIECES,)),
            vm((seqs, 2, seqs, LANES), F32),
            vm(((2 * levels + 1) * seqs, d), F32),
            vm((heads, (2 * levels + 1) * seqs, d), F32),
            dma((seqs - 1,)),
            dma((seqs - 1,)),
            vm((heads, d, d), F32),
            vm((heads, d, d), F32),
            dma((seqs - 1, chunks)),
            dma((seqs - 1, chunks)),
            dma((seqs - 1, chunks)),
            dma((seqs - 1, chunks)),
            dma((chunks,)),
            dma((chunks,)),
        ]
        + [vm((share[k], heads, d, d), BF16) for k in range(levels)],
        compiler_params=pltpu.CompilerParams(
            collective_id=call, has_side_effects=True, vmem_limit_bytes=67043328
        ),
    )(rate, destination, doc_starts, key, value, query)


def finish_kernel(width, *refs):
    sources, o_hbm = refs[:4], refs[4]
    flat, square, gain, mixed, out, scale, small_sem, in_sem, out_sem = refs[5:]
    groups = mixed.shape[0]
    rows = out.shape[0]
    size = rows // PARTS
    small = [
        pltpu.make_async_copy(source, target, small_sem.at[n])
        for n, (source, target) in enumerate(zip(sources, (flat, square, gain)))
    ]

    def in_copy(p):
        here = pl.ds(p * size * HG, size * HG)
        return pltpu.make_async_copy(sources[3].at[:, here], mixed.at[:, here], in_sem.at[p])

    def out_copy(p):
        here = pl.ds(p * size, size)
        return pltpu.make_async_copy(out.at[here], o_hbm.at[here], out_sem.at[p])

    for copy in small:
        copy.start()
    for p in range(PARTS):
        in_copy(p).start()
    for copy in small:
        copy.wait()
    mean = jnp.sum(square[...], axis=1, keepdims=True) * (1.0 / width)
    scale[...] = jnp.broadcast_to(lax.rsqrt(mean + eps_norm), scale.shape)
    gains = [gain[b * HG : (b + 1) * HG, :] for b in range(groups)]

    def part(p, _):
        in_copy(p).wait()

        def body(it, _):
            done = []
            for e in range(8):
                r = p * size + it * 8 + e
                factor = scale[pl.ds(flat[0, r], 1), :]
                here = pl.ds(pl.multiple_of(r * HG, HG), HG)
                scaled = [mixed[b, here, :] * factor * gains[b] for b in range(groups)]
                done.append((r, jnp.concatenate(scaled, axis=0).astype(BF16)))
            for r, value in done:
                out[r] = value
            return 0

        lax.fori_loop(0, size // 8, body, 0)
        out_copy(p).start()
        return 0

    lax.fori_loop(0, PARTS, part, 0)
    for p in range(PARTS):
        out_copy(p).wait()


def finish(flat, squares, gain, mixed):
    rows = flat.shape[1]
    heads, d = gain.shape
    vm = pltpu.VMEM
    dma = pltpu.SemaphoreType.DMA
    away = pl.BlockSpec(memory_space=pl.ANY)
    return pl.pallas_call(
        functools.partial(finish_kernel, heads * d),
        out_shape=jax.ShapeDtypeStruct((rows, heads, d), BF16),
        in_specs=[away] * 4,
        out_specs=away,
        scratch_shapes=[
            pltpu.SMEM(flat.shape, I32),
            vm(squares.shape, F32),
            vm(gain.shape, F32),
            vm(mixed.shape, F32),
            vm((rows, heads, d), BF16),
            vm(squares.shape, F32),
            dma((3,)),
            dma((PARTS,)),
            dma((PARTS,)),
        ],
        compiler_params=pltpu.CompilerParams(vmem_limit_bytes=67043328),
    )(flat, squares, gain, mixed)


def per_device(queries, key_rows, value_rows, destination, doc_starts, decay_rate, norm_gain):
    loaders = lax.axis_size("dp")
    shards = lax.axis_size("seq")
    rows, heads, d = queries.shape[2:]
    cap = 3 * rows // (2 * loaders)
    levels = loaders.bit_length() - 1
    passes = max(1, loaders // 8)
    width = heads // passes
    results = []
    for i in range(passes):
        results.append(
            scan_states(
                decay_rate,
                destination,
                doc_starts,
                key_rows,
                value_rows,
                queries,
                width,
                i * width,
                levels,
                loaders,
                shards,
                cap,
                i,
            )
        )
    mixed = results[0][0] if passes == 1 else jnp.concatenate([x[0] for x in results], axis=0)
    squares = sum(x[1] for x in results[1:]) + results[0][1] if passes > 1 else results[0][1]
    return finish(results[0][2], squares, norm_gain, mixed)[None, None]


def solution(mesh):
    placed = (
        P("dp", "seq", None, None, None),
        P("dp", "seq", None, None, None),
        P("dp", "seq", None, None, None),
        P("dp", "seq", None),
        P("dp", "seq", None),
        P(),
        P(),
    )
    return jax.shard_map(
        per_device,
        mesh=mesh,
        in_specs=placed,
        out_specs=P("dp", "seq", None, None, None),
        check_vma=False,
    )
```

```python
import functools
import jax
import jax.numpy as jnp
from jax import lax
from jax.experimental import pallas as pl
from jax.experimental.pallas import tpu as pltpu
from jax.sharding import PartitionSpec as P

MESH = pl.DeviceIdType.MESH
F32 = jnp.float32
BF16 = jnp.bfloat16
I32 = jnp.int32
eps_norm = 1e-06
LANES = 128
HG = 8
HI = 16
HC = 2
PARTS = 4
PIECES = 4
NEVER = 1e30
UP_LAG = 2
Z_LAG = 2


def prepare(seqs, cap, dest_ref, start_ref, src_ref, flat_ref, fact_ref, until_ref, since_ref, gap_ref):
    rows = dest_ref.shape[-1]
    drow = dest_ref[...]
    srow = start_ref[...]
    ci = lax.broadcasted_iota(I32, (LANES, rows), 1)
    ri = lax.broadcasted_iota(I32, (LANES, rows), 0)
    place = lax.broadcasted_iota(I32, (LANES, LANES), 1)
    rlocal = lax.broadcasted_iota(I32, (LANES, 1), 0)
    slot_row = jnp.zeros((1, rows), I32)
    source = [jnp.zeros((1, LANES), I32) for _ in range(seqs)]
    begins = [jnp.zeros((1, LANES), I32) for _ in range(seqs)]
    for b in range(rows // LANES):
        rb = ri + b * LANES
        dcol = jnp.sum(jnp.where(rb == ci, drow, 0), axis=1, keepdims=True)
        scol = jnp.sum(jnp.where(rb == ci, srow, 0), axis=1, keepdims=True)
        same = jnp.where(dcol == drow, 1, 0)
        slot_col = jnp.sum(jnp.where(ci < rb, same, 0), axis=1, keepdims=True)
        slot_row = slot_row + jnp.sum(jnp.where(rb < ci, same, 0), axis=0, keepdims=True)
        slot_wide = dcol * LANES + slot_col
        rcol = rlocal + b * LANES
        for g in range(seqs):
            hit = slot_wide == place + g * LANES
            source[g] = source[g] + jnp.sum(jnp.where(hit, rcol, 0), axis=0, keepdims=True)
            begins[g] = begins[g] + jnp.sum(jnp.where(hit, scol, 0), axis=0, keepdims=True)
    flat_ref[...] = jnp.clip(drow * cap + slot_row, 0, seqs * cap - 1)
    pi = lax.broadcasted_iota(I32, (cap, LANES), 0)
    pj = lax.broadcasted_iota(I32, (cap, LANES), 1)
    position = pi.astype(F32)
    for g in range(seqs):
        src_ref[:, g * LANES : (g + 1) * LANES] = jnp.clip(source[g], 0, rows - 1)
        begin = begins[g].astype(F32)
        number = jnp.sum(jnp.where(drow == g, 1.0, 0.0), axis=1, keepdims=True)
        doc_end = jnp.sum(begin, axis=1, keepdims=True)
        doc_col = jnp.sum(jnp.where(pj <= pi, begin, 0.0), axis=1, keepdims=True)
        begin_col = jnp.sum(jnp.where(pj == pi, begin, 0.0), axis=1, keepdims=True)
        doc_row = jnp.sum(jnp.where(pi <= pj, begin_col, 0.0), axis=0, keepdims=True)
        here = slice(g * cap, (g + 1) * cap)
        fact_ref[0, g : g + 1, :] = jnp.broadcast_to(number, (1, LANES))
        fact_ref[1, g : g + 1, :] = jnp.broadcast_to(doc_end, (1, LANES))
        ends = (position < number) & (doc_col == doc_end)
        until_ref[here, :] = jnp.where(ends, number - 1.0 - position, NEVER)
        since_ref[here, :] = jnp.where(
            jnp.broadcast_to(doc_col, (cap, LANES)) == 0.0, position + 1.0, NEVER
        )
        keep = (pi >= pj) & (doc_col == doc_row)
        gap_ref[here, :] = jnp.where(keep, (pi - pj).astype(F32), NEVER)


def scan_kernel(levels, shards, seqs, heads, cap, base, *refs):
    rate_hbm, dest_hbm, start_hbm = refs[:3]
    sources = refs[3:6]
    mixed_hbm, square_hbm, flat_hbm = refs[6:9]
    rate_ref, src_ref, flat_ref, dest_ref, start_ref, src_row, flat_row = refs[9:16]
    fact_ref, until_ref, since_ref, gap_ref, square_ref, small_sem = refs[16:22]
    refs = refs[22:]
    u_ref, out_ref, packed = refs[:3]
    tall = refs[3:6]
    inbuf = refs[6:9]
    in_sem, row_sem, facts, spans_ref, dec, f_s, f_r, total, zin = refs[9:18]
    up_s, up_r, dn_s, dn_r, z_s, z_r = refs[18:24]
    got = refs[24:]
    rows = flat_ref.shape[1]
    d = LANES
    me = lax.axis_index("dp")
    shard = lax.axis_index("seq")
    chunks = heads // HC
    per_group = HG // HC
    per_load = HI // HC
    tables = 2 * levels + 1
    share = [2 ** (levels - k - 1) for k in range(levels)]

    def bit(k):
        return lax.rem(lax.div(me, 2**k), 2)

    def partner(k):
        return me + 2**k - bit(k) * (2 ** (k + 1))

    def low(k):
        return lax.rem(me, 2**k)

    def decay(table, seq, head):
        return dec[head, pl.ds(table * seqs + seq, 1), :]

    def in_copy(n, b):
        return pltpu.make_async_copy(
            sources[n].at[0, 0, :, pl.ds(pl.multiple_of(base + b * HI, HI), HI), :],
            inbuf[n],
            in_sem.at[n],
        )

    loads = [
        pltpu.make_async_copy(dest_hbm.at[0], dest_ref, small_sem.at[0]),
        pltpu.make_async_copy(start_hbm.at[0], start_ref, small_sem.at[1]),
        pltpu.make_async_copy(rate_hbm, rate_ref, small_sem.at[5]),
    ]
    moves = [
        pltpu.make_async_copy(src_row, src_ref, small_sem.at[2]),
        pltpu.make_async_copy(flat_row, flat_ref, small_sem.at[3]),
        pltpu.make_async_copy(flat_row, flat_hbm, small_sem.at[4]),
    ]
    barrier = pltpu.get_barrier_semaphore()
    for i in range(1, seqs):
        peer = lax.rem(me + i, seqs)
        pl.semaphore_signal(barrier, inc=1, device_id=(peer, shard), device_id_type=MESH)

    @pl.when(shard > 0)
    def _():
        pl.semaphore_signal(barrier, inc=1, device_id=(me, shard - 1), device_id_type=MESH)

    @pl.when(shard < shards - 1)
    def _():
        pl.semaphore_signal(barrier, inc=1, device_id=(me, shard + 1), device_id_type=MESH)

    for copy in loads:
        copy.start()
    for n in range(3):
        in_copy(n, 0).start()
    @pl.when(shard == 0)
    def _():
        def clear(i, _):
            zin[pl.ds(i, 1)] = jnp.zeros((1,) + zin.shape[1:], zin.dtype)
            return 0

        lax.fori_loop(0, heads, clear, 0)

    square_ref[...] = jnp.zeros(square_ref.shape, F32)
    for copy in loads:
        copy.wait()
    prepare(
        seqs, cap, dest_ref, start_ref, src_row, flat_row, fact_ref, until_ref, since_ref, gap_ref
    )
    for copy in moves:
        copy.start()

    def part(c):
        return pl.ds(c * HC, HC)

    def slot(k, j):
        return share[k] - 1 + j

    def up_copy(k, c, j):
        seq = j * 2 ** (k + 1) + (1 - bit(k)) * 2**k + low(k)
        return pltpu.make_async_remote_copy(
            src_ref=u_ref.at[seq, part(c)],
            dst_ref=got[k].at[j, part(c)],
            send_sem=up_s.at[slot(k, j), c],
            recv_sem=up_r.at[slot(k, j), c],
            device_id=(partner(k), shard),
            device_id_type=MESH,
        )

    def down_copy(k, c, j, receive):
        owner = partner(k) if receive else me
        seq = j * 2 ** (k + 1) + lax.rem(owner, 2 ** (k + 1))
        return pltpu.make_async_remote_copy(
            src_ref=got[k].at[j, part(c)],
            dst_ref=out_ref.at[seq, part(c)],
            send_sem=dn_s.at[slot(k, j), c],
            recv_sem=dn_r.at[slot(k, j), c],
            device_id=(partner(k), shard),
            device_id_type=MESH,
        )

    def z_copy(c, target):
        return pltpu.make_async_remote_copy(
            src_ref=total.at[part(c)],
            dst_ref=zin.at[part(c)],
            send_sem=z_s.at[c],
            recv_sem=z_r.at[c],
            device_id=(me, target),
            device_id_type=MESH,
        )

    def row_copy(i, p):
        here = pl.ds(p * (rows * HG // PIECES), rows * HG // PIECES)
        return pltpu.make_async_copy(
            tall[2].at[here], mixed_hbm.at[i, here], row_sem.at[p]
        )

    def rows_back(p):
        slots = tall[0].reshape(seqs * cap, HG, d)
        steps = rows // PIECES // 16

        def body(it, _):
            first = (p * steps + it) * 16
            found = [slots[flat_ref[0, first + e]] for e in range(16)]
            for e in range(16):
                target = pl.multiple_of((first + e) * HG, HG)
                tall[2][pl.ds(target, HG), :] = found[e]
            return 0

        lax.fori_loop(0, steps, body, 0)

    def square_copy():
        return pltpu.make_async_copy(square_ref, square_hbm, small_sem.at[0])

    def gather_side(side):
        steps = cap // 16
        part_heads = slice(side * HG, (side + 1) * HG)

        def body(it, _):
            first = lax.div(it, steps) * LANES + lax.rem(it, steps) * 16
            for half in range(0, 16, 8):
                found = [
                    [inbuf[n][src_ref[0, first + half + e], part_heads, :].astype(F32) for n in range(3)]
                    for e in range(8)
                ]
                for e in range(8):
                    place = pl.multiple_of((it * 16 + half + e) * HG, HG)
                    for n in range(3):
                        tall[n][pl.ds(place, HG), :] = found[e][n]
            return 0

        lax.fori_loop(0, seqs * steps, body, 0)

    def gather(i):
        for side in range(HI // HG):

            @pl.when(lax.rem(i, HI // HG) == side)
            def _():
                gather_side(side)

    def update(c):
        def body(g, _):
            here = pl.ds(pl.multiple_of(g * cap, 16), cap)
            until = until_ref[here, :]
            for e in range(HC):
                head = c * HC + e
                j = lax.rem(head, HG)
                cols = pl.ds(pl.multiple_of(head * d, d), d)
                strided = pl.ds(g * cap * HG + j, cap, stride=HG)
                key = tall[0][strided, :]
                value = tall[1][strided, :].astype(BF16)
                weight = jnp.exp(-rate_ref[base + head] * until)
                scaled = (key * weight).astype(BF16)
                packed[0, here, cols] = key.astype(BF16)
                packed[1, here, cols] = value
                packed[2, here, cols] = tall[2][strided, :].astype(BF16)
                change = lax.dot_general(
                    scaled, value, (((0,), (0,)), ((), ())), preferred_element_type=F32
                )
                u_ref[g, head] = change.astype(BF16)
            return 0

        lax.fori_loop(0, seqs, body, 0, unroll=8)
        for j in range(share[0]):
            up_copy(0, c, j).start()

    def up(k, c):
        for j in range(share[k]):
            up_copy(k, c, j).wait_recv()
        first = (bit(k) == 0).astype(F32)

        def body(i, _):
            j, head = lax.div(i, HC), c * HC + lax.rem(i, HC)
            seq = j * 2 ** (k + 1) + low(k + 1)
            own = u_ref[seq, head].astype(F32)
            other = got[k][j, head].astype(F32)
            hi = decay(k, seq, head)
            own_w = first * hi + (1.0 - first)
            other_w = first + (1.0 - first) * hi
            both = own * own_w + other * other_w
            got[k][j, head] = (first * own + (1.0 - first) * other).astype(BF16)
            if k + 1 < levels:
                u_ref[seq, head] = both.astype(BF16)
            else:
                total[head] = both
            return 0

        lax.fori_loop(0, share[k] * HC, body, 0, unroll=2 if k + 1 == levels else 4)
        if k + 1 < levels:
            for j in range(share[k + 1]):
                up_copy(k + 1, c, j).start()

    def across(c):
        @pl.when(shard > 0)
        def _():
            z_copy(c, shard).wait_recv()

        def body(i, _):
            head = c * HC + i
            state = zin[head]
            out_ref[me, head] = state.astype(BF16)
            total[head] = state * decay(2 * levels, me, head) + total[head]
            return 0

        lax.fori_loop(0, HC, body, 0)

        @pl.when(shard < shards - 1)
        def _():
            z_copy(c, shard + 1).start()

    def down(k, c):
        if k + 1 < levels:
            for j in range(share[k + 1]):
                down_copy(k + 1, c, j, True).wait_recv()
        first = (bit(k) == 0).astype(F32)

        def body(i, _):
            j, head = lax.div(i, HC), c * HC + lax.rem(i, HC)
            seq = j * 2 ** (k + 1) + low(k + 1)
            start = out_ref[seq, head].astype(F32)
            later = start * decay(levels + k, seq, head) + got[k][j, head].astype(F32)
            out_ref[seq, head] = (first * start + (1.0 - first) * later).astype(BF16)
            got[k][j, head] = (first * later + (1.0 - first) * start).astype(BF16)
            return 0

        lax.fori_loop(0, share[k] * HC, body, 0, unroll=2 if k + 1 == levels else 4)
        for j in range(share[k]):
            down_copy(k, c, j, False).start()

    def attend(c):
        i = lax.div(c, per_group)
        for j in range(share[0]):
            down_copy(0, c, j, True).wait_recv()

        def body(g, _):
            here = pl.ds(pl.multiple_of(g * cap, 16), cap)
            gap = gap_ref[here, :cap]
            since = since_ref[here, :]
            squares = square_ref[here, :]
            for e in range(HC):
                head = c * HC + e
                j = lax.rem(head, HG)
                cols = pl.ds(pl.multiple_of(head * d, d), d)
                rate = rate_ref[base + head]
                query = packed[2, here, cols]
                scores = lax.dot_general(
                    query,
                    packed[0, here, cols],
                    (((1,), (1,)), ((), ())),
                    preferred_element_type=F32,
                )
                half = (scores * jnp.exp(-rate * gap)).astype(BF16)
                intra = jnp.dot(half, packed[1, here, cols], preferred_element_type=F32)
                inter = jnp.dot(query, out_ref[g, head], preferred_element_type=F32)
                mixed = intra + inter * jnp.exp(-rate * since)
                tall[0][pl.ds(g * cap * HG + j, cap, stride=HG), :] = mixed
                squares = squares + mixed * mixed
            square_ref[here, :] = squares
            return 0

        lax.fori_loop(0, seqs, body, 0, unroll=8)

        @pl.when(lax.rem(c, per_group) == per_group - 1)
        def _():
            @pl.when(c == chunks - 1)
            def _():
                square_copy().start()

            for p in range(PIECES):

                @pl.when(i > 0)
                def _():
                    row_copy(i - 1, p).wait()

                rows_back(p)
                row_copy(i, p).start()

    def fact_copy(i, receive):
        owner = lax.rem(me + seqs - i, seqs) if receive else me
        return pltpu.make_async_remote_copy(
            src_ref=fact_ref,
            dst_ref=facts.at[owner],
            send_sem=f_s.at[i - 1],
            recv_sem=f_r.at[i - 1],
            device_id=(lax.rem(me + i, seqs), shard),
            device_id_type=MESH,
        )

    ends = (shard > 0).astype(I32) + (shard < shards - 1).astype(I32)
    pl.semaphore_wait(barrier, seqs - 1 + ends)
    for i in range(1, seqs):
        fact_copy(i, False).start()
    for copy in moves:
        copy.wait()
    for n in range(3):
        in_copy(n, 0).wait()
    gather_side(0)
    update(0)
    facts[pl.ds(me, 1)] = fact_ref[...][None]
    for i in range(1, seqs):
        fact_copy(i, True).wait_recv()
    spans = [((me // 2 ** (k + 1) * 2 + 1) * 2**k, 2**k) for k in range(levels)]
    spans += [((me // 2 ** (k + 1) * 2) * 2**k, 2**k) for k in range(levels)]
    spans += [(me * 0, seqs)]
    for table, (begin, size) in enumerate(spans):
        count = jnp.zeros(fact_ref.shape[1:], F32)
        docs = jnp.zeros(fact_ref.shape[1:], F32)
        for loader in range(seqs):
            inside = ((loader >= begin) & (loader < begin + size)).astype(F32)
            count = count + facts[loader, 0] * inside
            docs = docs + facts[loader, 1] * inside
        spans_ref[table * seqs : (table + 1) * seqs, :] = jnp.where(docs == 0.0, count, NEVER)

    def fill(head, _):
        dec[head] = jnp.exp(-rate_ref[base + head] * spans_ref[...])
        return 0

    lax.fori_loop(0, heads, fill, 0)

    ups = [1 + UP_LAG * k for k in range(levels)]
    z_first = ups[-1] + 1
    d_first = max(z_first + Z_LAG * (shards - 1) + 1, chunks - levels - 2)
    downs = [d_first + 2 * (levels - 1 - k) for k in range(levels)]
    a_first = downs[0] + 1

    def during(c):
        return (c >= 0) & (c < chunks)

    def step(t, _):
        fresh = t < chunks

        @pl.when(fresh & (lax.rem(t, per_group) == 0))
        def _():
            i = lax.div(t, per_group)

            @pl.when(lax.rem(t, per_load) == 0)
            def _():
                for n in range(3):
                    in_copy(n, lax.div(t, per_load)).wait()

            gather(i)

            @pl.when((t < chunks - per_load) & (lax.rem(t, per_load) == per_load - per_group))
            def _():
                for n in range(3):
                    in_copy(n, lax.div(t, per_load) + 1).start()

        @pl.when(fresh)
        def _():
            update(t)

        for k in range(levels):

            @pl.when(during(t - ups[k]))
            def _():
                up(k, t - ups[k])

        cz = t - z_first - Z_LAG * shard

        @pl.when(during(cz))
        def _():
            across(cz)

        for k in range(levels - 1, -1, -1):

            @pl.when(during(t - downs[k]))
            def _():
                down(k, t - downs[k])

        @pl.when(during(t - a_first))
        def _():
            attend(t - a_first)
            settle(t - a_first)

        return 0

    def settle(c):
        for k in range(levels):
            for j in range(share[k]):
                up_copy(k, c, j).wait_send()
                down_copy(k, c, j, False).wait_send()

        @pl.when(shard < shards - 1)
        def _():
            z_copy(c, shard + 1).wait_send()

    lax.fori_loop(1, chunks + a_first, step, 0)
    square_copy().wait()
    for p in range(PIECES):
        row_copy(heads // HG - 1, p).wait()
    for i in range(1, seqs):
        fact_copy(i, False).wait_send()


def scan_states(rate, destination, doc_starts, key, value, query, heads, base, levels, seqs, shards, cap, call):
    d = key.shape[-1]
    rows = key.shape[2]
    total = seqs * cap
    chunks = heads // HC
    vm = pltpu.VMEM
    share = [2 ** (levels - k - 1) for k in range(levels)]
    dma = pltpu.SemaphoreType.DMA
    away = pl.BlockSpec(memory_space=pl.ANY)
    return pl.pallas_call(
        functools.partial(scan_kernel, levels, shards, seqs, heads, cap, base),
        out_shape=[
            jax.ShapeDtypeStruct((heads // HG, rows * HG, d), F32),
            jax.ShapeDtypeStruct((total, d), F32),
            jax.ShapeDtypeStruct((1, rows), I32),
        ],
        in_specs=[away] * 6,
        out_specs=[away] * 3,
        scratch_shapes=[
            pltpu.SMEM(rate.shape, F32),
            pltpu.SMEM((1, seqs * LANES), I32),
            pltpu.SMEM((1, rows), I32),
            vm((1, rows), I32),
            vm((1, rows), I32),
            vm((1, seqs * LANES), I32),
            vm((1, rows), I32),
            vm((2, seqs, LANES), F32),
            vm((total, LANES), F32),
            vm((total, LANES), F32),
            vm((total, LANES), F32),
            vm((total, d), F32),
            dma((6,)),
            vm((seqs, heads, d, d), BF16),
            vm((seqs, heads, d, d), BF16),
            vm((3, total, heads * d), BF16),
            vm((total * HG, d), F32),
            vm((total * HG, d), F32),
            vm((total * HG, d), F32),
            vm((rows, HI, d), BF16),
            vm((rows, HI, d), BF16),
            vm((rows, HI, d), BF16),
            dma((3,)),
            dma((PIECES,)),
            vm((seqs, 2, seqs, LANES), F32),
            vm(((2 * levels + 1) * seqs, d), F32),
            vm((heads, (2 * levels + 1) * seqs, d), F32),
            dma((seqs - 1,)),
            dma((seqs - 1,)),
            vm((heads, d, d), F32),
            vm((heads, d, d), F32),
            dma((seqs - 1, chunks)),
            dma((seqs - 1, chunks)),
            dma((seqs - 1, chunks)),
            dma((seqs - 1, chunks)),
            dma((chunks,)),
            dma((chunks,)),
        ]
        + [vm((share[k], heads, d, d), BF16) for k in range(levels)],
        compiler_params=pltpu.CompilerParams(
            collective_id=call, has_side_effects=True, vmem_limit_bytes=67043328
        ),
    )(rate, destination, doc_starts, key, value, query)


def finish_kernel(width, *refs):
    sources, o_hbm = refs[:4], refs[4]
    flat, square, gain, mixed, out, scale, small_sem, in_sem, out_sem = refs[5:]
    groups = mixed.shape[0]
    rows = out.shape[0]
    size = rows // PARTS
    small = [
        pltpu.make_async_copy(source, target, small_sem.at[n])
        for n, (source, target) in enumerate(zip(sources, (flat, square, gain)))
    ]

    def in_copy(p):
        here = pl.ds(p * size * HG, size * HG)
        return pltpu.make_async_copy(sources[3].at[:, here], mixed.at[:, here], in_sem.at[p])

    def out_copy(p):
        here = pl.ds(p * size, size)
        return pltpu.make_async_copy(out.at[here], o_hbm.at[here], out_sem.at[p])

    for copy in small:
        copy.start()
    for p in range(PARTS):
        in_copy(p).start()
    for copy in small:
        copy.wait()
    mean = jnp.sum(square[...], axis=1, keepdims=True) * (1.0 / width)
    scale[...] = jnp.broadcast_to(lax.rsqrt(mean + eps_norm), scale.shape)
    gains = [gain[b * HG : (b + 1) * HG, :] for b in range(groups)]

    def part(p, _):
        in_copy(p).wait()

        def body(it, _):
            done = []
            for e in range(8):
                r = p * size + it * 8 + e
                factor = scale[pl.ds(flat[0, r], 1), :]
                here = pl.ds(pl.multiple_of(r * HG, HG), HG)
                scaled = [mixed[b, here, :] * factor * gains[b] for b in range(groups)]
                done.append((r, jnp.concatenate(scaled, axis=0).astype(BF16)))
            for r, value in done:
                out[r] = value
            return 0

        lax.fori_loop(0, size // 8, body, 0)
        out_copy(p).start()
        return 0

    lax.fori_loop(0, PARTS, part, 0)
    for p in range(PARTS):
        out_copy(p).wait()


def finish(flat, squares, gain, mixed):
    rows = flat.shape[1]
    heads, d = gain.shape
    vm = pltpu.VMEM
    dma = pltpu.SemaphoreType.DMA
    away = pl.BlockSpec(memory_space=pl.ANY)
    return pl.pallas_call(
        functools.partial(finish_kernel, heads * d),
        out_shape=jax.ShapeDtypeStruct((rows, heads, d), BF16),
        in_specs=[away] * 4,
        out_specs=away,
        scratch_shapes=[
            pltpu.SMEM(flat.shape, I32),
            vm(squares.shape, F32),
            vm(gain.shape, F32),
            vm(mixed.shape, F32),
            vm((rows, heads, d), BF16),
            vm(squares.shape, F32),
            dma((3,)),
            dma((PARTS,)),
            dma((PARTS,)),
        ],
        compiler_params=pltpu.CompilerParams(vmem_limit_bytes=67043328),
    )(flat, squares, gain, mixed)


def per_device(queries, key_rows, value_rows, destination, doc_starts, decay_rate, norm_gain):
    loaders = lax.axis_size("dp")
    shards = lax.axis_size("seq")
    rows, heads, d = queries.shape[2:]
    cap = 3 * rows // (2 * loaders)
    levels = loaders.bit_length() - 1
    passes = max(1, loaders // 8)
    width = heads // passes
    results = []
    for i in range(passes):
        results.append(
            scan_states(
                decay_rate,
                destination,
                doc_starts,
                key_rows,
                value_rows,
                queries,
                width,
                i * width,
                levels,
                loaders,
                shards,
                cap,
                i,
            )
        )
    mixed = results[0][0] if passes == 1 else jnp.concatenate([x[0] for x in results], axis=0)
    squares = sum(x[1] for x in results[1:]) + results[0][1] if passes > 1 else results[0][1]
    return finish(results[0][2], squares, norm_gain, mixed)[None, None]


def solution(mesh):
    placed = (
        P("dp", "seq", None, None, None),
        P("dp", "seq", None, None, None),
        P("dp", "seq", None, None, None),
        P("dp", "seq", None),
        P("dp", "seq", None),
        P(),
        P(),
    )
    return jax.shard_map(
        per_device,
        mesh=mesh,
        in_specs=placed,
        out_specs=P("dp", "seq", None, None, None),
        check_vma=False,
    )
```

```python
import functools
import jax
import jax.numpy as jnp
from jax import lax
from jax.experimental import pallas as pl
from jax.experimental.pallas import tpu as pltpu
from jax.sharding import PartitionSpec as P

MESH = pl.DeviceIdType.MESH
F32 = jnp.float32
BF16 = jnp.bfloat16
I32 = jnp.int32
eps_norm = 1e-06
LANES = 128
HG = 8
HI = 16
HC = 2
PARTS = 4
PIECES = 4
NEVER = 1e30
UP_LAG = 3
Z_LAG = 2


def prepare(seqs, cap, dest_ref, start_ref, src_ref, flat_ref, fact_ref, until_ref, since_ref, gap_ref):
    rows = dest_ref.shape[-1]
    drow = dest_ref[...]
    srow = start_ref[...]
    ci = lax.broadcasted_iota(I32, (LANES, rows), 1)
    ri = lax.broadcasted_iota(I32, (LANES, rows), 0)
    place = lax.broadcasted_iota(I32, (LANES, LANES), 1)
    rlocal = lax.broadcasted_iota(I32, (LANES, 1), 0)
    slot_row = jnp.zeros((1, rows), I32)
    source = [jnp.zeros((1, LANES), I32) for _ in range(seqs)]
    begins = [jnp.zeros((1, LANES), I32) for _ in range(seqs)]
    for b in range(rows // LANES):
        rb = ri + b * LANES
        dcol = jnp.sum(jnp.where(rb == ci, drow, 0), axis=1, keepdims=True)
        scol = jnp.sum(jnp.where(rb == ci, srow, 0), axis=1, keepdims=True)
        same = jnp.where(dcol == drow, 1, 0)
        slot_col = jnp.sum(jnp.where(ci < rb, same, 0), axis=1, keepdims=True)
        slot_row = slot_row + jnp.sum(jnp.where(rb < ci, same, 0), axis=0, keepdims=True)
        slot_wide = dcol * LANES + slot_col
        rcol = rlocal + b * LANES
        for g in range(seqs):
            hit = slot_wide == place + g * LANES
            source[g] = source[g] + jnp.sum(jnp.where(hit, rcol, 0), axis=0, keepdims=True)
            begins[g] = begins[g] + jnp.sum(jnp.where(hit, scol, 0), axis=0, keepdims=True)
    flat_ref[...] = jnp.clip(drow * cap + slot_row, 0, seqs * cap - 1)
    pi = lax.broadcasted_iota(I32, (cap, LANES), 0)
    pj = lax.broadcasted_iota(I32, (cap, LANES), 1)
    position = pi.astype(F32)
    for g in range(seqs):
        src_ref[:, g * LANES : (g + 1) * LANES] = jnp.clip(source[g], 0, rows - 1)
        begin = begins[g].astype(F32)
        number = jnp.sum(jnp.where(drow == g, 1.0, 0.0), axis=1, keepdims=True)
        doc_end = jnp.sum(begin, axis=1, keepdims=True)
        doc_col = jnp.sum(jnp.where(pj <= pi, begin, 0.0), axis=1, keepdims=True)
        begin_col = jnp.sum(jnp.where(pj == pi, begin, 0.0), axis=1, keepdims=True)
        doc_row = jnp.sum(jnp.where(pi <= pj, begin_col, 0.0), axis=0, keepdims=True)
        here = slice(g * cap, (g + 1) * cap)
        fact_ref[0, g : g + 1, :] = jnp.broadcast_to(number, (1, LANES))
        fact_ref[1, g : g + 1, :] = jnp.broadcast_to(doc_end, (1, LANES))
        ends = (position < number) & (doc_col == doc_end)
        until_ref[here, :] = jnp.where(ends, number - 1.0 - position, NEVER)
        since_ref[here, :] = jnp.where(
            jnp.broadcast_to(doc_col, (cap, LANES)) == 0.0, position + 1.0, NEVER
        )
        keep = (pi >= pj) & (doc_col == doc_row)
        gap_ref[here, :] = jnp.where(keep, (pi - pj).astype(F32), NEVER)


def scan_kernel(levels, shards, seqs, heads, cap, base, *refs):
    rate_hbm, dest_hbm, start_hbm = refs[:3]
    sources = refs[3:6]
    mixed_hbm, square_hbm, flat_hbm = refs[6:9]
    rate_ref, src_ref, flat_ref, dest_ref, start_ref, src_row, flat_row = refs[9:16]
    fact_ref, until_ref, since_ref, gap_ref, square_ref, small_sem = refs[16:22]
    refs = refs[22:]
    u_ref, out_ref, packed = refs[:3]
    tall = refs[3:6]
    inbuf = refs[6:9]
    in_sem, row_sem, facts, spans_ref, dec, f_s, f_r, total, zin = refs[9:18]
    up_s, up_r, dn_s, dn_r, z_s, z_r = refs[18:24]
    got = refs[24:]
    rows = flat_ref.shape[1]
    d = LANES
    me = lax.axis_index("dp")
    shard = lax.axis_index("seq")
    chunks = heads // HC
    per_group = HG // HC
    per_load = HI // HC
    tables = 2 * levels + 1
    share = [2 ** (levels - k - 1) for k in range(levels)]

    def bit(k):
        return lax.rem(lax.div(me, 2**k), 2)

    def partner(k):
        return me + 2**k - bit(k) * (2 ** (k + 1))

    def low(k):
        return lax.rem(me, 2**k)

    def decay(table, seq, head):
        return dec[head, pl.ds(table * seqs + seq, 1), :]

    def in_copy(n, b):
        return pltpu.make_async_copy(
            sources[n].at[0, 0, :, pl.ds(pl.multiple_of(base + b * HI, HI), HI), :],
            inbuf[n],
            in_sem.at[n],
        )

    loads = [
        pltpu.make_async_copy(dest_hbm.at[0], dest_ref, small_sem.at[0]),
        pltpu.make_async_copy(start_hbm.at[0], start_ref, small_sem.at[1]),
        pltpu.make_async_copy(rate_hbm, rate_ref, small_sem.at[5]),
    ]
    moves = [
        pltpu.make_async_copy(src_row, src_ref, small_sem.at[2]),
        pltpu.make_async_copy(flat_row, flat_ref, small_sem.at[3]),
        pltpu.make_async_copy(flat_row, flat_hbm, small_sem.at[4]),
    ]
    barrier = pltpu.get_barrier_semaphore()
    for i in range(1, seqs):
        peer = lax.rem(me + i, seqs)
        pl.semaphore_signal(barrier, inc=1, device_id=(peer, shard), device_id_type=MESH)

    @pl.when(shard > 0)
    def _():
        pl.semaphore_signal(barrier, inc=1, device_id=(me, shard - 1), device_id_type=MESH)

    @pl.when(shard < shards - 1)
    def _():
        pl.semaphore_signal(barrier, inc=1, device_id=(me, shard + 1), device_id_type=MESH)

    for copy in loads:
        copy.start()
    for n in range(3):
        in_copy(n, 0).start()
    @pl.when(shard == 0)
    def _():
        def clear(i, _):
            zin[pl.ds(i, 1)] = jnp.zeros((1,) + zin.shape[1:], zin.dtype)
            return 0

        lax.fori_loop(0, heads, clear, 0)

    square_ref[...] = jnp.zeros(square_ref.shape, F32)
    for copy in loads:
        copy.wait()
    prepare(
        seqs, cap, dest_ref, start_ref, src_row, flat_row, fact_ref, until_ref, since_ref, gap_ref
    )
    for copy in moves:
        copy.start()

    def part(c):
        return pl.ds(c * HC, HC)

    def slot(k, j):
        return share[k] - 1 + j

    def up_copy(k, c, j):
        seq = j * 2 ** (k + 1) + (1 - bit(k)) * 2**k + low(k)
        return pltpu.make_async_remote_copy(
            src_ref=u_ref.at[seq, part(c)],
            dst_ref=got[k].at[j, part(c)],
            send_sem=up_s.at[slot(k, j), c],
            recv_sem=up_r.at[slot(k, j), c],
            device_id=(partner(k), shard),
            device_id_type=MESH,
        )

    def down_copy(k, c, j, receive):
        owner = partner(k) if receive else me
        seq = j * 2 ** (k + 1) + lax.rem(owner, 2 ** (k + 1))
        return pltpu.make_async_remote_copy(
            src_ref=got[k].at[j, part(c)],
            dst_ref=out_ref.at[seq, part(c)],
            send_sem=dn_s.at[slot(k, j), c],
            recv_sem=dn_r.at[slot(k, j), c],
            device_id=(partner(k), shard),
            device_id_type=MESH,
        )

    def z_copy(c, target):
        return pltpu.make_async_remote_copy(
            src_ref=total.at[part(c)],
            dst_ref=zin.at[part(c)],
            send_sem=z_s.at[c],
            recv_sem=z_r.at[c],
            device_id=(me, target),
            device_id_type=MESH,
        )

    def row_copy(i, p):
        here = pl.ds(p * (rows * HG // PIECES), rows * HG // PIECES)
        return pltpu.make_async_copy(
            tall[2].at[here], mixed_hbm.at[i, here], row_sem.at[p]
        )

    def rows_back(p):
        slots = tall[0].reshape(seqs * cap, HG, d)
        steps = rows // PIECES // 16

        def body(it, _):
            first = (p * steps + it) * 16
            found = [slots[flat_ref[0, first + e]] for e in range(16)]
            for e in range(16):
                target = pl.multiple_of((first + e) * HG, HG)
                tall[2][pl.ds(target, HG), :] = found[e]
            return 0

        lax.fori_loop(0, steps, body, 0)

    def square_copy():
        return pltpu.make_async_copy(square_ref, square_hbm, small_sem.at[0])

    def gather_side(side):
        steps = cap // 16
        part_heads = slice(side * HG, (side + 1) * HG)

        def body(it, _):
            first = lax.div(it, steps) * LANES + lax.rem(it, steps) * 16
            for half in range(0, 16, 8):
                found = [
                    [inbuf[n][src_ref[0, first + half + e], part_heads, :].astype(F32) for n in range(3)]
                    for e in range(8)
                ]
                for e in range(8):
                    place = pl.multiple_of((it * 16 + half + e) * HG, HG)
                    for n in range(3):
                        tall[n][pl.ds(place, HG), :] = found[e][n]
            return 0

        lax.fori_loop(0, seqs * steps, body, 0)

    def gather(i):
        for side in range(HI // HG):

            @pl.when(lax.rem(i, HI // HG) == side)
            def _():
                gather_side(side)

    def update(c):
        def body(g, _):
            here = pl.ds(pl.multiple_of(g * cap, 16), cap)
            until = until_ref[here, :]
            for e in range(HC):
                head = c * HC + e
                j = lax.rem(head, HG)
                cols = pl.ds(pl.multiple_of(head * d, d), d)
                strided = pl.ds(g * cap * HG + j, cap, stride=HG)
                key = tall[0][strided, :]
                value = tall[1][strided, :].astype(BF16)
                weight = jnp.exp(-rate_ref[base + head] * until)
                scaled = (key * weight).astype(BF16)
                packed[0, here, cols] = key.astype(BF16)
                packed[1, here, cols] = value
                packed[2, here, cols] = tall[2][strided, :].astype(BF16)
                change = lax.dot_general(
                    scaled, value, (((0,), (0,)), ((), ())), preferred_element_type=F32
                )
                u_ref[g, head] = change.astype(BF16)
            return 0

        lax.fori_loop(0, seqs, body, 0, unroll=8)
        for j in range(share[0]):
            up_copy(0, c, j).start()

    def up(k, c):
        for j in range(share[k]):
            up_copy(k, c, j).wait_recv()
        first = (bit(k) == 0).astype(F32)

        def body(i, _):
            j, head = lax.div(i, HC), c * HC + lax.rem(i, HC)
            seq = j * 2 ** (k + 1) + low(k + 1)
            own = u_ref[seq, head].astype(F32)
            other = got[k][j, head].astype(F32)
            hi = decay(k, seq, head)
            own_w = first * hi + (1.0 - first)
            other_w = first + (1.0 - first) * hi
            both = own * own_w + other * other_w
            got[k][j, head] = (first * own + (1.0 - first) * other).astype(BF16)
            if k + 1 < levels:
                u_ref[seq, head] = both.astype(BF16)
            else:
                total[head] = both
            return 0

        lax.fori_loop(0, share[k] * HC, body, 0, unroll=2 if k + 1 == levels else 4)
        if k + 1 < levels:
            for j in range(share[k + 1]):
                up_copy(k + 1, c, j).start()

    def across(c):
        @pl.when(shard > 0)
        def _():
            z_copy(c, shard).wait_recv()

        def body(i, _):
            head = c * HC + i
            state = zin[head]
            out_ref[me, head] = state.astype(BF16)
            total[head] = state * decay(2 * levels, me, head) + total[head]
            return 0

        lax.fori_loop(0, HC, body, 0)

        @pl.when(shard < shards - 1)
        def _():
            z_copy(c, shard + 1).start()

    def down(k, c):
        if k + 1 < levels:
            for j in range(share[k + 1]):
                down_copy(k + 1, c, j, True).wait_recv()
        first = (bit(k) == 0).astype(F32)

        def body(i, _):
            j, head = lax.div(i, HC), c * HC + lax.rem(i, HC)
            seq = j * 2 ** (k + 1) + low(k + 1)
            start = out_ref[seq, head].astype(F32)
            later = start * decay(levels + k, seq, head) + got[k][j, head].astype(F32)
            out_ref[seq, head] = (first * start + (1.0 - first) * later).astype(BF16)
            got[k][j, head] = (first * later + (1.0 - first) * start).astype(BF16)
            return 0

        lax.fori_loop(0, share[k] * HC, body, 0, unroll=2 if k + 1 == levels else 4)
        for j in range(share[k]):
            down_copy(k, c, j, False).start()

    def attend(c):
        i = lax.div(c, per_group)
        for j in range(share[0]):
            down_copy(0, c, j, True).wait_recv()

        def body(g, _):
            here = pl.ds(pl.multiple_of(g * cap, 16), cap)
            gap = gap_ref[here, :cap]
            since = since_ref[here, :]
            squares = square_ref[here, :]
            for e in range(HC):
                head = c * HC + e
                j = lax.rem(head, HG)
                cols = pl.ds(pl.multiple_of(head * d, d), d)
                rate = rate_ref[base + head]
                query = packed[2, here, cols]
                scores = lax.dot_general(
                    query,
                    packed[0, here, cols],
                    (((1,), (1,)), ((), ())),
                    preferred_element_type=F32,
                )
                half = (scores * jnp.exp(-rate * gap)).astype(BF16)
                intra = jnp.dot(half, packed[1, here, cols], preferred_element_type=F32)
                inter = jnp.dot(query, out_ref[g, head], preferred_element_type=F32)
                mixed = intra + inter * jnp.exp(-rate * since)
                tall[0][pl.ds(g * cap * HG + j, cap, stride=HG), :] = mixed
                squares = squares + mixed * mixed
            square_ref[here, :] = squares
            return 0

        lax.fori_loop(0, seqs, body, 0, unroll=8)

        @pl.when(lax.rem(c, per_group) == per_group - 1)
        def _():
            @pl.when(c == chunks - 1)
            def _():
                square_copy().start()

            for p in range(PIECES):

                @pl.when(i > 0)
                def _():
                    row_copy(i - 1, p).wait()

                rows_back(p)
                row_copy(i, p).start()

    def fact_copy(i, receive):
        owner = lax.rem(me + seqs - i, seqs) if receive else me
        return pltpu.make_async_remote_copy(
            src_ref=fact_ref,
            dst_ref=facts.at[owner],
            send_sem=f_s.at[i - 1],
            recv_sem=f_r.at[i - 1],
            device_id=(lax.rem(me + i, seqs), shard),
            device_id_type=MESH,
        )

    ends = (shard > 0).astype(I32) + (shard < shards - 1).astype(I32)
    pl.semaphore_wait(barrier, seqs - 1 + ends)
    for i in range(1, seqs):
        fact_copy(i, False).start()
    for copy in moves:
        copy.wait()
    for n in range(3):
        in_copy(n, 0).wait()
    gather_side(0)
    update(0)
    facts[pl.ds(me, 1)] = fact_ref[...][None]
    for i in range(1, seqs):
        fact_copy(i, True).wait_recv()
    spans = [((me // 2 ** (k + 1) * 2 + 1) * 2**k, 2**k) for k in range(levels)]
    spans += [((me // 2 ** (k + 1) * 2) * 2**k, 2**k) for k in range(levels)]
    spans += [(me * 0, seqs)]
    for table, (begin, size) in enumerate(spans):
        count = jnp.zeros(fact_ref.shape[1:], F32)
        docs = jnp.zeros(fact_ref.shape[1:], F32)
        for loader in range(seqs):
            inside = ((loader >= begin) & (loader < begin + size)).astype(F32)
            count = count + facts[loader, 0] * inside
            docs = docs + facts[loader, 1] * inside
        spans_ref[table * seqs : (table + 1) * seqs, :] = jnp.where(docs == 0.0, count, NEVER)

    def fill(head, _):
        dec[head] = jnp.exp(-rate_ref[base + head] * spans_ref[...])
        return 0

    lax.fori_loop(0, heads, fill, 0)

    ups = [1 + UP_LAG * k for k in range(levels)]
    z_first = ups[-1] + 1
    d_first = max(z_first + Z_LAG * (shards - 1) + 1, chunks - levels - 2)
    downs = [d_first + 2 * (levels - 1 - k) for k in range(levels)]
    a_first = downs[0] + 1

    def during(c):
        return (c >= 0) & (c < chunks)

    def step(t, _):
        fresh = t < chunks

        @pl.when(fresh & (lax.rem(t, per_group) == 0))
        def _():
            i = lax.div(t, per_group)

            @pl.when(lax.rem(t, per_load) == 0)
            def _():
                for n in range(3):
                    in_copy(n, lax.div(t, per_load)).wait()

            gather(i)

            @pl.when((t < chunks - per_load) & (lax.rem(t, per_load) == per_load - per_group))
            def _():
                for n in range(3):
                    in_copy(n, lax.div(t, per_load) + 1).start()

        @pl.when(fresh)
        def _():
            update(t)

        for k in range(levels):

            @pl.when(during(t - ups[k]))
            def _():
                up(k, t - ups[k])

        cz = t - z_first - Z_LAG * shard

        @pl.when(during(cz))
        def _():
            across(cz)

        for k in range(levels - 1, -1, -1):

            @pl.when(during(t - downs[k]))
            def _():
                down(k, t - downs[k])

        @pl.when(during(t - a_first))
        def _():
            attend(t - a_first)
            settle(t - a_first)

        return 0

    def settle(c):
        for k in range(levels):
            for j in range(share[k]):
                up_copy(k, c, j).wait_send()
                down_copy(k, c, j, False).wait_send()

        @pl.when(shard < shards - 1)
        def _():
            z_copy(c, shard + 1).wait_send()

    lax.fori_loop(1, chunks + a_first, step, 0)
    square_copy().wait()
    for p in range(PIECES):
        row_copy(heads // HG - 1, p).wait()
    for i in range(1, seqs):
        fact_copy(i, False).wait_send()


def scan_states(rate, destination, doc_starts, key, value, query, heads, base, levels, seqs, shards, cap, call):
    d = key.shape[-1]
    rows = key.shape[2]
    total = seqs * cap
    chunks = heads // HC
    vm = pltpu.VMEM
    share = [2 ** (levels - k - 1) for k in range(levels)]
    dma = pltpu.SemaphoreType.DMA
    away = pl.BlockSpec(memory_space=pl.ANY)
    return pl.pallas_call(
        functools.partial(scan_kernel, levels, shards, seqs, heads, cap, base),
        out_shape=[
            jax.ShapeDtypeStruct((heads // HG, rows * HG, d), F32),
            jax.ShapeDtypeStruct((total, d), F32),
            jax.ShapeDtypeStruct((1, rows), I32),
        ],
        in_specs=[away] * 6,
        out_specs=[away] * 3,
        scratch_shapes=[
            pltpu.SMEM(rate.shape, F32),
            pltpu.SMEM((1, seqs * LANES), I32),
            pltpu.SMEM((1, rows), I32),
            vm((1, rows), I32),
            vm((1, rows), I32),
            vm((1, seqs * LANES), I32),
            vm((1, rows), I32),
            vm((2, seqs, LANES), F32),
            vm((total, LANES), F32),
            vm((total, LANES), F32),
            vm((total, LANES), F32),
            vm((total, d), F32),
            dma((6,)),
            vm((seqs, heads, d, d), BF16),
            vm((seqs, heads, d, d), BF16),
            vm((3, total, heads * d), BF16),
            vm((total * HG, d), F32),
            vm((total * HG, d), F32),
            vm((total * HG, d), F32),
            vm((rows, HI, d), BF16),
            vm((rows, HI, d), BF16),
            vm((rows, HI, d), BF16),
            dma((3,)),
            dma((PIECES,)),
            vm((seqs, 2, seqs, LANES), F32),
            vm(((2 * levels + 1) * seqs, d), F32),
            vm((heads, (2 * levels + 1) * seqs, d), F32),
            dma((seqs - 1,)),
            dma((seqs - 1,)),
            vm((heads, d, d), F32),
            vm((heads, d, d), F32),
            dma((seqs - 1, chunks)),
            dma((seqs - 1, chunks)),
            dma((seqs - 1, chunks)),
            dma((seqs - 1, chunks)),
            dma((chunks,)),
            dma((chunks,)),
        ]
        + [vm((share[k], heads, d, d), BF16) for k in range(levels)],
        compiler_params=pltpu.CompilerParams(
            collective_id=call, has_side_effects=True, vmem_limit_bytes=67043328
        ),
    )(rate, destination, doc_starts, key, value, query)


def finish_kernel(width, *refs):
    sources, o_hbm = refs[:4], refs[4]
    flat, square, gain, mixed, out, scale, small_sem, in_sem, out_sem = refs[5:]
    groups = mixed.shape[0]
    rows = out.shape[0]
    size = rows // PARTS
    small = [
        pltpu.make_async_copy(source, target, small_sem.at[n])
        for n, (source, target) in enumerate(zip(sources, (flat, square, gain)))
    ]

    def in_copy(p):
        here = pl.ds(p * size * HG, size * HG)
        return pltpu.make_async_copy(sources[3].at[:, here], mixed.at[:, here], in_sem.at[p])

    def out_copy(p):
        here = pl.ds(p * size, size)
        return pltpu.make_async_copy(out.at[here], o_hbm.at[here], out_sem.at[p])

    for copy in small:
        copy.start()
    for p in range(PARTS):
        in_copy(p).start()
    for copy in small:
        copy.wait()
    mean = jnp.sum(square[...], axis=1, keepdims=True) * (1.0 / width)
    scale[...] = jnp.broadcast_to(lax.rsqrt(mean + eps_norm), scale.shape)
    gains = [gain[b * HG : (b + 1) * HG, :] for b in range(groups)]

    def part(p, _):
        in_copy(p).wait()

        def body(it, _):
            done = []
            for e in range(8):
                r = p * size + it * 8 + e
                factor = scale[pl.ds(flat[0, r], 1), :]
                here = pl.ds(pl.multiple_of(r * HG, HG), HG)
                scaled = [mixed[b, here, :] * factor * gains[b] for b in range(groups)]
                done.append((r, jnp.concatenate(scaled, axis=0).astype(BF16)))
            for r, value in done:
                out[r] = value
            return 0

        lax.fori_loop(0, size // 8, body, 0)
        out_copy(p).start()
        return 0

    lax.fori_loop(0, PARTS, part, 0)
    for p in range(PARTS):
        out_copy(p).wait()


def finish(flat, squares, gain, mixed):
    rows = flat.shape[1]
    heads, d = gain.shape
    vm = pltpu.VMEM
    dma = pltpu.SemaphoreType.DMA
    away = pl.BlockSpec(memory_space=pl.ANY)
    return pl.pallas_call(
        functools.partial(finish_kernel, heads * d),
        out_shape=jax.ShapeDtypeStruct((rows, heads, d), BF16),
        in_specs=[away] * 4,
        out_specs=away,
        scratch_shapes=[
            pltpu.SMEM(flat.shape, I32),
            vm(squares.shape, F32),
            vm(gain.shape, F32),
            vm(mixed.shape, F32),
            vm((rows, heads, d), BF16),
            vm(squares.shape, F32),
            dma((3,)),
            dma((PARTS,)),
            dma((PARTS,)),
        ],
        compiler_params=pltpu.CompilerParams(vmem_limit_bytes=67043328),
    )(flat, squares, gain, mixed)


def per_device(queries, key_rows, value_rows, destination, doc_starts, decay_rate, norm_gain):
    loaders = lax.axis_size("dp")
    shards = lax.axis_size("seq")
    rows, heads, d = queries.shape[2:]
    cap = 3 * rows // (2 * loaders)
    levels = loaders.bit_length() - 1
    passes = max(1, loaders // 8)
    width = heads // passes
    results = []
    for i in range(passes):
        results.append(
            scan_states(
                decay_rate,
                destination,
                doc_starts,
                key_rows,
                value_rows,
                queries,
                width,
                i * width,
                levels,
                loaders,
                shards,
                cap,
                i,
            )
        )
    mixed = results[0][0] if passes == 1 else jnp.concatenate([x[0] for x in results], axis=0)
    squares = sum(x[1] for x in results[1:]) + results[0][1] if passes > 1 else results[0][1]
    return finish(results[0][2], squares, norm_gain, mixed)[None, None]


def solution(mesh):
    placed = (
        P("dp", "seq", None, None, None),
        P("dp", "seq", None, None, None),
        P("dp", "seq", None, None, None),
        P("dp", "seq", None),
        P("dp", "seq", None),
        P(),
        P(),
    )
    return jax.shard_map(
        per_device,
        mesh=mesh,
        in_specs=placed,
        out_specs=P("dp", "seq", None, None, None),
        check_vma=False,
    )
```
